256 devices in a mesh: seq: 32 (over z, x), hg: 8 (over y, core).
Axes of the slice: x: 4, y: 4, z: 8, core: 2. Of those that a mesh axis runs over, the one named last changes fastest.
Arguments:
- conv_input: bfloat16 [65536, 4096], P('seq', 'hg'), may hold values from -6 to 6
- grad_output: bfloat16 [65536, 4096], P('seq', 'hg'), may hold values from -0.015625 to 0.015625
- inject: bfloat16 [65536, 128], P('seq'), may hold values from -6 to 6
- readout: bfloat16 [65536, 128], P('seq'), may hold values from -6 to 6
- conv_weight: bfloat16 [4, 4096], P(None, 'hg'), may hold values from -3 to 3
- decay_codes: int32 [64, 256], P('hg', 'seq'), may hold values from 0 to 1000, as said below
Outputs:
- grad_input: float32 [65536, 4096], P('seq', 'hg')
- grad_inject: float32 [65536, 128], P('seq')
- grad_readout: float32 [65536, 128], P('seq')
The draws below stay inside these ranges and needn't reach their ends.
Inputs may be any that keep to these rules, and one draw needn't show every extreme that they name: The decay of every step of span c in head h is 1 - 1e-6 decay_codes[h, c].
All inputs are finite; a program needn't handle non-finite values.
Results may differ from the reference program's by a relative error of at most 0.0029.
Values may be sent and summed in bfloat16 or wider, within the bound.
No kernel may reach another device: no remote copies, remote signals or barrier semaphores. Data moves between devices by JAX's collectives and lax.ppermute only.
A program may use at most 128 MiB of HBM per device.

```python
import jax
import jax.numpy as jnp
from jax import lax

HEADS = 64
HEAD_DIM = 64
STATE = 128
TOKENS = 65536
NCH = 256


def draw_decay_codes(key, part):
    key_head, key_span, key_spot, key_zero = jax.random.split(key, 4)
    powers = jax.random.randint(key_head, (HEADS, 1), 0, 11)
    limits = jnp.left_shift(jnp.ones((HEADS, 1), jnp.int32), powers)
    drawn = jax.random.randint(key_span, (HEADS, NCH), 0, 1 << 30)
    code_table = jnp.minimum(drawn % (limits + 1), 1000)
    position = jax.random.randint(key_spot, (), 0, HEADS * NCH)
    zero_spot = jax.random.randint(key_zero, (), 0, HEADS * NCH)
    flattened = code_table.reshape(-1).at[zero_spot].set(0).at[position].set(1000)
    return flattened.reshape(HEADS, NCH).astype(jnp.int32)


def block_levels(stream_key, shape, cuts, least, top_value):
    loudness, own = 1.0, jax.random.fold_in(stream_key, 6)
    for dim, shards_of in cuts:
        draws = jnp.exp(jax.random.uniform(jax.random.fold_in(own, dim), (shards_of,), jnp.float32, least / len(cuts), top_value / len(cuts)))
        loudness = loudness * jnp.repeat(draws, shape[dim] // shards_of).reshape([-1 if axis == dim else 1 for axis in range(len(shape))])
    return loudness


def normal_values(stream_key, shape, scale, bound, cuts=(), held_as=jnp.bfloat16):
    entries = jax.random.normal(stream_key, shape, jnp.float32) * scale
    if len(cuts) > 0:
        entries = block_levels(stream_key, shape, cuts, -0.22, 0.18) * entries
    return jnp.clip(entries, min=-bound, max=bound).astype(held_as)


def setup_inputs(seed: int = 0) -> dict:
    seeds = jax.random.split(jax.random.key(seed), 7)
    return {
        "conv_input": normal_values(seeds[0], (TOKENS, HEADS * HEAD_DIM), 1.0, 6.0, ((0, 32), (1, 8))),
        "grad_output": normal_values(seeds[1], (TOKENS, HEADS * HEAD_DIM), 0.001, 0.015625, ((0, 32), (1, 8))),
        "inject": normal_values(seeds[2], (TOKENS, STATE), 1.0, 6.0, ((0, 32),)),
        "readout": normal_values(seeds[3], (TOKENS, STATE), 1.0, 6.0, ((0, 32),)),
        "conv_weight": normal_values(seeds[4], (4, HEADS * HEAD_DIM), 4 ** -0.5, 3.0, ((1, 8),)),
        "decay_codes": draw_decay_codes(jax.random.fold_in(seeds[6], 71), 0),
    }


precise = lax.Precision.HIGHEST


def causal_conv(padded, weights, length):
    summed = weights[0] * padded[0:length].astype(jnp.float32)
    for offset in range(1, 4):
        summed = summed + weights[offset] * padded[offset:offset + length].astype(jnp.float32)
    return summed


def silu_slope(preact):
    squashed = jax.nn.sigmoid(preact)
    return squashed * (1.0 + preact * (1.0 - squashed))


def span_terms(block_act, block_grad, block_inject, block_readout, block_rates, grad_after):
    span_len = block_act.shape[0]
    places = jnp.arange(span_len).astype(jnp.float32)
    spread = places[:, None] - places[None, :]
    decay_mask = jnp.where(spread[None] >= 0.0, jnp.exp(jnp.maximum(spread, 0.0)[None] * block_rates[:, None, None]), 0.0)
    products = jnp.dot(block_readout, block_inject.T, preferred_element_type=jnp.float32)
    mixing = (products[None] * decay_mask).astype(jnp.bfloat16)
    grad_act = jnp.einsum("hji,jhp->ihp", mixing.astype(jnp.float32), block_grad.astype(jnp.float32))
    pair_weights = (jnp.einsum("ihp,jhp->hij", block_grad.astype(jnp.float32), block_act.astype(jnp.float32)) * decay_mask).astype(jnp.bfloat16)
    grad_readout = jnp.einsum("hij,jn->in", pair_weights.astype(jnp.float32), block_inject.astype(jnp.float32))
    grad_inject = jnp.einsum("hij,in->jn", pair_weights.astype(jnp.float32), block_readout.astype(jnp.float32))
    tail_decay = jnp.exp((span_len - 1.0 - places)[:, None] * block_rates[None, :])
    grad_act = grad_act + jnp.einsum("qn,hpn->qhp", block_inject.astype(jnp.float32), grad_after, precision=precise) * tail_decay[:, :, None]
    grad_inject = grad_inject + jnp.einsum("qhp,hpn->qn", block_act.astype(jnp.float32) * tail_decay[:, :, None], grad_after, precision=precise)
    return grad_act, grad_inject, grad_readout


def reference(conv_input, grad_output, inject, readout, conv_weight, decay_codes):
    tokens, channels = conv_input.shape
    head_count, spans = decay_codes.shape
    span_len = tokens // spans
    head_dim = channels // head_count
    states = inject.shape[1]
    weights = conv_weight.astype(jnp.float32)
    padded = jnp.concatenate([jnp.zeros((3, channels), jnp.bfloat16), conv_input], axis=0)
    preact = causal_conv(padded, weights, tokens)
    activated = jax.nn.silu(preact).astype(jnp.bfloat16)
    log_rates = jnp.log1p(-decay_codes.astype(jnp.float32) * 1e-6)
    act_blocks = activated.reshape(spans, span_len, head_count, head_dim)
    grad_blocks = grad_output.reshape(spans, span_len, head_count, head_dim)
    inject_blocks = inject.reshape(spans, span_len, states)
    readout_blocks = readout.reshape(spans, span_len, states)
    rate_blocks = log_rates.T
    places = jnp.arange(span_len).astype(jnp.float32)
    block_items = (act_blocks, grad_blocks, inject_blocks, readout_blocks, rate_blocks)

    def forward_step(carried, members):
        block_act, block_grad, block_inject, block_readout, block_rates = members
        lead_decay = jnp.exp((places + 1.0)[:, None] * block_rates[None, :])
        tail_decay = jnp.exp((span_len - 1.0 - places)[:, None] * block_rates[None, :])
        inter_readout = jnp.einsum("qhp,hpn->qn", block_grad.astype(jnp.float32) * lead_decay[:, :, None], carried, precision=precise)
        fresh_state = jnp.einsum("qhp,qn->hpn", block_act.astype(jnp.float32) * tail_decay[:, :, None], block_inject.astype(jnp.float32), precision=precise)
        renewed = jnp.exp(span_len * block_rates)[:, None, None] * carried + fresh_state
        return renewed, inter_readout

    def backward_step(carried, members):
        block_act, block_grad, block_inject, block_readout, block_rates = members
        lead_decay = jnp.exp((places + 1.0)[:, None] * block_rates[None, :])
        outputs = span_terms(block_act, block_grad, block_inject, block_readout, block_rates, carried)
        fresh_grad = jnp.einsum("qhp,qn->hpn", block_grad.astype(jnp.float32) * lead_decay[:, :, None], block_readout.astype(jnp.float32), precision=precise)
        renewed = jnp.exp(span_len * block_rates)[:, None, None] * carried + fresh_grad
        return renewed, outputs

    empty_state = jnp.zeros((head_count, head_dim, states), jnp.float32)
    unused_state, inter_readout = lax.scan(forward_step, empty_state, block_items)
    unused_grad, outputs = lax.scan(backward_step, empty_state, block_items, reverse=True)
    grad_act, grad_inject, grad_readout = outputs
    grad_pre = grad_act.reshape(tokens, channels) * silu_slope(preact)
    padded_grad = jnp.concatenate([grad_pre, jnp.zeros((3, channels), jnp.float32)], axis=0)
    grad_input = weights[0] * padded_grad[3:3 + tokens]
    for offset in range(1, 4):
        grad_input = grad_input + weights[offset] * padded_grad[3 - offset:3 - offset + tokens]
    grad_readout = grad_readout + inter_readout
    return grad_input, grad_inject.reshape(tokens, states), grad_readout.reshape(tokens, states)
```

```python
import functools

import jax
import jax.numpy as jnp
from jax import lax
from jax.experimental import pallas as pl
from jax.experimental.pallas import tpu as pltpu
from jax.sharding import Mesh
from jax.sharding import PartitionSpec as P

f32, bf16 = jnp.float32, jnp.bfloat16
SPAN = 256
SEQ, HG = ("z", "x"), ("y", "c")
PREV = 16

NN = (((1,), (0,)), ((), ()))
NT = (((1,), (1,)), ((), ()))
TN = (((0,), (0,)), ((), ()))


def dot(a, b, dims):
    return lax.dot_general(a, b, dims, preferred_element_type=f32)


def split(v):
    high = v.astype(bf16)
    return high, (v - high.astype(f32)).astype(bf16)


def dot2(exact, v, dims):
    high, low = split(v)
    return dot(exact, high, dims) + dot(exact, low, dims)


def dot3(ah, al, bh, bl, dims):
    return dot(ah, bh, dims) + (dot(ah, bl, dims) + dot(al, bh, dims))


def places():
    return lax.broadcasted_iota(jnp.int32, (SPAN, 1), 0).astype(f32)


def grads_kernel(grad_ref, read_ref, rate_ref, after_ref, own_ref, carry):
    step, spans = pl.program_id(0), pl.num_programs(0)
    span = spans - 1 - step

    @pl.when(step == 0)
    def _():
        carry[...] = jnp.zeros_like(carry)

    rate = rate_ref[pl.ds(span, 1), :]
    lead = jnp.exp((places() + 1.0) * rate)
    after_ref[0] = carry[...]
    fresh = dot2(read_ref[...], grad_ref[...].astype(f32) * lead, TN)
    carry[...] = jnp.exp(SPAN * rate) * carry[...] + fresh

    @pl.when(step == spans - 1)
    def _():
        own_ref[...] = carry[...]


def states_kernel(
    x_ref, prev_ref, halo_ref, inject_ref, rate_ref, weight_ref, own_grad_ref,
    act_ref, slope_ref, before_ref, pay_ref, carry, rows,
):
    span, spans = pl.program_id(0), pl.num_programs(0)

    @pl.when(span == 0)
    def _():
        carry[...] = jnp.zeros_like(carry)
        rows[0:PREV, :] = halo_ref[...].astype(f32)

    @pl.when(span > 0)
    def _():
        rows[0:PREV, :] = prev_ref[...].astype(f32)

    rows[PREV : PREV + SPAN, :] = x_ref[...].astype(f32)
    weights = weight_ref[...].astype(f32)
    preact = weights[0:1] * rows[PREV - 3 : PREV - 3 + SPAN, :]
    for k in range(1, 4):
        preact = preact + weights[k : k + 1] * rows[PREV - 3 + k : PREV - 3 + k + SPAN, :]
    squashed = 1.0 / (1.0 + jnp.exp(-preact))
    act = (preact * squashed).astype(bf16)
    act_ref[...] = act
    slope_ref[...] = squashed * (1.0 + preact * (1.0 - squashed))
    rate = rate_ref[pl.ds(span, 1), :]
    tail = jnp.exp((SPAN - 1.0 - places()) * rate)
    before_ref[0] = carry[...]
    fresh = dot2(inject_ref[...], act.astype(f32) * tail, TN)
    carry[...] = jnp.exp(SPAN * rate) * carry[...] + fresh

    @pl.when(span == spans - 1)
    def _():
        chunks, height, width = pay_ref.shape
        half = width // 2
        for d in range(chunks):
            r, l = height * (d // 2), half * (d % 2)
            pay_ref[d, :, 0:half] = carry[r : r + height, l : l + half]
            pay_ref[d, :, half:width] = own_grad_ref[r : r + height, l : l + half]


def scan_kernel(own_ref, log_ref, out_ref):
    chunks, height, width = own_ref.shape
    half = width // 2
    state = jnp.zeros((height, half), f32)
    grad = jnp.zeros((height, half), f32)
    for e in range(chunks):
        out_ref[e, :, 0:half] = state
        state = jnp.exp(log_ref[e : e + 1, :]) * state + own_ref[e, :, 0:half]
    for e in reversed(range(chunks)):
        out_ref[e, :, half:width] = grad
        grad = jnp.exp(log_ref[e : e + 1, :]) * grad + own_ref[e, :, half:width]


def local_kernel(
    grad_ref, act_ref, slope_ref, inject_ref, read_ref, rate_ref, prior_ref, later_ref,
    before_ref, after_ref,
    pre_ref, factor_ref, adh_ref, adl_ref, gdh_ref, gdl_ref, gi_ref, gr_ref,
):
    span = pl.program_id(0)
    rate = rate_ref[pl.ds(span, 1), :]
    later = jnp.exp(later_ref[pl.ds(span, 1), :])
    prior = jnp.exp(prior_ref[pl.ds(span, 1), :])
    inject, read = inject_ref[...], read_ref[...]
    grad, act = grad_ref[...].astype(f32), act_ref[...].astype(f32)
    slope = slope_ref[...]
    here = places()
    rising = jnp.exp(here * rate)
    falling = jnp.exp(-here * rate)
    tail = jnp.exp((SPAN - 1.0 - here) * rate)
    lead = jnp.exp((here + 1.0) * rate)
    lower = lax.broadcasted_iota(jnp.int32, (SPAN, SPAN), 0) >= lax.broadcasted_iota(
        jnp.int32, (SPAN, SPAN), 1
    )
    grad_up = (grad * rising).astype(bf16)
    act_down = (act * falling).astype(bf16)
    pairs = jnp.where(lower, dot(grad_up, act_down, NT), 0.0).astype(bf16)
    mixing = jnp.where(lower, dot(read, inject, NT), 0.0).astype(bf16)
    grad_act = falling * dot(mixing, grad_up, TN)
    after, before = after_ref[0], before_ref[0]
    after_h, after_l = split(after)
    before_h, before_l = split(before)
    grad_act = grad_act + tail * (dot(inject, after_h, NN) + dot(inject, after_l, NN))
    pre_ref[...] = slope * grad_act
    factor_ref[...] = slope * (tail * later)
    act_tail, grad_lead = act * tail, grad * lead
    ath, atl = split(act_tail)
    glh, gll = split(grad_lead)
    gi_ref[...] = dot(pairs, read, TN) + dot3(ath, atl, after_h, after_l, NT)
    gr_ref[...] = dot(pairs, inject, NN) + dot3(glh, gll, before_h, before_l, NT)
    adh_ref[...], adl_ref[...] = split(act_tail * later)
    gdh_ref[...], gdl_ref[...] = split(grad_lead * prior)


def final_kernel(
    core_ref, back_ref, pre_ref, factor_ref, adh_ref, adl_ref, gdh_ref, gdl_ref,
    inject_ref, gi_ref, gr_ref, weight_ref,
    out_ref, both_ref, first_ref, eh, el, ah, al, rows,
):
    del core_ref
    step, spans = pl.program_id(0), pl.num_programs(0)

    @pl.when(step == 0)
    def _():
        chunks, height, width = back_ref.shape
        half = width // 2
        for d in range(chunks):
            r, l = height * (d // 2), half * (d % 2)
            h, w = split(back_ref[d, :, 0:half])
            eh[r : r + height, l : l + half] = h
            el[r : r + height, l : l + half] = w
            h, w = split(back_ref[d, :, half:width])
            ah[r : r + height, l : l + half] = h
            al[r : r + height, l : l + half] = w
        rows[SPAN : SPAN + 8, :] = jnp.zeros((8, rows.shape[1]), f32)

    @pl.when(step > 0)
    def _():
        rows[SPAN : SPAN + 8, :] = rows[0:8, :]

    inject = inject_ref[...]
    carried = dot(inject, ah[...], NN) + dot(inject, al[...], NN)
    rows[0:SPAN, :] = pre_ref[...] + factor_ref[...] * carried
    weights = weight_ref[...].astype(f32)
    summed = weights[0:1] * rows[3 : 3 + SPAN, :]
    for k in range(1, 4):
        summed = summed + weights[k : k + 1] * rows[3 - k : 3 - k + SPAN, :]
    out_ref[...] = summed
    first_ref[...] = rows[0:8, :]
    both_ref[0] = gi_ref[...] + dot3(adh_ref[...], adl_ref[...], ah[...], al[...], NT)
    both_ref[1] = gr_ref[...] + dot3(gdh_ref[...], gdl_ref[...], eh[...], el[...], NT)


def whole(shape):
    return pl.BlockSpec(shape, lambda *_: (0,) * len(shape))


def params():
    return pltpu.CompilerParams(
        dimension_semantics=("arbitrary",), vmem_limit_bytes=48 << 20
    )


def cost(flops, nbytes):
    return pl.CostEstimate(flops=flops, bytes_accessed=nbytes, transcendentals=0)


def body(nseq, ny, nc, conv_input, grad_output, inject, readout, conv_weight, decay_codes):
    tokens, channels = conv_input.shape
    heads, spans = decay_codes.shape
    width = channels // heads
    states = inject.shape[1]
    shape = jax.ShapeDtypeStruct
    chunk = (nseq, 2 * states // nseq, channels)

    up = [(i, i + 1) for i in range(nseq - 1)]
    down = [(i + 1, i) for i in range(nseq - 1)]
    halo = lax.ppermute(conv_input[tokens - PREV :], SEQ, up)

    logs = jnp.log1p(-decay_codes.astype(f32) * 1e-6)
    own_log = SPAN * jnp.sum(logs, axis=1)
    all_logs = lax.all_gather(own_log, SEQ)
    half = lax.rem(lax.axis_index(SEQ), 2)
    half_logs = jnp.where(half == 0, all_logs[:, : heads // 2], all_logs[:, heads // 2 :])
    scan_logs = jnp.repeat(half_logs, width, axis=1)
    rates = jnp.repeat(logs.T, width, axis=1)
    order = jnp.arange(spans)
    sooner = (order[None, :] < order[:, None])[:, :, None]
    prior = SPAN * jnp.sum(jnp.where(sooner, rates[None], 0.0), axis=1)
    later = SPAN * jnp.sum(jnp.where(sooner.swapaxes(0, 1), rates[None], 0.0), axis=1)

    def token_block(cols, order):
        return pl.BlockSpec((SPAN, cols), lambda s: (order(s), 0))

    def state_block(order):
        return pl.BlockSpec((1, states, channels), lambda s: (order(s), 0, 0))

    ahead = lambda s: s
    back = lambda s: spans - 1 - s
    rate_spec = whole((spans, channels))

    after, own_grad = pl.pallas_call(
        grads_kernel,
        grid=(spans,),
        in_specs=[token_block(channels, back), token_block(states, back), rate_spec],
        out_specs=[state_block(back), whole((states, channels))],
        out_shape=[shape((spans, states, channels), f32), shape((states, channels), f32)],
        scratch_shapes=[pltpu.VMEM((states, channels), f32)],
        compiler_params=params(),
        cost_estimate=cost(4 * tokens * channels * states, 5 << 20),
        name="own_grads",
    )(grad_output, readout, rates)

    tiles = SPAN // PREV
    act, slope, before, payload = pl.pallas_call(
        states_kernel,
        grid=(spans,),
        in_specs=[
            token_block(channels, ahead),
            pl.BlockSpec((PREV, channels), lambda s: (jnp.maximum(s * tiles - 1, 0), 0)),
            whole((PREV, channels)),
            token_block(states, ahead),
            rate_spec,
            whole(conv_weight.shape),
            whole((states, channels)),
        ],
        out_specs=[
            token_block(channels, ahead), token_block(channels, ahead), state_block(ahead), whole(chunk),
        ],
        out_shape=[
            shape((tokens, channels), bf16), shape((tokens, channels), f32),
            shape((spans, states, channels), f32), shape(chunk, f32),
        ],
        scratch_shapes=[pltpu.VMEM((states, channels), f32), pltpu.VMEM((PREV + SPAN, channels), f32)],
        compiler_params=params(),
        cost_estimate=cost(4 * tokens * channels * states, 11 << 20),
        name="own_states",
    )(conv_input, conv_input, halo, inject, rates, conv_weight, own_grad)

    arrived = lax.all_to_all(payload, SEQ, 0, 0, tiled=True)

    wide, narrow = token_block(channels, ahead), token_block(states, ahead)
    pre, factor, adh, adl, gdh, gdl, gi, gr = pl.pallas_call(
        local_kernel,
        grid=(spans,),
        in_specs=[wide, wide, wide, narrow, narrow, rate_spec, rate_spec, rate_spec]
        + [state_block(ahead)] * 2,
        out_specs=[wide] * 6 + [narrow] * 2,
        out_shape=[shape((tokens, channels), f32)] * 2
        + [shape((tokens, channels), bf16)] * 4
        + [shape((tokens, states), f32)] * 2,
        compiler_params=params(),
        cost_estimate=cost(20 * tokens * channels * SPAN, 32 << 20),
        name="local_terms",
    )(grad_output, act, slope, inject, readout, rates, prior, later, before, after)

    scanned = pl.pallas_call(
        scan_kernel, out_shape=shape(chunk, f32), compiler_params=pltpu.CompilerParams(vmem_limit_bytes=16 << 20),
        cost_estimate=cost(1 << 18, 1 << 20), name="carry",
    )(arrived, scan_logs)
    returned = lax.all_to_all(scanned, SEQ, 0, 0, tiled=True)

    core = lax.axis_index("c").astype(jnp.int32).reshape(1)

    def tb(cols):
        return pl.BlockSpec((SPAN, cols), lambda s, core: (spans - 1 - s, 0))

    grad_input, both, first = pl.pallas_call(
        final_kernel,
        grid_spec=pltpu.PrefetchScalarGridSpec(
            num_scalar_prefetch=1,
            grid=(spans,),
            in_specs=[whole(chunk)] + [tb(channels)] * 6 + [tb(states)] * 3 + [whole(conv_weight.shape)],
            out_specs=[
                tb(channels),
                pl.BlockSpec((2, SPAN, states), lambda s, core: (0, spans - 1 - s, 0)),
                whole((8, channels)),
            ],
            scratch_shapes=[pltpu.VMEM((states, channels), bf16)] * 4
            + [pltpu.VMEM((SPAN + 8, channels), f32)],
        ),
        out_shape=[
            shape((tokens, channels), f32), shape((2, tokens, states), f32), shape((8, channels), f32),
        ],
        compiler_params=params(),
        cost_estimate=cost(16 * tokens * channels * states, 22 << 20),
        name="carried_terms",
    )(core, returned, pre, factor, adh, adl, gdh, gdl, inject, gi, gr, conv_weight)

    next_rows = lax.ppermute(first, SEQ, down)
    weights = conv_weight.astype(f32)
    tail_rows = []
    for row in range(3):
        tail_rows.append(sum(weights[k] * next_rows[row - k] for k in range(row + 1)))
    patch = jnp.concatenate([jnp.zeros((5, channels), f32), jnp.stack(tail_rows)], axis=0)
    last = lax.slice_in_dim(grad_input, tokens - 8, tokens) + patch
    grad_input = lax.dynamic_update_slice(grad_input, last, (tokens - 8, 0))

    mine_is_first = lax.axis_index("c") == 0
    mine = jnp.where(mine_is_first, both[0], both[1])
    theirs = jnp.where(mine_is_first, both[1], both[0])
    swap = [(i, i ^ 1) for i in range(nc)]
    chip = mine + lax.ppermute(theirs, "c", swap)
    quarters = lax.all_to_all(chip.reshape(ny, tokens // ny, states), "y", 0, 0, tiled=True)
    quarter = jnp.sum(quarters, axis=0)
    spread = jnp.broadcast_to(quarter[None], (ny,) + quarter.shape)
    done = lax.all_to_all(spread, "y", 0, 0, tiled=True).reshape(tokens, states)
    other = lax.ppermute(done, "c", swap)
    grad_inject = jnp.where(mine_is_first, done, other)
    grad_readout = jnp.where(mine_is_first, other, done)
    return grad_input, grad_inject, grad_readout


def build(devices, sizes):
    fine = Mesh(devices.reshape(sizes), ("z", "x", "y", "c"))
    nz, nx, ny, nc = sizes
    return jax.shard_map(
        functools.partial(body, nz * nx, ny, nc),
        mesh=fine,
        in_specs=(P(SEQ, HG), P(SEQ, HG), P(SEQ, None), P(SEQ, None), P(None, HG), P(HG, SEQ)),
        out_specs=(P(SEQ, HG), P(SEQ, None), P(SEQ, None)),
        check_vma=False,
    )


def solution(mesh):
    return build(mesh.devices, (8, 4, 4, 2))
```

```python
import functools

import jax
import jax.numpy as jnp
from jax import lax
from jax.experimental import pallas as pl
from jax.experimental.pallas import tpu as pltpu
from jax.sharding import Mesh
from jax.sharding import PartitionSpec as P

f32, bf16 = jnp.float32, jnp.bfloat16
SPAN = 256
SEQ, HG = ("z", "x"), ("y", "c")
PREV = 16

NN = (((1,), (0,)), ((), ()))
NT = (((1,), (1,)), ((), ()))
TN = (((0,), (0,)), ((), ()))


def dot(a, b, dims):
    return lax.dot_general(a, b, dims, preferred_element_type=f32)


def split(v):
    high = v.astype(bf16)
    return high, (v - high.astype(f32)).astype(bf16)


def dot2(exact, v, dims):
    high, low = split(v)
    return dot(exact, high, dims) + dot(exact, low, dims)


def dot3(ah, al, bh, bl, dims):
    return dot(ah, bh, dims) + (dot(ah, bl, dims) + dot(al, bh, dims))


def places():
    return lax.broadcasted_iota(jnp.int32, (SPAN, 1), 0).astype(f32)


def grads_kernel(grad_ref, read_ref, rate_ref, after_ref, own_ref, carry):
    step, spans = pl.program_id(0), pl.num_programs(0)
    span = spans - 1 - step

    @pl.when(step == 0)
    def _():
        carry[...] = jnp.zeros_like(carry)

    rate = rate_ref[pl.ds(span, 1), :]
    lead = jnp.exp((places() + 1.0) * rate)
    after_ref[0] = carry[...]
    fresh = dot2(read_ref[...], grad_ref[...].astype(f32) * lead, TN)
    carry[...] = jnp.exp(SPAN * rate) * carry[...] + fresh

    @pl.when(step == spans - 1)
    def _():
        own_ref[...] = carry[...]


def rebuilt(x_ref, prev_ref, halo_ref, weight_ref, rows, span):
    @pl.when(span == 0)
    def _():
        rows[0:PREV, :] = halo_ref[...].astype(f32)

    @pl.when(span > 0)
    def _():
        rows[0:PREV, :] = prev_ref[...].astype(f32)

    rows[PREV : PREV + SPAN, :] = x_ref[...].astype(f32)
    weights = weight_ref[...].astype(f32)
    preact = weights[0:1] * rows[PREV - 3 : PREV - 3 + SPAN, :]
    for k in range(1, 4):
        preact = preact + weights[k : k + 1] * rows[PREV - 3 + k : PREV - 3 + k + SPAN, :]
    return preact, jax.nn.sigmoid(preact)


def states_kernel(
    x_ref, prev_ref, halo_ref, inject_ref, rate_ref, weight_ref, own_grad_ref, log_ref,
    before_ref, pay_ref, carry, rows,
):
    span, spans = pl.program_id(0), pl.num_programs(0)

    @pl.when(span == 0)
    def _():
        carry[...] = jnp.zeros_like(carry)

    preact, squashed = rebuilt(x_ref, prev_ref, halo_ref, weight_ref, rows, span)
    act = (preact * squashed).astype(bf16)
    rate = rate_ref[pl.ds(span, 1), :]
    tail = jnp.exp((SPAN - 1.0 - places()) * rate)
    before_ref[0] = carry[...]
    fresh = dot2(inject_ref[...], act.astype(f32) * tail, TN)
    carry[...] = jnp.exp(SPAN * rate) * carry[...] + fresh

    @pl.when(span == spans - 1)
    def _():
        chunks, height, _ = pay_ref.shape
        half = carry.shape[1] // 2
        for d in range(chunks):
            r, l = height * (d // 2), half * (d % 2)
            pay_ref[d, :, 0:half] = carry[r : r + height, l : l + half]
            pay_ref[d, :, half : 2 * half] = own_grad_ref[r : r + height, l : l + half]
            for row in range(half // 128):
                at = l + 128 * row
                pay_ref[d, row : row + 1, 2 * half : 2 * half + 128] = log_ref[:, at : at + 128]


def scan_kernel(own_ref, out_ref):
    chunks, height, width = out_ref.shape
    half = width // 2

    def gain(e):
        logs = [own_ref[e, r : r + 1, width : width + 128] for r in range(half // 128)]
        return jnp.exp(jnp.concatenate(logs, axis=1))

    state = jnp.zeros((height, half), f32)
    grad = jnp.zeros((height, half), f32)
    for e in range(chunks):
        out_ref[e, :, 0:half] = state
        state = gain(e) * state + own_ref[e, :, 0:half]
    for e in reversed(range(chunks)):
        out_ref[e, :, half:width] = grad
        grad = gain(e) * grad + own_ref[e, :, half:width]


def causal():
    row = lax.broadcasted_iota(jnp.int32, (SPAN, SPAN), 0)
    return row >= lax.broadcasted_iota(jnp.int32, (SPAN, SPAN), 1)


def local_input_kernel(
    x_ref, prev_ref, halo_ref, grad_ref, inject_ref, read_ref, rate_ref, later_ref,
    after_ref, weight_ref,
    act_ref, pre_ref, factor_ref, rows,
):
    span = pl.program_id(0)
    preact, squashed = rebuilt(x_ref, prev_ref, halo_ref, weight_ref, rows, span)
    act_ref[...] = (preact * squashed).astype(bf16)
    slope = squashed * (1.0 + preact * (1.0 - squashed))
    rate = rate_ref[pl.ds(span, 1), :]
    later = jnp.exp(later_ref[pl.ds(span, 1), :])
    inject, read = inject_ref[...], read_ref[...]
    here = places()
    falling = jnp.exp(-here * rate)
    end = jnp.exp((SPAN - 1.0) * rate)
    grad_up = (grad_ref[...].astype(f32) * jnp.exp(here * rate)).astype(bf16)
    mixing = jnp.where(causal(), dot(read, inject, NT), 0.0).astype(bf16)
    high, low = split(after_ref[0] * end)
    stacked = jnp.concatenate([high, low], axis=0)
    doubled = jnp.concatenate([inject, inject], axis=1)
    steep = slope * falling
    pre_ref[...] = steep * (dot(mixing, grad_up, TN) + dot(doubled, stacked, NN))
    factor_ref[...] = steep * (end * later)


def wide_product(high, low, both, states):
    wide = dot(high, both, NT)
    return wide[:, :states] + (wide[:, states:] + dot(low, both[0:states, :], NT))


def local_shared_kernel(
    grad_ref, act_ref, inject_ref, read_ref, rate_ref, prior_ref, later_ref,
    before_ref, after_ref,
    adh_ref, adl_ref, gdh_ref, gdl_ref, gi_ref, gr_ref,
):
    span = pl.program_id(0)
    rate = rate_ref[pl.ds(span, 1), :]
    later = later_ref[pl.ds(span, 1), :]
    prior = prior_ref[pl.ds(span, 1), :]
    inject, read = inject_ref[...], read_ref[...]
    states = inject.shape[1]
    here = places()
    up = grad_ref[...].astype(f32) * jnp.exp(here * rate)
    down = act_ref[...].astype(f32) * jnp.exp(-here * rate)
    uph, upl = split(up)
    downh, downl = split(down)
    pairs = jnp.where(causal(), dot(uph, downh, NT), 0.0).astype(bf16)
    afters = jnp.concatenate(split(after_ref[0] * jnp.exp((SPAN - 1.0) * rate)), axis=0)
    befores = jnp.concatenate(split(before_ref[0] * jnp.exp(rate)), axis=0)
    gi_ref[...] = dot(pairs, read, TN) + wide_product(downh, downl, afters, states)
    gr_ref[...] = dot(pairs, inject, NN) + wide_product(uph, upl, befores, states)
    adh_ref[...], adl_ref[...] = split(down * jnp.exp((SPAN - 1.0) * rate + later))
    gdh_ref[...], gdl_ref[...] = split(up * jnp.exp(rate + prior))


def unpacked(back_ref, high, low, grads):
    chunks, height, width = back_ref.shape
    half = width // 2
    start = half if grads else 0
    states = high.shape[0] // 2 if low is None else high.shape[0]
    for d in range(chunks):
        r, l = height * (d // 2), half * (d % 2)
        h, w = split(back_ref[d, :, start : start + half])
        high[r : r + height, l : l + half] = h
        if low is None:
            high[states + r : states + r + height, l : l + half] = w
        else:
            low[r : r + height, l : l + half] = w


def shared_kernel(
    core_ref, back_ref, adh_ref, adl_ref, gdh_ref, gdl_ref, gi_ref, gr_ref,
    mine_ref, theirs_ref, grads, carried,
):
    @pl.when(pl.program_id(0) == 0)
    def _():
        unpacked(back_ref, grads, None, True)
        unpacked(back_ref, carried, None, False)

    states = gi_ref.shape[1]
    gi = gi_ref[...] + wide_product(adh_ref[...], adl_ref[...], grads[...], states)
    gr = gr_ref[...] + wide_product(gdh_ref[...], gdl_ref[...], carried[...], states)
    first = core_ref[0] == 0
    mine_ref[...] = jnp.where(first, gi, gr)
    theirs_ref[...] = jnp.where(first, gr, gi)


def input_kernel(
    back_ref, pre_ref, factor_ref, inject_ref, weight_ref, out_ref, first_ref, grads, rows
):
    @pl.when(pl.program_id(0) == 0)
    def _():
        unpacked(back_ref, grads, None, True)
        rows[SPAN : SPAN + 8, :] = jnp.zeros((8, rows.shape[1]), f32)

    @pl.when(pl.program_id(0) > 0)
    def _():
        rows[SPAN : SPAN + 8, :] = rows[0:8, :]

    inject = inject_ref[...]
    carried = dot(jnp.concatenate([inject, inject], axis=1), grads[...], NN)
    rows[0:SPAN, :] = pre_ref[...] + factor_ref[...] * carried
    weights = weight_ref[...].astype(f32)
    summed = weights[0:1] * rows[3 : 3 + SPAN, :]
    for k in range(1, 4):
        summed = summed + weights[k : k + 1] * rows[3 - k : 3 - k + SPAN, :]
    out_ref[...] = summed
    first_ref[...] = rows[0:8, :]


def whole(shape):
    return pl.BlockSpec(shape, lambda *_: (0,) * len(shape))


def params(mib=53):
    return pltpu.CompilerParams(vmem_limit_bytes=mib << 20)


def cost(flops, nbytes):
    return pl.CostEstimate(flops=flops, bytes_accessed=nbytes, transcendentals=0)


def body(nseq, ny, nc, conv_input, grad_output, inject, readout, conv_weight, decay_codes):
    tokens, channels = conv_input.shape
    heads, spans = decay_codes.shape
    width = channels // heads
    states = inject.shape[1]
    shape = jax.ShapeDtypeStruct
    height = 2 * states // nseq
    chunk = (nseq, height, channels)

    up = [(i, i + 1) for i in range(nseq - 1)]
    down = [(i + 1, i) for i in range(nseq - 1)]
    halo = lax.ppermute(conv_input[tokens - PREV :], SEQ, up)

    logs = jnp.log1p(-decay_codes.astype(f32) * 1e-6)
    rates = jnp.repeat(logs.T, width, axis=1)
    own_log = SPAN * jnp.sum(rates, axis=0, keepdims=True)
    order = jnp.arange(spans)
    sooner = (order[None, :] < order[:, None])[:, :, None]
    prior = SPAN * jnp.sum(jnp.where(sooner, rates[None], 0.0), axis=1)
    later = SPAN * jnp.sum(jnp.where(sooner.swapaxes(0, 1), rates[None], 0.0), axis=1)

    def token_block(cols, order):
        return pl.BlockSpec((SPAN, cols), lambda s, *_: (order(s), 0))

    def state_block(order):
        return pl.BlockSpec((1, states, channels), lambda s: (order(s), 0, 0))

    ahead = lambda s: s
    back = lambda s: spans - 1 - s
    rate_spec = whole((spans, channels))
    tiles = SPAN // PREV
    x_specs = [
        token_block(channels, ahead),
        pl.BlockSpec((PREV, channels), lambda s: (jnp.maximum(s * tiles - 1, 0), 0)),
        whole((PREV, channels)),
    ]
    wide, narrow = token_block(channels, ahead), token_block(states, ahead)
    rows = pltpu.VMEM((PREV + SPAN, channels), f32)

    after, own_grad = pl.pallas_call(
        grads_kernel,
        grid=(spans,),
        in_specs=[token_block(channels, back), token_block(states, back), rate_spec],
        out_specs=[state_block(back), whole((states, channels))],
        out_shape=[shape((spans, states, channels), f32), shape((states, channels), f32)],
        scratch_shapes=[pltpu.VMEM((states, channels), f32)],
        compiler_params=params(),
        cost_estimate=cost(4 * tokens * channels * states, 5 << 20),
        name="own_grads",
    )(grad_output, readout, rates)

    before, payload = pl.pallas_call(
        states_kernel,
        grid=(spans,),
        in_specs=x_specs
        + [narrow, rate_spec, whole(conv_weight.shape), whole((states, channels)), whole((1, channels))],
        out_specs=[state_block(ahead), whole((nseq, height, channels + 128))],
        out_shape=[
            shape((spans, states, channels), f32), shape((nseq, height, channels + 128), f32),
        ],
        scratch_shapes=[pltpu.VMEM((states, channels), f32), rows],
        compiler_params=params(),
        cost_estimate=cost(4 * tokens * channels * states, 11 << 20),
        name="own_states",
    )(conv_input, conv_input, halo, inject, rates, conv_weight, own_grad, own_log)

    arrived = lax.all_to_all(payload, SEQ, 0, 0, tiled=True)

    act, pre, factor = pl.pallas_call(
        local_input_kernel,
        grid=(spans,),
        in_specs=x_specs + [wide, narrow, narrow, rate_spec, rate_spec, state_block(ahead)]
        + [whole(conv_weight.shape)],
        out_specs=[wide] * 3,
        out_shape=[shape((tokens, channels), bf16)] + [shape((tokens, channels), f32)] * 2,
        scratch_shapes=[rows],
        compiler_params=params(),
        cost_estimate=cost(8 * tokens * channels * SPAN, 18 << 20),
        name="local_input",
    )(
        conv_input, conv_input, halo, grad_output, inject, readout, rates, later,
        after, conv_weight,
    )
    arrived, act = lax.optimization_barrier((arrived, act))

    adh, adl, gdh, gdl, gi, gr = pl.pallas_call(
        local_shared_kernel,
        grid=(spans,),
        in_specs=[wide, wide, narrow, narrow, rate_spec, rate_spec, rate_spec]
        + [state_block(ahead)] * 2,
        out_specs=[wide] * 4 + [narrow] * 2,
        out_shape=[shape((tokens, channels), bf16)] * 4 + [shape((tokens, states), f32)] * 2,
        compiler_params=params(),
        cost_estimate=cost(12 * tokens * channels * SPAN, 19 << 20),
        name="local_shared",
    )(grad_output, act, inject, readout, rates, prior, later, before, after)

    scanned = pl.pallas_call(
        scan_kernel, out_shape=shape(chunk, f32), compiler_params=params(8),
        cost_estimate=cost(1 << 18, 1 << 20), name="carry",
    )(arrived)
    returned = lax.all_to_all(scanned, SEQ, 0, 0, tiled=True)

    core = lax.axis_index("c").astype(jnp.int32).reshape(1)
    mine, theirs = pl.pallas_call(
        shared_kernel,
        grid_spec=pltpu.PrefetchScalarGridSpec(
            num_scalar_prefetch=1,
            grid=(spans,),
            in_specs=[whole(chunk)] + [wide] * 4 + [narrow] * 2,
            out_specs=[narrow, narrow],
            scratch_shapes=[pltpu.VMEM((2 * states, channels), bf16)] * 2,
        ),
        out_shape=[shape((tokens, states), f32)] * 2,
        compiler_params=params(),
        cost_estimate=cost(12 * tokens * channels * states, 13 << 20),
        name="shared_terms",
    )(core, returned, adh, adl, gdh, gdl, gi, gr)

    swap = [(i, i ^ 1) for i in range(nc)]
    chip = mine + lax.ppermute(theirs, "c", swap)
    here = lax.axis_index("y")
    part = tokens // ny

    def turn(array, by):
        return lax.ppermute(array, "y", [(i, (i + by) % ny) for i in range(ny)])

    def cut(array, which):
        return lax.dynamic_slice_in_dim(array, lax.rem(here + which, ny) * part, part)

    sent = [turn(cut(chip, by).astype(bf16), by) for by in range(1, ny)]

    grad_input, first = pl.pallas_call(
        input_kernel,
        grid=(spans,),
        in_specs=[
            whole(chunk), token_block(channels, back), token_block(channels, back),
            token_block(states, back), whole(conv_weight.shape),
        ],
        out_specs=[token_block(channels, back), whole((8, channels))],
        out_shape=[shape((tokens, channels), f32), shape((8, channels), f32)],
        scratch_shapes=[
            pltpu.VMEM((2 * states, channels), bf16), pltpu.VMEM((SPAN + 8, channels), f32),
        ],
        compiler_params=params(),
        cost_estimate=cost(4 * tokens * channels * states, 13 << 20),
        name="input_grads",
    )(returned, pre, factor, inject, conv_weight)

    *sent, first = lax.optimization_barrier((*sent, first))
    quarter = cut(chip, 0)
    for piece in sent:
        quarter = quarter + piece.astype(f32)
    quarter = quarter.astype(bf16)
    done = jnp.zeros((tokens, states), bf16)
    for by in range(ny):
        piece = quarter if by == 0 else turn(quarter, by)
        done = lax.dynamic_update_slice_in_dim(
            done, piece, lax.rem(here - by + ny, ny) * part, 0
        )
    other = lax.ppermute(done, "c", swap)
    mine_is_first = lax.axis_index("c") == 0
    grad_inject = jnp.where(mine_is_first, done, other).astype(f32)
    grad_readout = jnp.where(mine_is_first, other, done).astype(f32)

    next_rows = lax.ppermute(first, SEQ, down)
    weights = conv_weight.astype(f32)
    tail_rows = []
    for row in range(3):
        tail_rows.append(sum(weights[k] * next_rows[row - k] for k in range(row + 1)))
    patch = jnp.concatenate([jnp.zeros((5, channels), f32), jnp.stack(tail_rows)], axis=0)
    last = lax.slice_in_dim(grad_input, tokens - 8, tokens) + patch
    grad_input = lax.dynamic_update_slice(grad_input, last, (tokens - 8, 0))
    return grad_input, grad_inject, grad_readout


def build(devices, sizes):
    fine = Mesh(devices.reshape(sizes), ("z", "x", "y", "c"))
    nz, nx, ny, nc = sizes
    return jax.shard_map(
        functools.partial(body, nz * nx, ny, nc),
        mesh=fine,
        in_specs=(P(SEQ, HG), P(SEQ, HG), P(SEQ, None), P(SEQ, None), P(None, HG), P(HG, SEQ)),
        out_specs=(P(SEQ, HG), P(SEQ, None), P(SEQ, None)),
        check_vma=False,
    )


def solution(mesh):
    return build(mesh.devices, (8, 4, 4, 2))
```

```python
import functools

import jax
import jax.numpy as jnp
from jax import lax
from jax.experimental import pallas as pl
from jax.experimental.pallas import tpu as pltpu
from jax.sharding import Mesh
from jax.sharding import PartitionSpec as P

f32, bf16 = jnp.float32, jnp.bfloat16
SPAN = 256
SEQ, HG = ("z", "x"), ("y", "c")
PREV = 16

NN = (((1,), (0,)), ((), ()))
NT = (((1,), (1,)), ((), ()))
TN = (((0,), (0,)), ((), ()))


def dot(a, b, dims):
    return lax.dot_general(a, b, dims, preferred_element_type=f32)


def split(v):
    high = v.astype(bf16)
    return high, (v - high.astype(f32)).astype(bf16)


def dot2(exact, v, dims):
    high, low = split(v)
    return dot(exact, high, dims) + dot(exact, low, dims)


def dot3(ah, al, bh, bl, dims):
    return dot(ah, bh, dims) + (dot(ah, bl, dims) + dot(al, bh, dims))


def places():
    return lax.broadcasted_iota(jnp.int32, (SPAN, 1), 0).astype(f32)


def span_at(span):
    return pl.ds(pl.multiple_of(span * SPAN, SPAN), SPAN)


def each_span(spans, step, backwards=False):
    def visit(i, _):
        step(spans - 1 - i if backwards else i)
        return 0

    lax.fori_loop(0, spans, visit, 0)


def by_span(source, target, sems):
    def piece(span):
        if len(source.shape) == 3:
            return pltpu.make_async_copy(source.at[span], target.at[span], sems.at[span])
        rows = span_at(span)
        return pltpu.make_async_copy(source.at[rows, :], target.at[rows, :], sems.at[span])

    return piece


def fetch(spans, whole, pieces, backwards=False):
    for copy in whole:
        copy.start()
    for i in range(spans):
        for piece in pieces:
            piece(spans - 1 - i if backwards else i).start()
    for copy in whole:
        copy.wait()


def drain(spans, pieces):
    for span in range(spans):
        for piece in pieces:
            piece(span).wait()


def grads_kernel(
    code_hbm, grad_hbm, read_hbm, rate_ref, prior_ref, later_ref, log_ref, carry,
    code_ref, grad_ref, read_ref, csem, gsem, rsem,
):
    heads, spans = code_ref.shape
    channels = carry.shape[1]
    pieces = [by_span(grad_hbm, grad_ref, gsem), by_span(read_hbm, read_ref, rsem)]
    fetch(spans, [pltpu.make_async_copy(code_hbm, code_ref, csem)], pieces, backwards=True)
    logs = jnp.log1p(-code_ref[...].astype(f32) * 1e-6)
    lane = lax.broadcasted_iota(jnp.int32, (heads, channels), 1)
    row = lax.broadcasted_iota(jnp.int32, (heads, channels), 0)
    width = channels // heads
    owns = jnp.where((lane >= row * width) & (lane < (row + 1) * width), 1.0, 0.0)
    rate_ref[...] = lax.dot_general(
        logs, owns, TN, precision=lax.Precision.HIGHEST, preferred_element_type=f32
    )
    total = jnp.zeros((1, channels), f32)
    for span in range(spans):
        prior_ref[span : span + 1, :] = total
        total = total + SPAN * rate_ref[span : span + 1, :]
    log_ref[...] = total
    total = jnp.zeros((1, channels), f32)
    for span in reversed(range(spans)):
        later_ref[span : span + 1, :] = total
        total = total + SPAN * rate_ref[span : span + 1, :]
    carry[...] = jnp.zeros_like(carry)

    def step(span):
        for piece in pieces:
            piece(span).wait()
        rate = rate_ref[pl.ds(span, 1), :]
        up = grad_ref[span_at(span), :].astype(f32) * jnp.exp(places() * rate)
        fresh = dot2(read_ref[span_at(span), :], up, TN)
        carry[...] = jnp.exp(SPAN * rate) * carry[...] + jnp.exp(rate) * fresh

    each_span(spans, step, backwards=True)


def convolved(x, before, weights):
    rows = jnp.concatenate([before, x], axis=0)
    preact = weights[0:1] * pltpu.roll(rows, 3, axis=0)[8:]
    for k in range(1, 3):
        preact = preact + weights[k : k + 1] * pltpu.roll(rows, 3 - k, axis=0)[8:]
    return preact + weights[3:4] * x


def states_kernel(
    x_hbm, halo_hbm, inject_hbm, rate_hbm, weight_hbm, own_grad_hbm, log_hbm,
    pay_ref,
    x_ref, halo_ref, inject_ref, rate_ref, weight_ref, own_grad_ref, log_ref, carry, prev,
    xsem, isem, sems,
):
    spans = rate_ref.shape[0]
    pieces = [by_span(x_hbm, x_ref, xsem), by_span(inject_hbm, inject_ref, isem)]
    late = pltpu.make_async_copy(own_grad_hbm, own_grad_ref, sems.at[4])
    fetch(
        spans,
        [
            pltpu.make_async_copy(halo_hbm, halo_ref, sems.at[0]),
            pltpu.make_async_copy(rate_hbm, rate_ref, sems.at[1]),
            pltpu.make_async_copy(weight_hbm, weight_ref, sems.at[2]),
            pltpu.make_async_copy(log_hbm, log_ref, sems.at[3]),
        ],
        pieces,
    )
    late.start()
    carry[...] = jnp.zeros_like(carry)
    prev[...] = halo_ref[...].astype(f32)[PREV - 8 :]
    weights = weight_ref[...].astype(f32)

    def step(span):
        for piece in pieces:
            piece(span).wait()
        x = x_ref[span_at(span), :].astype(f32)
        preact = convolved(x, prev[...], weights)
        prev[...] = x[SPAN - 8 :]
        act = (preact * jax.nn.sigmoid(preact)).astype(bf16)
        rate = rate_ref[pl.ds(span, 1), :]
        tail = jnp.exp((SPAN - 1.0 - places()) * rate)
        fresh = dot2(inject_ref[span_at(span), :], act.astype(f32) * tail, TN)
        carry[...] = jnp.exp(SPAN * rate) * carry[...] + fresh

    each_span(spans, step)
    late.wait()
    chunks, height, _ = pay_ref.shape
    half = carry.shape[1] // 2
    for d in range(chunks):
        r, l = height * (d // 2), half * (d % 2)
        pay_ref[d, :, 0:half] = carry[r : r + height, l : l + half]
        pay_ref[d, :, half : 2 * half] = own_grad_ref[r : r + height, l : l + half]
        for row in range(half // 128):
            at = l + 128 * row
            pay_ref[d, row : row + 1, 2 * half : 2 * half + 128] = log_ref[:, at : at + 128]


def scan_kernel(own_ref, out_ref):
    chunks, height, width = out_ref.shape
    half = width // 2

    def gain(e):
        logs = [own_ref[e, r : r + 1, width : width + 128] for r in range(half // 128)]
        return jnp.exp(jnp.concatenate(logs, axis=1))

    state = jnp.zeros((height, half), f32)
    grad = jnp.zeros((height, half), f32)
    for e in range(chunks):
        out_ref[e, :, 0:half] = state
        state = gain(e) * state + own_ref[e, :, 0:half]
    for e in reversed(range(chunks)):
        out_ref[e, :, half:width] = grad
        grad = gain(e) * grad + own_ref[e, :, half:width]


def causal():
    row = lax.broadcasted_iota(jnp.int32, (SPAN, SPAN), 0)
    return row >= lax.broadcasted_iota(jnp.int32, (SPAN, SPAN), 1)


def local_input_kernel(
    x_hbm, halo_hbm, grad_hbm, inject_hbm, read_hbm, rate_hbm, later_hbm, weight_hbm,
    act_hbm, pre_hbm, factor_hbm, after_hbm,
    x_ref, halo_ref, grad_ref, inject_ref, read_ref, rate_ref, later_ref, weight_ref,
    act_ref, pre_ref, factor_ref, after_ref, carry,
    xsem, gsem, isem, rsem, sems, osems,
):
    spans = rate_ref.shape[0]
    pieces = [
        by_span(x_hbm, x_ref, xsem), by_span(grad_hbm, grad_ref, gsem),
        by_span(inject_hbm, inject_ref, isem), by_span(read_hbm, read_ref, rsem),
    ]
    outs = [
        by_span(act_ref, act_hbm, osems.at[0]), by_span(pre_ref, pre_hbm, osems.at[1]),
        by_span(factor_ref, factor_hbm, osems.at[2]), by_span(after_ref, after_hbm, osems.at[3]),
    ]
    fetch(
        spans,
        [
            pltpu.make_async_copy(halo_hbm, halo_ref, sems.at[0]),
            pltpu.make_async_copy(rate_hbm, rate_ref, sems.at[1]),
            pltpu.make_async_copy(weight_hbm, weight_ref, sems.at[2]),
            pltpu.make_async_copy(later_hbm, later_ref, sems.at[3]),
        ],
        pieces,
        backwards=True,
    )
    carry[...] = jnp.zeros_like(carry)
    weights = weight_ref[...].astype(f32)
    pieces[0](spans - 1).wait()

    def step(span):
        @pl.when(span > 0)
        def _():
            pieces[0](jnp.maximum(span - 1, 0)).wait()

        for piece in pieces[1:]:
            piece(span).wait()
        rows = span_at(span)
        x = x_ref[rows, :].astype(f32)
        start = pl.multiple_of(jnp.maximum(span * SPAN - PREV, 0), PREV)
        last = jnp.where(span == 0, halo_ref[...].astype(f32), x_ref[pl.ds(start, PREV), :].astype(f32))
        preact = convolved(x, last[PREV - 8 :], weights)
        squashed = jax.nn.sigmoid(preact)
        act_ref[rows, :] = (preact * squashed).astype(bf16)
        slope = squashed * (1.0 + preact * (1.0 - squashed))
        rate = rate_ref[pl.ds(span, 1), :]
        later = jnp.exp(later_ref[pl.ds(span, 1), :])
        inject, read = inject_ref[rows, :], read_ref[rows, :]
        here = places()
        steep = slope * jnp.exp(-here * rate)
        end = jnp.exp((SPAN - 1.0) * rate)
        up_high, up_low = split(grad_ref[rows, :].astype(f32) * jnp.exp(here * rate))
        mixing = jnp.where(causal(), dot(read, inject, NT), 0.0).astype(bf16)
        after = carry[...]
        after_ref[span] = after
        stacked = jnp.concatenate(split(after * end), axis=0)
        doubled = jnp.concatenate([inject, inject], axis=1)
        pre_ref[rows, :] = steep * (dot(mixing, up_high, TN) + dot(doubled, stacked, NN))
        factor_ref[rows, :] = steep * (end * later)
        fresh = dot(read, up_high, TN) + dot(read, up_low, TN)
        carry[...] = jnp.exp(SPAN * rate) * after + jnp.exp(rate) * fresh
        for out in outs:
            out(span).start()

    each_span(spans, step, backwards=True)
    drain(spans, outs)


def wide_product(high, low, both, states):
    wide = dot(high, both, NT)
    return wide[:, :states] + (wide[:, states:] + dot(low, both[0:states, :], NT))


def local_shared_kernel(
    grad_hbm, act_hbm, inject_hbm, read_hbm, after_hbm, rate_hbm, prior_hbm, later_hbm,
    adh_hbm, adl_hbm, gdh_hbm, gdl_hbm, gi_hbm, gr_hbm,
    grad_ref, act_ref, inject_ref, read_ref, after_ref, rate_ref, prior_ref, later_ref,
    adh_ref, adl_ref, gdh_ref, gdl_ref, gi_ref, gr_ref, carry,
    isems, sems, osems,
):
    spans = rate_ref.shape[0]
    sources = [grad_hbm, act_hbm, inject_hbm, read_hbm, after_hbm]
    targets = [grad_ref, act_ref, inject_ref, read_ref, after_ref]
    pieces = [by_span(a, b, isems.at[k]) for k, (a, b) in enumerate(zip(sources, targets))]
    made = [adh_ref, adl_ref, gdh_ref, gdl_ref, gi_ref, gr_ref]
    places_to = [adh_hbm, adl_hbm, gdh_hbm, gdl_hbm, gi_hbm, gr_hbm]
    outs = [by_span(a, b, osems.at[k]) for k, (a, b) in enumerate(zip(made, places_to))]
    fetch(
        spans,
        [
            pltpu.make_async_copy(rate_hbm, rate_ref, sems.at[0]),
            pltpu.make_async_copy(prior_hbm, prior_ref, sems.at[1]),
            pltpu.make_async_copy(later_hbm, later_ref, sems.at[2]),
        ],
        pieces,
    )
    carry[...] = jnp.zeros_like(carry)

    def step(span):
        for piece in pieces:
            piece(span).wait()
        rows = span_at(span)
        rate = rate_ref[pl.ds(span, 1), :]
        later = later_ref[pl.ds(span, 1), :]
        prior = prior_ref[pl.ds(span, 1), :]
        inject, read = inject_ref[rows, :], read_ref[rows, :]
        states = inject.shape[1]
        here = places()
        up = grad_ref[rows, :].astype(f32) * jnp.exp(here * rate)
        down = act_ref[rows, :].astype(f32) * jnp.exp(-here * rate)
        uph, upl = split(up)
        downh, downl = split(down)
        pairs = jnp.where(causal(), dot(uph, downh, NT), 0.0).astype(bf16)
        end = jnp.exp((SPAN - 1.0) * rate)
        afters = jnp.concatenate(split(after_ref[span] * end), axis=0)
        before = carry[...]
        befores = jnp.concatenate(split(before * jnp.exp(rate)), axis=0)
        gi_ref[rows, :] = dot(pairs, read, TN) + wide_product(downh, downl, afters, states)
        gr_ref[rows, :] = dot(pairs, inject, NN) + wide_product(uph, upl, befores, states)
        fresh = dot(inject, downh, TN) + dot(inject, downl, TN)
        carry[...] = jnp.exp(SPAN * rate) * before + end * fresh
        adh_ref[rows, :], adl_ref[rows, :] = split(down * jnp.exp((SPAN - 1.0) * rate + later))
        gdh_ref[rows, :], gdl_ref[rows, :] = split(up * jnp.exp(rate + prior))
        for out in outs:
            out(span).start()

    each_span(spans, step)
    drain(spans, outs)


def unpacked(back_ref, high, low, grads):
    chunks, height, width = back_ref.shape
    half = width // 2
    start = half if grads else 0
    states = high.shape[0] // 2 if low is None else high.shape[0]
    for d in range(chunks):
        r, l = height * (d // 2), half * (d % 2)
        h, w = split(back_ref[d, :, start : start + half])
        high[r : r + height, l : l + half] = h
        if low is None:
            high[states + r : states + r + height, l : l + half] = w
        else:
            low[r : r + height, l : l + half] = w


def shared_kernel(
    core_ref, back_ref, adh_hbm, adl_hbm, gdh_hbm, gdl_hbm, gi_hbm, gr_hbm,
    mine_ref, theirs_ref,
    adh_ref, adl_ref, gdh_ref, gdl_ref, gi_ref, gr_ref, grads, carried, isems,
):
    tokens, states = gi_ref.shape
    spans = tokens // SPAN
    sources = [adh_hbm, adl_hbm, gdh_hbm, gdl_hbm, gi_hbm, gr_hbm]
    targets = [adh_ref, adl_ref, gdh_ref, gdl_ref, gi_ref, gr_ref]
    pieces = [by_span(a, b, isems.at[k]) for k, (a, b) in enumerate(zip(sources, targets))]
    fetch(spans, [], pieces)
    unpacked(back_ref, grads, None, True)
    unpacked(back_ref, carried, None, False)
    first = core_ref[0] == 0

    def step(span):
        for piece in pieces:
            piece(span).wait()
        rows = span_at(span)
        gi = gi_ref[rows, :] + wide_product(adh_ref[rows, :], adl_ref[rows, :], grads[...], states)
        gr = gr_ref[rows, :] + wide_product(gdh_ref[rows, :], gdl_ref[rows, :], carried[...], states)
        mine_ref[rows, :] = jnp.where(first, gi, gr)
        theirs_ref[rows, :] = jnp.where(first, gr, gi)

    each_span(spans, step)


def input_kernel(
    back_ref, pre_hbm, factor_hbm, inject_hbm, weight_ref,
    out_hbm, first_ref,
    pre_ref, factor_ref, inject_ref, grads, after, made, isems, osems,
):
    spans = pre_ref.shape[0] // SPAN
    pieces = [
        by_span(pre_hbm, pre_ref, isems.at[0]), by_span(factor_hbm, factor_ref, isems.at[1]),
        by_span(inject_hbm, inject_ref, isems.at[2]),
    ]
    out = by_span(made, out_hbm, osems)
    fetch(spans, [], pieces, backwards=True)
    unpacked(back_ref, grads, None, True)
    after[...] = jnp.zeros_like(after)
    weights = weight_ref[...].astype(f32)

    def step(span):
        for piece in pieces:
            piece(span).wait()
        rows = span_at(span)
        inject = inject_ref[rows, :]
        carried = dot(jnp.concatenate([inject, inject], axis=1), grads[...], NN)
        now = pre_ref[rows, :] + factor_ref[rows, :] * carried
        joined = jnp.concatenate([now, after[...]], axis=0)
        summed = weights[3:4] * now
        for k in range(3):
            ahead = pltpu.roll(joined, SPAN + 8 - (3 - k), axis=0)[:SPAN]
            summed = summed + weights[k : k + 1] * ahead
        after[...] = now[0:8]
        made[rows, :] = summed
        out(span).start()

    each_span(spans, step, backwards=True)
    first_ref[...] = after[...]
    drain(spans, [out])


def params(mib=53):
    return pltpu.CompilerParams(vmem_limit_bytes=mib << 20)


def cost(flops, nbytes):
    return pl.CostEstimate(flops=flops, bytes_accessed=nbytes, transcendentals=0)


def body(nseq, ny, nc, conv_input, grad_output, inject, readout, conv_weight, decay_codes):
    tokens, channels = conv_input.shape
    spans = decay_codes.shape[1]
    states = inject.shape[1]
    shape = jax.ShapeDtypeStruct
    height = 2 * states // nseq
    chunk = (nseq, height, channels)
    smem = pl.BlockSpec(memory_space=pltpu.SMEM)
    wide, wide16 = shape((tokens, channels), f32), shape((tokens, channels), bf16)
    narrow, row = shape((tokens, states), f32), shape((spans, channels), f32)
    local = shape((spans, states, channels), f32)
    state = shape((states, channels), f32)

    up = [(i, i + 1) for i in range(nseq - 1)]
    down = [(i + 1, i) for i in range(nseq - 1)]
    halo = lax.ppermute(conv_input[tokens - PREV :], SEQ, up)

    anywhere = pl.BlockSpec(memory_space=pl.ANY)
    hbm = pl.BlockSpec(memory_space=pltpu.HBM)
    plain = pl.BlockSpec()
    wide_v, wide16_v = pltpu.VMEM(wide.shape, f32), pltpu.VMEM(wide.shape, bf16)
    narrow_v, narrow16_v = pltpu.VMEM(narrow.shape, f32), pltpu.VMEM(narrow.shape, bf16)
    row_v, state_v = pltpu.VMEM(row.shape, f32), pltpu.VMEM(state.shape, f32)
    local_v = pltpu.VMEM(local.shape, f32)
    halo_v, weight_v = pltpu.VMEM((PREV, channels), bf16), pltpu.VMEM(conv_weight.shape, bf16)
    dma = pltpu.SemaphoreType.DMA

    rates, prior, later, own_log, own_grad = pl.pallas_call(
        grads_kernel,
        in_specs=[hbm] * 3,
        out_specs=[plain] * 5,
        out_shape=[row, row, row, shape((1, channels), f32), state],
        scratch_shapes=[
            pltpu.VMEM(decay_codes.shape, jnp.int32), wide16_v, narrow16_v,
            dma, dma((spans,)), dma((spans,)),
        ],
        compiler_params=params(),
        cost_estimate=cost(4 * tokens * channels * states, 3 << 20),
        name="own_grads",
    )(decay_codes, grad_output, readout)

    payload = pl.pallas_call(
        states_kernel,
        in_specs=[hbm, anywhere, hbm, anywhere, hbm, anywhere, anywhere],
        out_specs=plain,
        out_shape=shape((nseq, height, channels + 128), f32),
        scratch_shapes=[
            wide16_v, halo_v, narrow16_v, row_v, weight_v, state_v, pltpu.VMEM((1, channels), f32),
            state_v, pltpu.VMEM((8, channels), f32), dma((spans,)), dma((spans,)), dma((5,)),
        ],
        compiler_params=params(),
        cost_estimate=cost(4 * tokens * channels * states, 4 << 20),
        name="own_states",
    )(conv_input, halo, inject, rates, conv_weight, own_grad, own_log)

    arrived = lax.all_to_all(payload, SEQ, 0, 0, tiled=True)

    act, pre, factor, after = pl.pallas_call(
        local_input_kernel,
        in_specs=[hbm, anywhere, hbm, hbm, hbm, anywhere, anywhere, hbm],
        out_specs=[hbm] * 4,
        out_shape=[wide16, wide, wide, local],
        scratch_shapes=[
            wide16_v, halo_v, wide16_v, narrow16_v, narrow16_v, row_v, row_v, weight_v,
            wide16_v, wide_v, wide_v, local_v, state_v,
        ]
        + [dma((spans,))] * 4 + [dma((4,)), dma((4, spans))],
        compiler_params=params(),
        cost_estimate=cost(8 * tokens * channels * SPAN, 18 << 20),
        name="local_input",
    )(conv_input, halo, grad_output, inject, readout, rates, later, conv_weight)
    arrived, act = lax.optimization_barrier((arrived, act))

    adh, adl, gdh, gdl, gi, gr = pl.pallas_call(
        local_shared_kernel,
        in_specs=[hbm] * 5 + [anywhere] * 3,
        out_specs=[hbm] * 6,
        out_shape=[wide16] * 4 + [narrow] * 2,
        scratch_shapes=[wide16_v] * 2 + [narrow16_v] * 2 + [local_v] + [row_v] * 3
        + [wide16_v] * 4 + [narrow_v] * 2 + [state_v]
        + [dma((5, spans)), dma((3,)), dma((6, spans))],
        compiler_params=params(),
        cost_estimate=cost(12 * tokens * channels * SPAN, 19 << 20),
        name="local_shared",
    )(grad_output, act, inject, readout, after, rates, prior, later)

    scanned = pl.pallas_call(
        scan_kernel,
        out_shape=shape(chunk, f32),
        compiler_params=params(8),
        cost_estimate=cost(1 << 18, 1 << 20),
        name="carry",
    )(arrived)
    returned = lax.all_to_all(scanned, SEQ, 0, 0, tiled=True)

    core = lax.axis_index("c").astype(jnp.int32).reshape(1)
    stacked = pltpu.VMEM((2 * states, channels), bf16)
    mine, theirs = pl.pallas_call(
        shared_kernel,
        in_specs=[smem, plain] + [hbm] * 6,
        out_specs=[plain] * 2,
        out_shape=[narrow] * 2,
        scratch_shapes=[wide16_v] * 4 + [narrow_v] * 2 + [stacked] * 2 + [dma((6, spans))],
        compiler_params=params(),
        cost_estimate=cost(12 * tokens * channels * states, 13 << 20),
        name="shared_terms",
    )(core, returned, adh, adl, gdh, gdl, gi, gr)

    swap = [(i, i ^ 1) for i in range(nc)]
    chip = mine + lax.ppermute(theirs, "c", swap)
    here = lax.axis_index("y")
    part = tokens // ny

    def turn(array, by):
        return lax.ppermute(array, "y", [(i, (i + by) % ny) for i in range(ny)])

    def cut(array, which):
        return lax.dynamic_slice_in_dim(array, lax.rem(here + which, ny) * part, part)

    sent = [turn(cut(chip, by).astype(bf16), by) for by in range(1, ny)]

    grad_input, first = pl.pallas_call(
        input_kernel,
        in_specs=[plain] + [hbm] * 3 + [plain],
        out_specs=[hbm, plain],
        out_shape=[wide, shape((8, channels), f32)],
        scratch_shapes=[
            wide_v, wide_v, narrow16_v, stacked, pltpu.VMEM((8, channels), f32), wide_v,
            dma((3, spans)), dma((spans,)),
        ],
        compiler_params=params(),
        cost_estimate=cost(4 * tokens * channels * states, 13 << 20),
        name="input_grads",
    )(returned, pre, factor, inject, conv_weight)

    *sent, first = lax.optimization_barrier((*sent, first))
    quarter = cut(chip, 0)
    for piece in sent:
        quarter = quarter + piece.astype(f32)
    quarter = quarter.astype(bf16)
    turned = [turn(quarter, by) for by in range(1, ny)]
    next_rows = lax.ppermute(first, SEQ, down)
    *turned, next_rows = lax.optimization_barrier((*turned, next_rows))
    done = jnp.zeros((tokens, states), bf16)
    for by, piece in enumerate([quarter] + turned):
        done = lax.dynamic_update_slice_in_dim(
            done, piece, lax.rem(here - by + ny, ny) * part, 0
        )
    other = lax.ppermute(done, "c", swap)
    mine_is_first = lax.axis_index("c") == 0
    grad_inject = jnp.where(mine_is_first, done, other).astype(f32)
    grad_readout = jnp.where(mine_is_first, other, done).astype(f32)

    weights = conv_weight.astype(f32)
    tail_rows = []
    for row in range(3):
        tail_rows.append(sum(weights[k] * next_rows[row - k] for k in range(row + 1)))
    patch = jnp.concatenate([jnp.zeros((5, channels), f32), jnp.stack(tail_rows)], axis=0)
    last = lax.slice_in_dim(grad_input, tokens - 8, tokens) + patch
    grad_input = lax.dynamic_update_slice(grad_input, last, (tokens - 8, 0))
    return grad_input, grad_inject, grad_readout


def build(devices, sizes):
    fine = Mesh(devices.reshape(sizes), ("z", "x", "y", "c"))
    nz, nx, ny, nc = sizes
    return jax.shard_map(
        functools.partial(body, nz * nx, ny, nc),
        mesh=fine,
        in_specs=(P(SEQ, HG), P(SEQ, HG), P(SEQ, None), P(SEQ, None), P(None, HG), P(HG, SEQ)),
        out_specs=(P(SEQ, HG), P(SEQ, None), P(SEQ, None)),
        check_vma=False,
    )


def solution(mesh):
    return build(mesh.devices, (8, 4, 4, 2))
```

```python
import functools

import jax
import jax.numpy as jnp
from jax import lax
from jax.experimental import pallas as pl
from jax.experimental.pallas import tpu as pltpu
from jax.sharding import Mesh
from jax.sharding import PartitionSpec as P

f32, bf16 = jnp.float32, jnp.bfloat16
SPAN = 256
SEQ, HG = ("z", "x"), ("y", "c")
LANES = 128
PREV = 16

NN = (((1,), (0,)), ((), ()))
NT = (((1,), (1,)), ((), ()))
TN = (((0,), (0,)), ((), ()))


def dot(a, b, dims):
    return lax.dot_general(a, b, dims, preferred_element_type=f32)


def split(v):
    high = v.astype(bf16)
    return high, (v - high.astype(f32)).astype(bf16)


def dot2(exact, v, dims):
    high, low = split(v)
    return dot(exact, high, dims) + dot(exact, low, dims)


def dot3(ah, al, bh, bl, dims):
    return dot(ah, bh, dims) + (dot(ah, bl, dims) + dot(al, bh, dims))


def places():
    return lax.broadcasted_iota(jnp.int32, (SPAN, 1), 0).astype(f32)


def span_at(span):
    return pl.ds(pl.multiple_of(span * SPAN, SPAN), SPAN)


def each_span(spans, step, backwards=False):
    def visit(i, _):
        step(spans - 1 - i if backwards else i)
        return 0

    lax.fori_loop(0, spans, visit, 0)


def by_span(source, target, sems):
    def piece(span):
        if len(source.shape) == 3:
            return pltpu.make_async_copy(source.at[span], target.at[span], sems.at[span])
        rows = span_at(span)
        return pltpu.make_async_copy(source.at[rows, :], target.at[rows, :], sems.at[span])

    return piece


def fetch(spans, whole, pieces, backwards=False):
    for copy in whole:
        copy.start()
    for i in range(spans):
        for piece in pieces:
            piece(spans - 1 - i if backwards else i).start()
    for copy in whole:
        copy.wait()


def drain(spans, pieces):
    for span in range(spans):
        for piece in pieces:
            piece(span).wait()


TOP = 32000.0
STEPS = 4096.0


def coded(v, axis):
    most = jnp.max(jnp.abs(v), axis=axis, keepdims=True)
    power = jnp.ceil(jnp.log2(jnp.maximum(most, 2.0**-120)))
    whole = jnp.round(v * jnp.exp2(-power) * TOP).astype(jnp.int32)
    return whole.astype(jnp.int16), power


def decoded(whole, power):
    return whole.astype(f32) * (jnp.exp2(power.astype(f32)) * (1.0 / TOP))


def log_codes(log):
    steps = log * -STEPS
    high = jnp.floor(steps)
    return high, jnp.round((steps - high) * TOP)


def log_of(high, low):
    return (high.astype(f32) + low.astype(f32) * (1.0 / TOP)) * (-1.0 / STEPS)


def side_tile(height, rows):
    blank = jnp.zeros((height - len(rows), rows[0].shape[1]), f32)
    return jnp.concatenate(rows + [blank], axis=0).astype(jnp.int32).astype(jnp.int16)


def grads_kernel(
    code_hbm, grad_hbm, read_hbm, rate_ref, prior_ref, later_ref, log_ref, carry,
    code_ref, grad_ref, read_ref, csem, gsem, rsem,
):
    heads, spans = code_ref.shape
    channels = carry.shape[1]
    pieces = [by_span(grad_hbm, grad_ref, gsem), by_span(read_hbm, read_ref, rsem)]
    fetch(spans, [pltpu.make_async_copy(code_hbm, code_ref, csem)], pieces, backwards=True)
    logs = jnp.log1p(-code_ref[...].astype(f32) * 1e-6)
    lane = lax.broadcasted_iota(jnp.int32, (heads, channels), 1)
    row = lax.broadcasted_iota(jnp.int32, (heads, channels), 0)
    width = channels // heads
    owns = jnp.where((lane >= row * width) & (lane < (row + 1) * width), 1.0, 0.0)
    rate_ref[...] = lax.dot_general(
        logs, owns, TN, precision=lax.Precision.HIGHEST, preferred_element_type=f32
    )
    total = jnp.zeros((1, channels), f32)
    for span in range(spans):
        prior_ref[span : span + 1, :] = total
        total = total + SPAN * rate_ref[span : span + 1, :]
    log_ref[...] = total
    total = jnp.zeros((1, channels), f32)
    for span in reversed(range(spans)):
        later_ref[span : span + 1, :] = total
        total = total + SPAN * rate_ref[span : span + 1, :]
    carry[...] = jnp.zeros_like(carry)

    def step(span):
        for piece in pieces:
            piece(span).wait()
        rate = rate_ref[pl.ds(span, 1), :]
        up = grad_ref[span_at(span), :].astype(f32) * jnp.exp(places() * rate)
        fresh = dot2(read_ref[span_at(span), :], up, TN)
        carry[...] = jnp.exp(SPAN * rate) * carry[...] + jnp.exp(rate) * fresh

    each_span(spans, step, backwards=True)


def convolved(x, before, weights):
    rows = jnp.concatenate([before, x], axis=0)
    preact = weights[0:1] * pltpu.roll(rows, 3, axis=0)[8:]
    for k in range(1, 3):
        preact = preact + weights[k : k + 1] * pltpu.roll(rows, 3 - k, axis=0)[8:]
    return preact + weights[3:4] * x


def states_kernel(
    x_hbm, halo_hbm, inject_hbm, rate_hbm, weight_hbm, own_grad_hbm, log_hbm,
    pay_ref,
    x_ref, halo_ref, inject_ref, rate_ref, weight_ref, own_grad_ref, log_ref, carry, prev,
    xsem, isem, sems,
):
    spans = rate_ref.shape[0]
    pieces = [by_span(x_hbm, x_ref, xsem), by_span(inject_hbm, inject_ref, isem)]
    late = pltpu.make_async_copy(own_grad_hbm, own_grad_ref, sems.at[4])
    fetch(
        spans,
        [
            pltpu.make_async_copy(halo_hbm, halo_ref, sems.at[0]),
            pltpu.make_async_copy(rate_hbm, rate_ref, sems.at[1]),
            pltpu.make_async_copy(weight_hbm, weight_ref, sems.at[2]),
            pltpu.make_async_copy(log_hbm, log_ref, sems.at[3]),
        ],
        pieces,
    )
    late.start()
    carry[...] = jnp.zeros_like(carry)
    prev[...] = halo_ref[...].astype(f32)[PREV - 8 :]
    weights = weight_ref[...].astype(f32)

    def step(span):
        for piece in pieces:
            piece(span).wait()
        x = x_ref[span_at(span), :].astype(f32)
        preact = convolved(x, prev[...], weights)
        prev[...] = x[SPAN - 8 :]
        act = (preact * jax.nn.sigmoid(preact)).astype(bf16)
        rate = rate_ref[pl.ds(span, 1), :]
        tail = jnp.exp((SPAN - 1.0 - places()) * rate)
        fresh = dot2(inject_ref[span_at(span), :], act.astype(f32) * tail, TN)
        carry[...] = jnp.exp(SPAN * rate) * carry[...] + fresh

    each_span(spans, step)
    late.wait()
    chunks, height, _ = pay_ref.shape
    state_codes, state_power = coded(carry[...], 0)
    grad_codes, grad_power = coded(own_grad_ref[...], 0)
    side = side_tile(height, [state_power, grad_power, *log_codes(log_ref[...])])
    for d in range(chunks):
        rows, lanes = chunk_place(d, height)
        pay_ref[d, :, 0:LANES] = state_codes[rows, lanes]
        pay_ref[d, :, LANES : 2 * LANES] = grad_codes[rows, lanes]
        pay_ref[d, :, 2 * LANES :] = side[:, lanes]


def chunk_place(d, height):
    r, l = height * (d // 4), LANES * (d % 4)
    return slice(r, r + height), slice(l, l + LANES)


def scan_kernel(own_ref, out_ref, made):
    chunks, height, _ = out_ref.shape
    gains, states, grads = [], [], []
    for e in range(chunks):
        side = own_ref[e, :, 2 * LANES :].astype(f32)
        gains.append(jnp.exp(log_of(side[2:3], side[3:4])))
        states.append(decoded(own_ref[e, :, 0:LANES], side[0:1]))
        grads.append(decoded(own_ref[e, :, LANES : 2 * LANES], side[1:2]))
    state = jnp.zeros((height, LANES), f32)
    grad = jnp.zeros((height, LANES), f32)
    for e in range(chunks):
        made[e, :, 0:LANES] = state
        state = gains[e] * state + states[e]
    for e in reversed(range(chunks)):
        made[e, :, LANES:] = grad
        grad = gains[e] * grad + grads[e]
    for e in range(chunks):
        codes, power = coded(made[e], 0)
        out_ref[e, :, 0 : 2 * LANES] = codes
        out_ref[e, :, 2 * LANES :] = side_tile(height, [power[:, :LANES], power[:, LANES:]])


def causal():
    row = lax.broadcasted_iota(jnp.int32, (SPAN, SPAN), 0)
    return row >= lax.broadcasted_iota(jnp.int32, (SPAN, SPAN), 1)


def local_input_kernel(
    x_hbm, halo_hbm, grad_hbm, inject_hbm, read_hbm, rate_hbm, later_hbm, weight_hbm,
    act_hbm, pre_hbm, factor_hbm, after_hbm,
    x_ref, halo_ref, grad_ref, inject_ref, read_ref, rate_ref, later_ref, weight_ref,
    act_ref, pre_ref, factor_ref, after_ref, carry,
    xsem, gsem, isem, rsem, sems, osems,
):
    spans = rate_ref.shape[0]
    pieces = [
        by_span(x_hbm, x_ref, xsem), by_span(grad_hbm, grad_ref, gsem),
        by_span(inject_hbm, inject_ref, isem), by_span(read_hbm, read_ref, rsem),
    ]
    outs = [
        by_span(act_ref, act_hbm, osems.at[0]), by_span(pre_ref, pre_hbm, osems.at[1]),
        by_span(factor_ref, factor_hbm, osems.at[2]), by_span(after_ref, after_hbm, osems.at[3]),
    ]
    fetch(
        spans,
        [
            pltpu.make_async_copy(halo_hbm, halo_ref, sems.at[0]),
            pltpu.make_async_copy(rate_hbm, rate_ref, sems.at[1]),
            pltpu.make_async_copy(weight_hbm, weight_ref, sems.at[2]),
            pltpu.make_async_copy(later_hbm, later_ref, sems.at[3]),
        ],
        pieces,
        backwards=True,
    )
    carry[...] = jnp.zeros_like(carry)
    weights = weight_ref[...].astype(f32)
    pieces[0](spans - 1).wait()

    def step(span):
        @pl.when(span > 0)
        def _():
            pieces[0](jnp.maximum(span - 1, 0)).wait()

        for piece in pieces[1:]:
            piece(span).wait()
        rows = span_at(span)
        x = x_ref[rows, :].astype(f32)
        start = pl.multiple_of(jnp.maximum(span * SPAN - PREV, 0), PREV)
        last = jnp.where(span == 0, halo_ref[...].astype(f32), x_ref[pl.ds(start, PREV), :].astype(f32))
        preact = convolved(x, last[PREV - 8 :], weights)
        squashed = jax.nn.sigmoid(preact)
        act_ref[rows, :] = (preact * squashed).astype(bf16)
        slope = squashed * (1.0 + preact * (1.0 - squashed))
        rate = rate_ref[pl.ds(span, 1), :]
        later = jnp.exp(later_ref[pl.ds(span, 1), :])
        inject, read = inject_ref[rows, :], read_ref[rows, :]
        here = places()
        steep = slope * jnp.exp(-here * rate)
        end = jnp.exp((SPAN - 1.0) * rate)
        up_high, up_low = split(grad_ref[rows, :].astype(f32) * jnp.exp(here * rate))
        mixing = jnp.where(causal(), dot(read, inject, NT), 0.0).astype(bf16)
        after = carry[...]
        after_ref[span] = after
        stacked = jnp.concatenate(split(after * end), axis=0)
        doubled = jnp.concatenate([inject, inject], axis=1)
        pre_ref[rows, :] = steep * (dot(mixing, up_high, TN) + dot(doubled, stacked, NN))
        factor_ref[rows, :] = steep * (end * later)
        fresh = dot(read, up_high, TN) + dot(read, up_low, TN)
        carry[...] = jnp.exp(SPAN * rate) * after + jnp.exp(rate) * fresh
        for out in outs:
            out(span).start()

    each_span(spans, step, backwards=True)
    drain(spans, outs)


def wide_product(high, low, both, states):
    wide = dot(high, both, NT)
    return wide[:, :states] + (wide[:, states:] + dot(low, both[0:states, :], NT))


def local_shared_kernel(
    grad_hbm, act_hbm, inject_hbm, read_hbm, after_hbm, rate_hbm,
    gi_hbm, gr_hbm,
    grad_ref, act_ref, inject_ref, read_ref, after_ref, rate_ref,
    gi_ref, gr_ref, carry,
    isems, sem, osems,
):
    spans = rate_ref.shape[0]
    sources = [grad_hbm, act_hbm, inject_hbm, read_hbm, after_hbm]
    targets = [grad_ref, act_ref, inject_ref, read_ref, after_ref]
    pieces = [by_span(a, b, isems.at[k]) for k, (a, b) in enumerate(zip(sources, targets))]
    outs = [by_span(gi_ref, gi_hbm, osems.at[0]), by_span(gr_ref, gr_hbm, osems.at[1])]
    fetch(spans, [pltpu.make_async_copy(rate_hbm, rate_ref, sem)], pieces)
    carry[...] = jnp.zeros_like(carry)

    def step(span):
        for piece in pieces:
            piece(span).wait()
        rows = span_at(span)
        rate = rate_ref[pl.ds(span, 1), :]
        inject, read = inject_ref[rows, :], read_ref[rows, :]
        states = inject.shape[1]
        here = places()
        up = grad_ref[rows, :].astype(f32) * jnp.exp(here * rate)
        down = act_ref[rows, :].astype(f32) * jnp.exp(-here * rate)
        uph, upl = split(up)
        downh, downl = split(down)
        pairs = jnp.where(causal(), dot(uph, downh, NT), 0.0).astype(bf16)
        end = jnp.exp((SPAN - 1.0) * rate)
        afters = jnp.concatenate(split(after_ref[span] * end), axis=0)
        before = carry[...]
        befores = jnp.concatenate(split(before * jnp.exp(rate)), axis=0)
        gi_ref[rows, :] = dot(pairs, read, TN) + wide_product(downh, downl, afters, states)
        gr_ref[rows, :] = dot(pairs, inject, NN) + wide_product(uph, upl, befores, states)
        fresh = dot(inject, downh, TN) + dot(inject, downl, TN)
        carry[...] = jnp.exp(SPAN * rate) * before + end * fresh
        for out in outs:
            out(span).start()

    each_span(spans, step)
    drain(spans, outs)


def unpacked(back_ref, both, which):
    chunks, height, _ = back_ref.shape
    states = both.shape[0] // 2
    for d in range(chunks):
        rows, lanes = chunk_place(d, height)
        power = back_ref[d, :, 2 * LANES :].astype(f32)[which : which + 1]
        v = decoded(back_ref[d, :, LANES * which : LANES * which + LANES], power)
        high, low = split(v)
        both[rows, lanes] = high
        both[states + rows.start : states + rows.stop, lanes] = low


def shared_kernel(
    grads_turn, core_ref, back_ref, grad_hbm, act_hbm, gr_hbm, gi_hbm, rate_hbm, prior_hbm, later_hbm,
    out_ref,
    in_ref, sum_ref, rate_ref, prior_ref, later_ref, both, isems, sems,
):
    tokens, states = sum_ref.shape
    spans = tokens // SPAN
    readouts = core_ref[0] == grads_turn
    small = [
        pltpu.make_async_copy(rate_hbm, rate_ref, sems.at[0]),
        pltpu.make_async_copy(prior_hbm, prior_ref, sems.at[1]),
        pltpu.make_async_copy(later_hbm, later_ref, sems.at[2]),
    ]
    for copy in small:
        copy.start()

    @pl.when(readouts)
    def _():
        pieces = [by_span(grad_hbm, in_ref, isems.at[0]), by_span(gr_hbm, sum_ref, isems.at[1])]
        fetch(spans, [], pieces)
        unpacked(back_ref, both, 0)

    @pl.when(jnp.logical_not(readouts))
    def _():
        pieces = [by_span(act_hbm, in_ref, isems.at[0]), by_span(gi_hbm, sum_ref, isems.at[1])]
        fetch(spans, [], pieces)
        unpacked(back_ref, both, 1)

    for copy in small:
        copy.wait()
    arriving = [by_span(grad_hbm, in_ref, isems.at[0]), by_span(gr_hbm, sum_ref, isems.at[1])]

    def step(span):
        for piece in arriving:
            piece(span).wait()
        rows = span_at(span)
        rate = rate_ref[pl.ds(span, 1), :]
        ahead = rate + prior_ref[pl.ds(span, 1), :]
        behind = (SPAN - 1.0) * rate + later_ref[pl.ds(span, 1), :]
        slope = jnp.where(readouts, rate, -rate)
        offset = jnp.where(readouts, ahead, behind)
        high, low = split(in_ref[rows, :].astype(f32) * jnp.exp(places() * slope + offset))
        out_ref[rows, :] = sum_ref[rows, :] + wide_product(high, low, both[...], states)

    each_span(spans, step)


def input_kernel(
    back_ref, pre_hbm, factor_hbm, inject_hbm, weight_ref,
    out_hbm, first_ref,
    pre_ref, factor_ref, inject_ref, grads, after, made, isems, osems,
):
    spans = pre_ref.shape[0] // SPAN
    pieces = [
        by_span(pre_hbm, pre_ref, isems.at[0]), by_span(factor_hbm, factor_ref, isems.at[1]),
        by_span(inject_hbm, inject_ref, isems.at[2]),
    ]
    out = by_span(made, out_hbm, osems)
    fetch(spans, [], pieces, backwards=True)
    unpacked(back_ref, grads, 1)
    after[...] = jnp.zeros_like(after)
    weights = weight_ref[...].astype(f32)

    def step(span):
        for piece in pieces:
            piece(span).wait()
        rows = span_at(span)
        inject = inject_ref[rows, :]
        carried = dot(jnp.concatenate([inject, inject], axis=1), grads[...], NN)
        now = pre_ref[rows, :] + factor_ref[rows, :] * carried
        joined = jnp.concatenate([now, after[...]], axis=0)
        summed = weights[3:4] * now
        for k in range(3):
            ahead = pltpu.roll(joined, SPAN + 8 - (3 - k), axis=0)[:SPAN]
            summed = summed + weights[k : k + 1] * ahead
        after[...] = now[0:8]
        made[rows, :] = summed
        out(span).start()

    each_span(spans, step, backwards=True)
    first_ref[...] = after[...]
    drain(spans, [out])


def params(mib=54):
    return pltpu.CompilerParams(vmem_limit_bytes=mib << 20)


def cost(flops, nbytes):
    return pl.CostEstimate(flops=flops, bytes_accessed=nbytes, transcendentals=0)


def body(nseq, ny, nc, conv_input, grad_output, inject, readout, conv_weight, decay_codes):
    tokens, channels = conv_input.shape
    spans = decay_codes.shape[1]
    states = inject.shape[1]
    shape = jax.ShapeDtypeStruct
    height = 4 * states // nseq
    chunk = (nseq, height, 3 * LANES)
    smem = pl.BlockSpec(memory_space=pltpu.SMEM)
    wide, wide16 = shape((tokens, channels), f32), shape((tokens, channels), bf16)
    narrow, row = shape((tokens, states), f32), shape((spans, channels), f32)
    local = shape((spans, states, channels), f32)
    state = shape((states, channels), f32)

    up = [(i, i + 1) for i in range(nseq - 1)]
    down = [(i + 1, i) for i in range(nseq - 1)]
    halo = lax.ppermute(conv_input[tokens - PREV :], SEQ, up)

    anywhere = pl.BlockSpec(memory_space=pl.ANY)
    hbm = pl.BlockSpec(memory_space=pltpu.HBM)
    plain = pl.BlockSpec()
    wide_v, wide16_v = pltpu.VMEM(wide.shape, f32), pltpu.VMEM(wide.shape, bf16)
    narrow_v, narrow16_v = pltpu.VMEM(narrow.shape, f32), pltpu.VMEM(narrow.shape, bf16)
    row_v, state_v = pltpu.VMEM(row.shape, f32), pltpu.VMEM(state.shape, f32)
    local_v = pltpu.VMEM(local.shape, f32)
    halo_v, weight_v = pltpu.VMEM((PREV, channels), bf16), pltpu.VMEM(conv_weight.shape, bf16)
    dma = pltpu.SemaphoreType.DMA

    rates, prior, later, own_log, own_grad = pl.pallas_call(
        grads_kernel,
        in_specs=[hbm] * 3,
        out_specs=[plain] * 5,
        out_shape=[row, row, row, shape((1, channels), f32), state],
        scratch_shapes=[
            pltpu.VMEM(decay_codes.shape, jnp.int32), wide16_v, narrow16_v,
            dma, dma((spans,)), dma((spans,)),
        ],
        compiler_params=params(),
        cost_estimate=cost(4 * tokens * channels * states, 3 << 20),
        name="own_grads",
    )(decay_codes, grad_output, readout)

    payload = pl.pallas_call(
        states_kernel,
        in_specs=[hbm, anywhere, hbm, anywhere, hbm, anywhere, anywhere],
        out_specs=plain,
        out_shape=shape(chunk, jnp.int16),
        scratch_shapes=[
            wide16_v, halo_v, narrow16_v, row_v, weight_v, state_v, pltpu.VMEM((1, channels), f32),
            state_v, pltpu.VMEM((8, channels), f32), dma((spans,)), dma((spans,)), dma((5,)),
        ],
        compiler_params=params(),
        cost_estimate=cost(4 * tokens * channels * states, 4 << 20),
        name="own_states",
    )(conv_input, halo, inject, rates, conv_weight, own_grad, own_log)

    arrived = lax.all_to_all(payload, SEQ, 0, 0, tiled=True)

    act, pre, factor, after = pl.pallas_call(
        local_input_kernel,
        in_specs=[hbm, anywhere, hbm, hbm, hbm, anywhere, anywhere, hbm],
        out_specs=[hbm] * 4,
        out_shape=[wide16, wide, wide, local],
        scratch_shapes=[
            wide16_v, halo_v, wide16_v, narrow16_v, narrow16_v, row_v, row_v, weight_v,
            wide16_v, wide_v, wide_v, local_v, state_v,
        ]
        + [dma((spans,))] * 4 + [dma((4,)), dma((4, spans))],
        compiler_params=params(),
        cost_estimate=cost(8 * tokens * channels * SPAN, 18 << 20),
        name="local_input",
    )(conv_input, halo, grad_output, inject, readout, rates, later, conv_weight)
    arrived, act = lax.optimization_barrier((arrived, act))

    gi, gr = pl.pallas_call(
        local_shared_kernel,
        in_specs=[hbm] * 5 + [anywhere],
        out_specs=[hbm] * 2,
        out_shape=[narrow] * 2,
        scratch_shapes=[wide16_v] * 2 + [narrow16_v] * 2 + [local_v, row_v]
        + [narrow_v] * 2 + [state_v] + [dma((5, spans)), dma, dma((2, spans))],
        compiler_params=params(),
        cost_estimate=cost(12 * tokens * channels * SPAN, 9 << 20),
        name="local_shared",
    )(grad_output, act, inject, readout, after, rates)

    scanned = pl.pallas_call(
        scan_kernel,
        out_shape=shape(chunk, jnp.int16),
        scratch_shapes=[pltpu.VMEM((nseq, height, 2 * LANES), f32)],
        compiler_params=params(8),
        cost_estimate=cost(1 << 18, 1 << 20),
        name="carry",
    )(arrived)
    returned = lax.all_to_all(scanned, SEQ, 0, 0, tiled=True)

    core = lax.axis_index("c").astype(jnp.int32).reshape(1)
    stacked = pltpu.VMEM((2 * states, channels), bf16)

    def shared(turn):
        return pl.pallas_call(
            functools.partial(shared_kernel, turn),
            in_specs=[smem, plain] + [hbm] * 4 + [anywhere] * 3,
            out_specs=plain,
            out_shape=narrow,
            scratch_shapes=[wide16_v, narrow_v] + [row_v] * 3 + [stacked, dma((2, spans)), dma((3,))],
            compiler_params=params(53),
            cost_estimate=cost(6 * tokens * channels * states, 4 << 20),
            name=f"shared_terms_{turn}",
        )(core, returned, grad_output, act, gr, gi, rates, prior, later)

    swap = [(i, i ^ 1) for i in range(nc)]
    swapped = lax.ppermute(shared(0), "c", swap)
    chip = shared(1) + swapped
    here = lax.axis_index("y")
    part = tokens // ny

    def turn(array, by):
        return lax.ppermute(array, "y", [(i, (i + by) % ny) for i in range(ny)])

    def cut(array, which):
        return lax.dynamic_slice_in_dim(array, lax.rem(here + which, ny) * part, part)

    sent = [turn(cut(chip, by).astype(bf16), by) for by in range(1, ny)]

    grad_input, first = pl.pallas_call(
        input_kernel,
        in_specs=[plain] + [hbm] * 3 + [plain],
        out_specs=[hbm, plain],
        out_shape=[wide, shape((8, channels), f32)],
        scratch_shapes=[
            wide_v, wide_v, narrow16_v, stacked, pltpu.VMEM((8, channels), f32), wide_v,
            dma((3, spans)), dma((spans,)),
        ],
        compiler_params=params(53),
        cost_estimate=cost(4 * tokens * channels * states, 13 << 20),
        name="input_grads",
    )(returned, pre, factor, inject, conv_weight)

    *sent, first = lax.optimization_barrier((*sent, first))
    quarter = cut(chip, 0)
    for piece in sent:
        quarter = quarter + piece.astype(f32)
    quarter = quarter.astype(bf16)
    turned = [turn(quarter, by) for by in range(1, ny)]
    next_rows = lax.ppermute(first, SEQ, down)
    *turned, next_rows = lax.optimization_barrier((*turned, next_rows))
    done = jnp.zeros((tokens, states), bf16)
    for by, piece in enumerate([quarter] + turned):
        done = lax.dynamic_update_slice_in_dim(
            done, piece, lax.rem(here - by + ny, ny) * part, 0
        )
    other = lax.ppermute(done, "c", swap)
    mine_is_first = lax.axis_index("c") == 0
    grad_inject = jnp.where(mine_is_first, done, other).astype(f32)
    grad_readout = jnp.where(mine_is_first, other, done).astype(f32)

    weights = conv_weight.astype(f32)
    tail_rows = []
    for row in range(3):
        tail_rows.append(sum(weights[k] * next_rows[row - k] for k in range(row + 1)))
    patch = jnp.concatenate([jnp.zeros((5, channels), f32), jnp.stack(tail_rows)], axis=0)
    last = lax.slice_in_dim(grad_input, tokens - 8, tokens) + patch
    grad_input = lax.dynamic_update_slice(grad_input, last, (tokens - 8, 0))
    return grad_input, grad_inject, grad_readout


def build(devices, sizes):
    fine = Mesh(devices.reshape(sizes), ("z", "x", "y", "c"))
    nz, nx, ny, nc = sizes
    return jax.shard_map(
        functools.partial(body, nz * nx, ny, nc),
        mesh=fine,
        in_specs=(P(SEQ, HG), P(SEQ, HG), P(SEQ, None), P(SEQ, None), P(None, HG), P(HG, SEQ)),
        out_specs=(P(SEQ, HG), P(SEQ, None), P(SEQ, None)),
        check_vma=False,
    )


def solution(mesh):
    return build(mesh.devices, (8, 4, 4, 2))
```

```python
import functools

import jax
import jax.numpy as jnp
from jax import lax
from jax.experimental import pallas as pl
from jax.experimental.pallas import tpu as pltpu
from jax.sharding import Mesh
from jax.sharding import PartitionSpec as P

f32, bf16 = jnp.float32, jnp.bfloat16
SPAN = 256
SEQ, HG = ("z", "x"), ("y", "c")
LANES = 128
PREV = 16

NN = (((1,), (0,)), ((), ()))
NT = (((1,), (1,)), ((), ()))
TN = (((0,), (0,)), ((), ()))


def dot(a, b, dims):
    return lax.dot_general(a, b, dims, preferred_element_type=f32)


def split(v):
    high = v.astype(bf16)
    return high, (v - high.astype(f32)).astype(bf16)


def dot2(exact, v, dims):
    high, low = split(v)
    return dot(exact, high, dims) + dot(exact, low, dims)


def dot3(ah, al, bh, bl, dims):
    return dot(ah, bh, dims) + (dot(ah, bl, dims) + dot(al, bh, dims))


def places():
    return lax.broadcasted_iota(jnp.int32, (SPAN, 1), 0).astype(f32)


def span_at(span):
    return pl.ds(pl.multiple_of(span * SPAN, SPAN), SPAN)


AHEAD = 3


def each_span(spans, step, start, pieces, backwards=False, ahead=AHEAD):
    def visit(i, _):
        span = spans - 1 - i if backwards else i
        for piece in pieces:
            piece(span).wait()

        @pl.when(i + ahead < spans)
        def _():
            start(span - ahead if backwards else span + ahead)

        step(span)
        return 0

    lax.fori_loop(0, spans, visit, 0)


def starting(pieces):
    def start(span):
        for piece in pieces:
            piece(span).start()

    return start


def by_span(source, target, sems):
    def piece(span):
        if len(source.shape) == 3:
            return pltpu.make_async_copy(source.at[span], target.at[span], sems.at[span])
        rows = span_at(span)
        return pltpu.make_async_copy(source.at[rows, :], target.at[rows, :], sems.at[span])

    return piece


def fetch(spans, whole, start, backwards=False, ahead=AHEAD):
    for copy in whole:
        copy.start()
    for i in range(min(ahead, spans)):
        start(spans - 1 - i if backwards else i)
    for copy in whole:
        copy.wait()


def drain(spans, pieces):
    for span in range(spans):
        for piece in pieces:
            piece(span).wait()


TOP = 32000.0
STEPS = 4096.0


def coded(v, axis):
    most = jnp.max(jnp.abs(v), axis=axis, keepdims=True)
    power = jnp.ceil(jnp.log2(jnp.maximum(most, 2.0**-120)))
    whole = jnp.round(v * jnp.exp2(-power) * TOP).astype(jnp.int32)
    return whole.astype(jnp.int16), power


def decoded(whole, power):
    return whole.astype(f32) * (jnp.exp2(power.astype(f32)) * (1.0 / TOP))


def log_codes(log):
    steps = log * -STEPS
    high = jnp.floor(steps)
    return high, jnp.round((steps - high) * TOP)


def log_of(high, low):
    return (high.astype(f32) + low.astype(f32) * (1.0 / TOP)) * (-1.0 / STEPS)


def side_tile(height, rows):
    blank = jnp.zeros((height - len(rows), rows[0].shape[1]), f32)
    return jnp.concatenate(rows + [blank], axis=0).astype(jnp.int32).astype(jnp.int16)


def grads_kernel(
    code_hbm, grad_hbm, read_hbm, rate_ref, prior_ref, later_ref, log_ref, carry, after_hbm,
    code_ref, grad_ref, read_ref, after_ref, csem, gsem, rsem, asem,
):
    heads, spans = code_ref.shape
    sending = by_span(after_ref, after_hbm, asem)
    channels = carry.shape[1]
    pieces = [by_span(grad_hbm, grad_ref, gsem), by_span(read_hbm, read_ref, rsem)]
    start = starting(pieces)
    fetch(spans, [pltpu.make_async_copy(code_hbm, code_ref, csem)], start, backwards=True)
    logs = jnp.log1p(-code_ref[...].astype(f32) * 1e-6)
    lane = lax.broadcasted_iota(jnp.int32, (heads, channels), 1)
    row = lax.broadcasted_iota(jnp.int32, (heads, channels), 0)
    width = channels // heads
    owns = jnp.where((lane >= row * width) & (lane < (row + 1) * width), 1.0, 0.0)
    rate_ref[...] = lax.dot_general(
        logs, owns, TN, precision=lax.Precision.HIGHEST, preferred_element_type=f32
    )
    total = jnp.zeros((1, channels), f32)
    for span in range(spans):
        prior_ref[span : span + 1, :] = total
        total = total + SPAN * rate_ref[span : span + 1, :]
    log_ref[...] = total
    total = jnp.zeros((1, channels), f32)
    for span in reversed(range(spans)):
        later_ref[span : span + 1, :] = total
        total = total + SPAN * rate_ref[span : span + 1, :]
    carry[...] = jnp.zeros_like(carry)

    def step(span):
        rate = rate_ref[pl.ds(span, 1), :]
        after = carry[...]
        after_ref[span] = after
        sending(span).start()
        up = grad_ref[span_at(span), :].astype(f32) * jnp.exp(places() * rate)
        fresh = dot2(read_ref[span_at(span), :], up, TN)
        carry[...] = jnp.exp(SPAN * rate) * after + jnp.exp(rate) * fresh

    each_span(spans, step, start, pieces, backwards=True)
    drain(spans, [sending])


def convolved(x, before, weights):
    rows = jnp.concatenate([before, x], axis=0)
    one = pltpu.roll(rows, 1, axis=0)
    older = weights[1:2] * rows + weights[0:1] * one
    return (weights[3:4] * x + weights[2:3] * one[8:]) + pltpu.roll(older, 2, axis=0)[8:]


def states_kernel(
    x_hbm, halo_hbm, inject_hbm, rate_hbm, weight_hbm, own_grad_hbm, log_hbm,
    pay_ref, act_hbm, slope_hbm, before_hbm,
    x_ref, halo_ref, inject_ref, rate_ref, weight_ref, own_grad_ref, log_ref, carry, prev,
    act_ref, slope_ref, before_ref, xsem, isem, sems, osems,
):
    spans = rate_ref.shape[0]
    pieces = [by_span(x_hbm, x_ref, xsem), by_span(inject_hbm, inject_ref, isem)]
    outs = [
        by_span(act_ref, act_hbm, osems.at[0]), by_span(slope_ref, slope_hbm, osems.at[1]),
        by_span(before_ref, before_hbm, osems.at[2]),
    ]
    start = starting(pieces)
    late = pltpu.make_async_copy(own_grad_hbm, own_grad_ref, sems.at[4])
    fetch(
        spans,
        [
            pltpu.make_async_copy(halo_hbm, halo_ref, sems.at[0]),
            pltpu.make_async_copy(rate_hbm, rate_ref, sems.at[1]),
            pltpu.make_async_copy(weight_hbm, weight_ref, sems.at[2]),
            pltpu.make_async_copy(log_hbm, log_ref, sems.at[3]),
        ],
        start,
    )
    late.start()
    carry[...] = jnp.zeros_like(carry)
    prev[...] = halo_ref[...].astype(f32)[PREV - 8 :]
    weights = weight_ref[...].astype(f32)

    def step(span):
        x = x_ref[span_at(span), :].astype(f32)
        preact = convolved(x, prev[...], weights)
        prev[...] = x[SPAN - 8 :]
        squashed = jax.nn.sigmoid(preact)
        act = (preact * squashed).astype(bf16)
        act_ref[span_at(span), :] = act
        slope_ref[span_at(span), :] = squashed * (1.0 + preact * (1.0 - squashed))
        rate = rate_ref[pl.ds(span, 1), :]
        tail = jnp.exp((SPAN - 1.0 - places()) * rate)
        before = carry[...]
        before_ref[span] = before
        for out in outs:
            out(span).start()
        fresh = dot2(inject_ref[span_at(span), :], act.astype(f32) * tail, TN)
        carry[...] = jnp.exp(SPAN * rate) * before + fresh

    each_span(spans, step, start, pieces)
    late.wait()
    chunks, height, _ = pay_ref.shape
    state_codes, state_power = coded(carry[...], 0)
    grad_codes, grad_power = coded(own_grad_ref[...], 0)
    side = side_tile(height, [state_power, grad_power, *log_codes(log_ref[...])])
    for d in range(chunks):
        rows, lanes = chunk_place(d, height)
        pay_ref[d, :, 0:LANES] = state_codes[rows, lanes]
        pay_ref[d, :, LANES : 2 * LANES] = grad_codes[rows, lanes]
        pay_ref[d, :, 2 * LANES :] = side[:, lanes]
    drain(spans, outs)


def chunk_place(d, height):
    r, l = height * (d // 4), LANES * (d % 4)
    return slice(r, r + height), slice(l, l + LANES)


def scan_kernel(own_ref, out_ref, made):
    chunks, height, _ = out_ref.shape
    gains, states, grads = [], [], []
    for e in range(chunks):
        side = own_ref[e, :, 2 * LANES :].astype(f32)
        gains.append(jnp.exp(log_of(side[2:3], side[3:4])))
        states.append(decoded(own_ref[e, :, 0:LANES], side[0:1]))
        grads.append(decoded(own_ref[e, :, LANES : 2 * LANES], side[1:2]))
    state = jnp.zeros((height, LANES), f32)
    grad = jnp.zeros((height, LANES), f32)
    for e in range(chunks):
        made[e, :, 0:LANES] = state
        state = gains[e] * state + states[e]
    for e in reversed(range(chunks)):
        made[e, :, LANES:] = grad
        grad = gains[e] * grad + grads[e]
    for e in range(chunks):
        codes, power = coded(made[e], 0)
        out_ref[e, :, 0 : 2 * LANES] = codes
        out_ref[e, :, 2 * LANES :] = side_tile(height, [power[:, :LANES], power[:, LANES:]])


def causal():
    row = lax.broadcasted_iota(jnp.int32, (SPAN, SPAN), 0)
    return row >= lax.broadcasted_iota(jnp.int32, (SPAN, SPAN), 1)


def local_input_kernel(
    slope_hbm, grad_hbm, inject_hbm, read_hbm, after_hbm, rate_hbm, later_hbm,
    pre_hbm, factor_hbm,
    slope_ref, grad_ref, inject_ref, read_ref, after_ref, rate_ref, later_ref,
    pre_ref, factor_ref, isems, sems, osems,
):
    spans = rate_ref.shape[0]
    sources = [slope_hbm, grad_hbm, inject_hbm, read_hbm, after_hbm]
    targets = [slope_ref, grad_ref, inject_ref, read_ref, after_ref]
    pieces = [by_span(a, b, isems.at[k]) for k, (a, b) in enumerate(zip(sources, targets))]
    start = starting(pieces)
    outs = [by_span(pre_ref, pre_hbm, osems.at[0]), by_span(factor_ref, factor_hbm, osems.at[1])]
    fetch(
        spans,
        [
            pltpu.make_async_copy(rate_hbm, rate_ref, sems.at[0]),
            pltpu.make_async_copy(later_hbm, later_ref, sems.at[1]),
        ],
        start,
    )

    def step(span):
        rows = span_at(span)
        rate = rate_ref[pl.ds(span, 1), :]
        later = jnp.exp(later_ref[pl.ds(span, 1), :])
        inject, read = inject_ref[rows, :], read_ref[rows, :]
        here = places()
        steep = slope_ref[rows, :] * jnp.exp(-here * rate)
        end = jnp.exp((SPAN - 1.0) * rate)
        up = (grad_ref[rows, :].astype(f32) * jnp.exp(here * rate)).astype(bf16)
        mixing = jnp.where(causal(), dot(read, inject, NT), 0.0).astype(bf16)
        stacked = jnp.concatenate(split(after_ref[span] * end), axis=0)
        doubled = jnp.concatenate([inject, inject], axis=1)
        pre = steep * (dot(mixing, up, TN) + dot(doubled, stacked, NN))
        pre_ref[rows, :] = pre.astype(bf16)
        factor_ref[rows, :] = (steep * (end * later)).astype(bf16)
        for out in outs:
            out(span).start()

    each_span(spans, step, start, pieces)
    drain(spans, outs)


def wide_product(high, low, both, states):
    wide = dot(high, both, NT)
    return wide[:, :states] + (wide[:, states:] + dot(low, both[0:states, :], NT))


def local_shared_kernel(
    grad_hbm, act_hbm, inject_hbm, read_hbm, after_hbm, before_hbm, rate_hbm,
    gi_hbm, gr_hbm,
    grad_ref, act_ref, inject_ref, read_ref, after_ref, before_ref, rate_ref,
    gi_ref, gr_ref,
    isems, sem, osems,
):
    spans = rate_ref.shape[0]
    sources = [grad_hbm, act_hbm, inject_hbm, read_hbm, after_hbm, before_hbm]
    targets = [grad_ref, act_ref, inject_ref, read_ref, after_ref, before_ref]
    pieces = [by_span(a, b, isems.at[k]) for k, (a, b) in enumerate(zip(sources, targets))]
    start = starting(pieces)
    outs = [by_span(gi_ref, gi_hbm, osems.at[0]), by_span(gr_ref, gr_hbm, osems.at[1])]
    fetch(spans, [pltpu.make_async_copy(rate_hbm, rate_ref, sem)], start)

    def step(span):
        rows = span_at(span)
        rate = rate_ref[pl.ds(span, 1), :]
        inject, read = inject_ref[rows, :], read_ref[rows, :]
        states = inject.shape[1]
        here = places()
        up = grad_ref[rows, :].astype(f32) * jnp.exp(here * rate)
        down = act_ref[rows, :].astype(f32) * jnp.exp(-here * rate)
        uph, upl = split(up)
        downh, downl = split(down)
        pairs = jnp.where(causal(), dot(uph, downh, NT), 0.0).astype(bf16)
        end = jnp.exp((SPAN - 1.0) * rate)
        afters = jnp.concatenate(split(after_ref[span] * end), axis=0)
        befores = jnp.concatenate(split(before_ref[span] * jnp.exp(rate)), axis=0)
        gi_ref[rows, :] = dot(pairs, read, TN) + wide_product(downh, downl, afters, states)
        gr_ref[rows, :] = dot(pairs, inject, NN) + wide_product(uph, upl, befores, states)
        for out in outs:
            out(span).start()

    each_span(spans, step, start, pieces)
    drain(spans, outs)


def unpacked(back_ref, both, which):
    chunks, height, _ = back_ref.shape
    states = both.shape[0] // 2
    for d in range(chunks):
        rows, lanes = chunk_place(d, height)
        power = back_ref[d, :, 2 * LANES :].astype(f32)[which : which + 1]
        v = decoded(back_ref[d, :, LANES * which : LANES * which + LANES], power)
        high, low = split(v)
        both[rows, lanes] = high
        both[states + rows.start : states + rows.stop, lanes] = low


def shared_kernel(
    grads_turn, core_ref, back_ref, grad_hbm, act_hbm, gr_hbm, gi_hbm, rate_hbm, prior_hbm, later_hbm,
    out_hbm,
    in_ref, sum_ref, rate_ref, prior_ref, later_ref, both, out_ref, isems, sems, osems,
):
    tokens, states = sum_ref.shape
    spans = tokens // SPAN
    readouts = core_ref[0] == grads_turn
    small = [
        pltpu.make_async_copy(rate_hbm, rate_ref, sems.at[0]),
        pltpu.make_async_copy(prior_hbm, prior_ref, sems.at[1]),
        pltpu.make_async_copy(later_hbm, later_ref, sems.at[2]),
    ]
    for copy in small:
        copy.start()

    pieces = [by_span(grad_hbm, in_ref, isems.at[0]), by_span(gr_hbm, sum_ref, isems.at[1])]
    others = [by_span(act_hbm, in_ref, isems.at[0]), by_span(gi_hbm, sum_ref, isems.at[1])]

    def start(span):
        @pl.when(readouts)
        def _():
            starting(pieces)(span)

        @pl.when(jnp.logical_not(readouts))
        def _():
            starting(others)(span)

    fetch(spans, [], start, ahead=spans)

    @pl.when(readouts)
    def _():
        unpacked(back_ref, both, 0)

    @pl.when(jnp.logical_not(readouts))
    def _():
        unpacked(back_ref, both, 1)

    for copy in small:
        copy.wait()
    sending = by_span(out_ref, out_hbm, osems)

    def step(span):
        rows = span_at(span)
        rate = rate_ref[pl.ds(span, 1), :]
        ahead = rate + prior_ref[pl.ds(span, 1), :]
        behind = (SPAN - 1.0) * rate + later_ref[pl.ds(span, 1), :]
        slope = jnp.where(readouts, rate, -rate)
        offset = jnp.where(readouts, ahead, behind)
        high, low = split(in_ref[rows, :].astype(f32) * jnp.exp(places() * slope + offset))
        out_ref[rows, :] = sum_ref[rows, :] + wide_product(high, low, both[...], states)
        sending(span).start()

    each_span(spans, step, start, pieces, ahead=spans)
    drain(spans, [sending])


def input_kernel(
    back_ref, pre_hbm, factor_hbm, inject_hbm, weight_ref,
    out_hbm, first_ref,
    pre_ref, factor_ref, inject_ref, grads, after, made, isems, osems,
):
    spans = pre_ref.shape[0] // SPAN
    pieces = [
        by_span(pre_hbm, pre_ref, isems.at[0]), by_span(factor_hbm, factor_ref, isems.at[1]),
        by_span(inject_hbm, inject_ref, isems.at[2]),
    ]
    out = by_span(made, out_hbm, osems)
    start = starting(pieces)
    fetch(spans, [], start, backwards=True, ahead=spans)
    unpacked(back_ref, grads, 1)
    after[...] = jnp.zeros_like(after)
    weights = weight_ref[...].astype(f32)

    def step(span):
        rows = span_at(span)
        inject = inject_ref[rows, :]
        carried = dot(jnp.concatenate([inject, inject], axis=1), grads[...], NN)
        now = pre_ref[rows, :].astype(f32) + factor_ref[rows, :].astype(f32) * carried
        joined = jnp.concatenate([now, after[...]], axis=0)
        summed = weights[3:4] * now
        for k in range(3):
            ahead = pltpu.roll(joined, SPAN + 8 - (3 - k), axis=0)[:SPAN]
            summed = summed + weights[k : k + 1] * ahead
        after[...] = now[0:8]
        made[rows, :] = summed
        out(span).start()

    each_span(spans, step, start, pieces, backwards=True, ahead=spans)
    first_ref[...] = after[...]
    drain(spans, [out])


def params(mib=54):
    return pltpu.CompilerParams(vmem_limit_bytes=mib << 20)


def cost(flops, nbytes):
    return pl.CostEstimate(flops=flops, bytes_accessed=nbytes, transcendentals=0)


def body(nseq, ny, nc, conv_input, grad_output, inject, readout, conv_weight, decay_codes):
    tokens, channels = conv_input.shape
    spans = decay_codes.shape[1]
    states = inject.shape[1]
    shape = jax.ShapeDtypeStruct
    height = 4 * states // nseq
    chunk = (nseq, height, 3 * LANES)
    smem = pl.BlockSpec(memory_space=pltpu.SMEM)
    wide, wide16 = shape((tokens, channels), f32), shape((tokens, channels), bf16)
    narrow, row = shape((tokens, states), f32), shape((spans, channels), f32)
    local = shape((spans, states, channels), f32)
    state = shape((states, channels), f32)

    up = [(i, i + 1) for i in range(nseq - 1)]
    down = [(i + 1, i) for i in range(nseq - 1)]
    halo = lax.ppermute(conv_input[tokens - PREV :], SEQ, up)

    anywhere = pl.BlockSpec(memory_space=pl.ANY)
    hbm = pl.BlockSpec(memory_space=pltpu.HBM)
    plain = pl.BlockSpec()
    wide_v, wide16_v = pltpu.VMEM(wide.shape, f32), pltpu.VMEM(wide.shape, bf16)
    narrow_v, narrow16_v = pltpu.VMEM(narrow.shape, f32), pltpu.VMEM(narrow.shape, bf16)
    row_v, state_v = pltpu.VMEM(row.shape, f32), pltpu.VMEM(state.shape, f32)
    local_v = pltpu.VMEM(local.shape, f32)
    halo_v, weight_v = pltpu.VMEM((PREV, channels), bf16), pltpu.VMEM(conv_weight.shape, bf16)
    dma = pltpu.SemaphoreType.DMA

    rates, prior, later, own_log, own_grad, after = pl.pallas_call(
        grads_kernel,
        in_specs=[hbm] * 3,
        out_specs=[plain] * 5 + [hbm],
        out_shape=[row, row, row, shape((1, channels), f32), state, local],
        scratch_shapes=[
            pltpu.VMEM(decay_codes.shape, jnp.int32), wide16_v, narrow16_v, local_v,
            dma, dma((spans,)), dma((spans,)), dma((spans,)),
        ],
        compiler_params=params(),
        cost_estimate=cost(4 * tokens * channels * states, 3 << 20),
        name="own_grads",
    )(decay_codes, grad_output, readout)

    payload, act, slope, before = pl.pallas_call(
        states_kernel,
        in_specs=[hbm, anywhere, hbm, anywhere, hbm, anywhere, anywhere],
        out_specs=[plain] + [hbm] * 3,
        out_shape=[shape(chunk, jnp.int16), wide16, wide, local],
        scratch_shapes=[
            wide16_v, halo_v, narrow16_v, row_v, weight_v, state_v, pltpu.VMEM((1, channels), f32),
            state_v, pltpu.VMEM((8, channels), f32), wide16_v, wide_v, local_v,
            dma((spans,)), dma((spans,)), dma((5,)), dma((3, spans)),
        ],
        compiler_params=params(),
        cost_estimate=cost(4 * tokens * channels * states, 4 << 20),
        name="own_states",
    )(conv_input, halo, inject, rates, conv_weight, own_grad, own_log)

    arrived = lax.all_to_all(payload, SEQ, 0, 0, tiled=True)

    pre, factor = pl.pallas_call(
        local_input_kernel,
        in_specs=[hbm] * 5 + [anywhere] * 2,
        out_specs=[hbm] * 2,
        out_shape=[wide16] * 2,
        scratch_shapes=[wide_v, wide16_v, narrow16_v, narrow16_v, local_v, row_v, row_v]
        + [wide16_v] * 2 + [dma((5, spans)), dma((2,)), dma((2, spans))],
        compiler_params=params(),
        cost_estimate=cost(8 * tokens * channels * SPAN, 13 << 20),
        name="local_input",
    )(slope, grad_output, inject, readout, after, rates, later)
    arrived, pre = lax.optimization_barrier((arrived, pre))

    gi, gr = pl.pallas_call(
        local_shared_kernel,
        in_specs=[hbm] * 6 + [anywhere],
        out_specs=[hbm] * 2,
        out_shape=[narrow] * 2,
        scratch_shapes=[wide16_v] * 2 + [narrow16_v] * 2 + [local_v, local_v, row_v]
        + [narrow_v] * 2 + [dma((6, spans)), dma, dma((2, spans))],
        compiler_params=params(),
        cost_estimate=cost(12 * tokens * channels * SPAN, 9 << 20),
        name="local_shared",
    )(grad_output, act, inject, readout, after, before, rates)

    scanned = pl.pallas_call(
        scan_kernel,
        out_shape=shape(chunk, jnp.int16),
        scratch_shapes=[pltpu.VMEM((nseq, height, 2 * LANES), f32)],
        compiler_params=params(8),
        cost_estimate=cost(1 << 18, 1 << 20),
        name="carry",
    )(arrived)
    returned = lax.all_to_all(scanned, SEQ, 0, 0, tiled=True)

    core = lax.axis_index("c").astype(jnp.int32).reshape(1)
    stacked = pltpu.VMEM((2 * states, channels), bf16)

    def shared(turn):
        return pl.pallas_call(
            functools.partial(shared_kernel, turn),
            in_specs=[smem, plain] + [hbm] * 4 + [anywhere] * 3,
            out_specs=anywhere,
            out_shape=narrow,
            scratch_shapes=[wide16_v, narrow_v] + [row_v] * 3
            + [stacked, narrow_v, dma((2, spans)), dma((3,)), dma((spans,))],
            compiler_params=params(53),
            cost_estimate=cost(6 * tokens * channels * states, 4 << 20),
            name=f"shared_terms_{turn}",
        )(core, returned, grad_output, act, gr, gi, rates, prior, later)

    swap = [(i, i ^ 1) for i in range(nc)]
    swapped = lax.ppermute(shared(0), "c", swap)
    chip = shared(1) + swapped
    here = lax.axis_index("y")
    part = tokens // ny

    def turn(array, by):
        return lax.ppermute(array, "y", [(i, (i + by) % ny) for i in range(ny)])

    def cut(array, which):
        return lax.dynamic_slice_in_dim(array, lax.rem(here + which, ny) * part, part)

    sent = [turn(cut(chip, by).astype(bf16), by) for by in range(1, ny)]

    grad_input, first = pl.pallas_call(
        input_kernel,
        in_specs=[plain] + [hbm] * 3 + [plain],
        out_specs=[hbm, plain],
        out_shape=[wide, shape((8, channels), f32)],
        scratch_shapes=[
            wide16_v, wide16_v, narrow16_v, stacked, pltpu.VMEM((8, channels), f32), wide_v,
            dma((3, spans)), dma((spans,)),
        ],
        compiler_params=params(53),
        cost_estimate=cost(4 * tokens * channels * states, 13 << 20),
        name="input_grads",
    )(returned, pre, factor, inject, conv_weight)

    *sent, first = lax.optimization_barrier((*sent, first))
    quarter = cut(chip, 0)
    for piece in sent:
        quarter = quarter + piece.astype(f32)
    quarter = quarter.astype(bf16)
    turned = [turn(quarter, by) for by in range(1, ny)]
    next_rows = lax.ppermute(first, SEQ, down)
    *turned, next_rows = lax.optimization_barrier((*turned, next_rows))
    done = jnp.zeros((tokens, states), bf16)
    for by, piece in enumerate([quarter] + turned):
        done = lax.dynamic_update_slice_in_dim(
            done, piece, lax.rem(here - by + ny, ny) * part, 0
        )
    other = lax.ppermute(done, "c", swap)
    mine_is_first = lax.axis_index("c") == 0
    grad_inject = jnp.where(mine_is_first, done, other).astype(f32)
    grad_readout = jnp.where(mine_is_first, other, done).astype(f32)

    weights = conv_weight.astype(f32)
    tail_rows = []
    for row in range(3):
        tail_rows.append(sum(weights[k] * next_rows[row - k] for k in range(row + 1)))
    patch = jnp.concatenate([jnp.zeros((5, channels), f32), jnp.stack(tail_rows)], axis=0)
    last = lax.slice_in_dim(grad_input, tokens - 8, tokens) + patch
    grad_input = lax.dynamic_update_slice(grad_input, last, (tokens - 8, 0))
    return grad_input, grad_inject, grad_readout


def build(devices, sizes):
    fine = Mesh(devices.reshape(sizes), ("z", "x", "y", "c"))
    nz, nx, ny, nc = sizes
    return jax.shard_map(
        functools.partial(body, nz * nx, ny, nc),
        mesh=fine,
        in_specs=(P(SEQ, HG), P(SEQ, HG), P(SEQ, None), P(SEQ, None), P(None, HG), P(HG, SEQ)),
        out_specs=(P(SEQ, HG), P(SEQ, None), P(SEQ, None)),
        check_vma=False,
    )


def solution(mesh):
    return build(mesh.devices, (8, 4, 4, 2))
```

```python
import functools

import jax
import jax.numpy as jnp
from jax import lax
from jax.experimental import pallas as pl
from jax.experimental.pallas import tpu as pltpu
from jax.sharding import Mesh
from jax.sharding import PartitionSpec as P

f32, bf16 = jnp.float32, jnp.bfloat16
SPAN = 256
SEQ, HG = ("z", "x"), ("y", "c")
LANES = 128
PREV = 16

NN = (((1,), (0,)), ((), ()))
NT = (((1,), (1,)), ((), ()))
TN = (((0,), (0,)), ((), ()))


def dot(a, b, dims):
    return lax.dot_general(a, b, dims, preferred_element_type=f32)


def split(v):
    high = v.astype(bf16)
    return high, (v - high.astype(f32)).astype(bf16)


def dot2(exact, v, dims):
    high, low = split(v)
    return dot(exact, high, dims) + dot(exact, low, dims)


def dot3(ah, al, bh, bl, dims):
    return dot(ah, bh, dims) + (dot(ah, bl, dims) + dot(al, bh, dims))


def places():
    return lax.broadcasted_iota(jnp.int32, (SPAN, 1), 0).astype(f32)


def span_at(span):
    return pl.ds(pl.multiple_of(span * SPAN, SPAN), SPAN)


AHEAD = 3


def each_span(spans, step, start, pieces, backwards=False, ahead=AHEAD):
    def visit(i, _):
        span = spans - 1 - i if backwards else i
        for piece in pieces:
            piece(span).wait()

        @pl.when(i + ahead < spans)
        def _():
            start(span - ahead if backwards else span + ahead)

        step(span)
        return 0

    lax.fori_loop(0, spans, visit, 0)


def starting(pieces):
    def start(span):
        for piece in pieces:
            piece(span).start()

    return start


def by_span(source, target, sems):
    def piece(span):
        if len(source.shape) == 3:
            return pltpu.make_async_copy(source.at[span], target.at[span], sems.at[span])
        rows = span_at(span)
        return pltpu.make_async_copy(source.at[rows, :], target.at[rows, :], sems.at[span])

    return piece


def fetch(spans, whole, start, backwards=False, ahead=AHEAD):
    for copy in whole:
        copy.start()
    for i in range(min(ahead, spans)):
        start(spans - 1 - i if backwards else i)
    for copy in whole:
        copy.wait()


def drain(spans, pieces):
    for span in range(spans):
        for piece in pieces:
            piece(span).wait()


TOP = 32000.0
STEPS = 4096.0


def coded(v, axis):
    most = jnp.max(jnp.abs(v), axis=axis, keepdims=True)
    power = jnp.ceil(jnp.log2(jnp.maximum(most, 2.0**-120)))
    whole = jnp.round(v * jnp.exp2(-power) * TOP).astype(jnp.int32)
    return whole.astype(jnp.int16), power


def decoded(whole, power):
    return whole.astype(f32) * (jnp.exp2(power.astype(f32)) * (1.0 / TOP))


def log_codes(log):
    steps = log * -STEPS
    high = jnp.floor(steps)
    return high, jnp.round((steps - high) * TOP)


def log_of(high, low):
    return (high.astype(f32) + low.astype(f32) * (1.0 / TOP)) * (-1.0 / STEPS)


def side_tile(height, rows):
    blank = jnp.zeros((height - len(rows), rows[0].shape[1]), f32)
    return jnp.concatenate(rows + [blank], axis=0).astype(jnp.int32).astype(jnp.int16)


def grads_kernel(
    code_hbm, grad_hbm, read_hbm, rate_ref, prior_ref, later_ref, log_ref, carry, after_hbm,
    code_ref, grad_ref, read_ref, after_ref, csem, gsem, rsem, asem,
):
    heads, spans = code_ref.shape
    sending = by_span(after_ref, after_hbm, asem)
    channels = carry.shape[1]
    pieces = [by_span(grad_hbm, grad_ref, gsem), by_span(read_hbm, read_ref, rsem)]
    start = starting(pieces)
    fetch(spans, [pltpu.make_async_copy(code_hbm, code_ref, csem)], start, backwards=True)
    logs = jnp.log1p(-code_ref[...].astype(f32) * 1e-6)
    lane = lax.broadcasted_iota(jnp.int32, (heads, channels), 1)
    row = lax.broadcasted_iota(jnp.int32, (heads, channels), 0)
    width = channels // heads
    owns = jnp.where((lane >= row * width) & (lane < (row + 1) * width), 1.0, 0.0)
    rate_ref[...] = lax.dot_general(
        logs, owns, TN, precision=lax.Precision.HIGHEST, preferred_element_type=f32
    )
    total = jnp.zeros((1, channels), f32)
    for span in range(spans):
        prior_ref[span : span + 1, :] = total
        total = total + SPAN * rate_ref[span : span + 1, :]
    log_ref[...] = total
    total = jnp.zeros((1, channels), f32)
    for span in reversed(range(spans)):
        later_ref[span : span + 1, :] = total
        total = total + SPAN * rate_ref[span : span + 1, :]
    carry[...] = jnp.zeros_like(carry)

    def step(span):
        rate = rate_ref[pl.ds(span, 1), :]
        after = carry[...]
        after_ref[span] = after
        sending(span).start()
        up = grad_ref[span_at(span), :].astype(f32) * jnp.exp(places() * rate)
        fresh = dot2(read_ref[span_at(span), :], up, TN)
        carry[...] = jnp.exp(SPAN * rate) * after + jnp.exp(rate) * fresh

    each_span(spans, step, start, pieces, backwards=True)
    drain(spans, [sending])


def convolved(x, before, weights):
    rows = jnp.concatenate([before, x], axis=0)
    one = pltpu.roll(rows, 1, axis=0)
    older = weights[1:2] * rows + weights[0:1] * one
    return (weights[3:4] * x + weights[2:3] * one[8:]) + pltpu.roll(older, 2, axis=0)[8:]


def states_kernel(
    x_hbm, halo_hbm, inject_hbm, rate_hbm, weight_hbm, own_grad_hbm, log_hbm,
    pay_ref, before_hbm,
    x_ref, halo_ref, inject_ref, rate_ref, weight_ref, own_grad_ref, log_ref, carry, prev,
    before_ref, xsem, isem, sems, osem,
):
    spans = rate_ref.shape[0]
    pieces = [by_span(x_hbm, x_ref, xsem), by_span(inject_hbm, inject_ref, isem)]
    sending = by_span(before_ref, before_hbm, osem)
    start = starting(pieces)
    late = pltpu.make_async_copy(own_grad_hbm, own_grad_ref, sems.at[4])
    fetch(
        spans,
        [
            pltpu.make_async_copy(halo_hbm, halo_ref, sems.at[0]),
            pltpu.make_async_copy(rate_hbm, rate_ref, sems.at[1]),
            pltpu.make_async_copy(weight_hbm, weight_ref, sems.at[2]),
            pltpu.make_async_copy(log_hbm, log_ref, sems.at[3]),
        ],
        start,
    )
    late.start()
    carry[...] = jnp.zeros_like(carry)
    prev[...] = halo_ref[...].astype(f32)[PREV - 8 :]
    weights = weight_ref[...].astype(f32)

    def step(span):
        x = x_ref[span_at(span), :].astype(f32)
        preact = convolved(x, prev[...], weights)
        prev[...] = x[SPAN - 8 :]
        act = (preact * jax.nn.sigmoid(preact)).astype(bf16)
        rate = rate_ref[pl.ds(span, 1), :]
        tail = jnp.exp((SPAN - 1.0 - places()) * rate)
        before = carry[...]
        before_ref[span] = before
        sending(span).start()
        fresh = dot2(inject_ref[span_at(span), :], act.astype(f32) * tail, TN)
        carry[...] = jnp.exp(SPAN * rate) * before + fresh

    each_span(spans, step, start, pieces)
    late.wait()
    chunks, height, _ = pay_ref.shape
    state_codes, state_power = coded(carry[...], 0)
    grad_codes, grad_power = coded(own_grad_ref[...], 0)
    side = side_tile(height, [state_power, grad_power, *log_codes(log_ref[...])])
    for d in range(chunks):
        rows, lanes = chunk_place(d, height)
        pay_ref[d, :, 0:LANES] = state_codes[rows, lanes]
        pay_ref[d, :, LANES : 2 * LANES] = grad_codes[rows, lanes]
        pay_ref[d, :, 2 * LANES :] = side[:, lanes]
    drain(spans, [sending])


def chunk_place(d, height):
    r, l = height * (d // 4), LANES * (d % 4)
    return slice(r, r + height), slice(l, l + LANES)


def scan_kernel(own_ref, out_ref, made):
    chunks, height, _ = out_ref.shape
    gains, states, grads = [], [], []
    for e in range(chunks):
        side = own_ref[e, :, 2 * LANES :].astype(f32)
        gains.append(jnp.exp(log_of(side[2:3], side[3:4])))
        states.append(decoded(own_ref[e, :, 0:LANES], side[0:1]))
        grads.append(decoded(own_ref[e, :, LANES : 2 * LANES], side[1:2]))
    state = jnp.zeros((height, LANES), f32)
    grad = jnp.zeros((height, LANES), f32)
    for e in range(chunks):
        made[e, :, 0:LANES] = state
        state = gains[e] * state + states[e]
    for e in reversed(range(chunks)):
        made[e, :, LANES:] = grad
        grad = gains[e] * grad + grads[e]
    for e in range(chunks):
        codes, power = coded(made[e], 0)
        out_ref[e, :, 0 : 2 * LANES] = codes
        out_ref[e, :, 2 * LANES :] = side_tile(height, [power[:, :LANES], power[:, LANES:]])


def causal():
    row = lax.broadcasted_iota(jnp.int32, (SPAN, SPAN), 0)
    return row >= lax.broadcasted_iota(jnp.int32, (SPAN, SPAN), 1)


def local_input_kernel(
    x_hbm, grad_hbm, inject_hbm, read_hbm, after_hbm, rate_hbm, later_hbm, halo_hbm, weight_hbm,
    act_hbm, pre_hbm, factor_hbm,
    x_ref, grad_ref, inject_ref, read_ref, after_ref, rate_ref, later_ref, halo_ref, weight_ref,
    act_ref, pre_ref, factor_ref, prev, isems, sems, osems,
):
    spans = rate_ref.shape[0]
    sources = [x_hbm, grad_hbm, inject_hbm, read_hbm, after_hbm]
    targets = [x_ref, grad_ref, inject_ref, read_ref, after_ref]
    pieces = [by_span(a, b, isems.at[k]) for k, (a, b) in enumerate(zip(sources, targets))]
    start = starting(pieces)
    outs = [
        by_span(act_ref, act_hbm, osems.at[0]), by_span(pre_ref, pre_hbm, osems.at[1]),
        by_span(factor_ref, factor_hbm, osems.at[2]),
    ]
    fetch(
        spans,
        [
            pltpu.make_async_copy(rate_hbm, rate_ref, sems.at[0]),
            pltpu.make_async_copy(later_hbm, later_ref, sems.at[1]),
            pltpu.make_async_copy(halo_hbm, halo_ref, sems.at[2]),
            pltpu.make_async_copy(weight_hbm, weight_ref, sems.at[3]),
        ],
        start,
    )
    prev[...] = halo_ref[...].astype(f32)[PREV - 8 :]
    weights = weight_ref[...].astype(f32)

    def step(span):
        rows = span_at(span)
        rate = rate_ref[pl.ds(span, 1), :]
        later = jnp.exp(later_ref[pl.ds(span, 1), :])
        inject, read = inject_ref[rows, :], read_ref[rows, :]
        here = places()
        x = x_ref[rows, :].astype(f32)
        preact = convolved(x, prev[...], weights)
        prev[...] = x[SPAN - 8 :]
        squashed = jax.nn.sigmoid(preact)
        act_ref[rows, :] = (preact * squashed).astype(bf16)
        slope = squashed * (1.0 + preact * (1.0 - squashed))
        steep = slope * jnp.exp(-here * rate)
        end = jnp.exp((SPAN - 1.0) * rate)
        up = (grad_ref[rows, :].astype(f32) * jnp.exp(here * rate)).astype(bf16)
        mixing = jnp.where(causal(), dot(read, inject, NT), 0.0).astype(bf16)
        stacked = jnp.concatenate(split(after_ref[span] * end), axis=0)
        doubled = jnp.concatenate([inject, inject], axis=1)
        pre = steep * (dot(mixing, up, TN) + dot(doubled, stacked, NN))
        pre_ref[rows, :] = pre.astype(bf16)
        factor_ref[rows, :] = (steep * (end * later)).astype(bf16)
        for out in outs:
            out(span).start()

    each_span(spans, step, start, pieces)
    drain(spans, outs)


def wide_product(high, low, both, states):
    wide = dot(high, both, NT)
    return wide[:, :states] + (wide[:, states:] + dot(low, both[0:states, :], NT))


def local_shared_kernel(
    grad_hbm, act_hbm, inject_hbm, read_hbm, after_hbm, before_hbm, rate_hbm,
    gi_hbm, gr_hbm,
    grad_ref, act_ref, inject_ref, read_ref, after_ref, before_ref, rate_ref,
    gi_ref, gr_ref,
    isems, sem, osems,
):
    spans = rate_ref.shape[0]
    sources = [grad_hbm, act_hbm, inject_hbm, read_hbm, after_hbm, before_hbm]
    targets = [grad_ref, act_ref, inject_ref, read_ref, after_ref, before_ref]
    pieces = [by_span(a, b, isems.at[k]) for k, (a, b) in enumerate(zip(sources, targets))]
    start = starting(pieces)
    outs = [by_span(gi_ref, gi_hbm, osems.at[0]), by_span(gr_ref, gr_hbm, osems.at[1])]
    fetch(spans, [pltpu.make_async_copy(rate_hbm, rate_ref, sem)], start)

    def step(span):
        rows = span_at(span)
        rate = rate_ref[pl.ds(span, 1), :]
        inject, read = inject_ref[rows, :], read_ref[rows, :]
        states = inject.shape[1]
        here = places()
        up = grad_ref[rows, :].astype(f32) * jnp.exp(here * rate)
        down = act_ref[rows, :].astype(f32) * jnp.exp(-here * rate)
        uph, upl = split(up)
        downh, downl = split(down)
        pairs = jnp.where(causal(), dot(uph, downh, NT), 0.0).astype(bf16)
        end = jnp.exp((SPAN - 1.0) * rate)
        afters = jnp.concatenate(split(after_ref[span] * end), axis=0)
        befores = jnp.concatenate(split(before_ref[span] * jnp.exp(rate)), axis=0)
        gi_ref[rows, :] = dot(pairs, read, TN) + wide_product(downh, downl, afters, states)
        gr_ref[rows, :] = dot(pairs, inject, NN) + wide_product(uph, upl, befores, states)
        for out in outs:
            out(span).start()

    each_span(spans, step, start, pieces)
    drain(spans, outs)


def unpacked(back_ref, both, which):
    chunks, height, _ = back_ref.shape
    states = both.shape[0] // 2
    for d in range(chunks):
        rows, lanes = chunk_place(d, height)
        power = back_ref[d, :, 2 * LANES :].astype(f32)[which : which + 1]
        v = decoded(back_ref[d, :, LANES * which : LANES * which + LANES], power)
        high, low = split(v)
        both[rows, lanes] = high
        both[states + rows.start : states + rows.stop, lanes] = low


def shared_kernel(
    grads_turn, core_ref, back_ref, grad_hbm, act_hbm, gr_hbm, gi_hbm, rate_hbm, prior_hbm, later_hbm,
    out_hbm,
    in_ref, sum_ref, rate_ref, prior_ref, later_ref, both, out_ref, isems, sems, osems,
):
    tokens, states = sum_ref.shape
    spans = tokens // SPAN
    readouts = core_ref[0] == grads_turn
    small = [
        pltpu.make_async_copy(rate_hbm, rate_ref, sems.at[0]),
        pltpu.make_async_copy(prior_hbm, prior_ref, sems.at[1]),
        pltpu.make_async_copy(later_hbm, later_ref, sems.at[2]),
    ]
    for copy in small:
        copy.start()

    pieces = [by_span(grad_hbm, in_ref, isems.at[0]), by_span(gr_hbm, sum_ref, isems.at[1])]
    others = [by_span(act_hbm, in_ref, isems.at[0]), by_span(gi_hbm, sum_ref, isems.at[1])]

    def start(span):
        @pl.when(readouts)
        def _():
            starting(pieces)(span)

        @pl.when(jnp.logical_not(readouts))
        def _():
            starting(others)(span)

    fetch(spans, [], start, ahead=spans)

    @pl.when(readouts)
    def _():
        unpacked(back_ref, both, 0)

    @pl.when(jnp.logical_not(readouts))
    def _():
        unpacked(back_ref, both, 1)

    for copy in small:
        copy.wait()
    sending = by_span(out_ref, out_hbm, osems)

    def step(span):
        rows = span_at(span)
        rate = rate_ref[pl.ds(span, 1), :]
        ahead = rate + prior_ref[pl.ds(span, 1), :]
        behind = (SPAN - 1.0) * rate + later_ref[pl.ds(span, 1), :]
        slope = jnp.where(readouts, rate, -rate)
        offset = jnp.where(readouts, ahead, behind)
        high, low = split(in_ref[rows, :].astype(f32) * jnp.exp(places() * slope + offset))
        out_ref[rows, :] = sum_ref[rows, :] + wide_product(high, low, both[...], states)
        sending(span).start()

    each_span(spans, step, start, pieces, ahead=spans)
    drain(spans, [sending])


def input_kernel(
    back_ref, pre_hbm, factor_hbm, inject_hbm, weight_ref,
    out_hbm, first_ref,
    pre_ref, factor_ref, inject_ref, grads, after, made, isems, osems,
):
    spans = pre_ref.shape[0] // SPAN
    pieces = [
        by_span(pre_hbm, pre_ref, isems.at[0]), by_span(factor_hbm, factor_ref, isems.at[1]),
        by_span(inject_hbm, inject_ref, isems.at[2]),
    ]
    out = by_span(made, out_hbm, osems)
    start = starting(pieces)
    fetch(spans, [], start, backwards=True, ahead=spans)
    unpacked(back_ref, grads, 1)
    after[...] = jnp.zeros_like(after)
    weights = weight_ref[...].astype(f32)

    def step(span):
        rows = span_at(span)
        inject = inject_ref[rows, :]
        carried = dot(jnp.concatenate([inject, inject], axis=1), grads[...], NN)
        now = pre_ref[rows, :].astype(f32) + factor_ref[rows, :].astype(f32) * carried
        joined = jnp.concatenate([now, after[...]], axis=0)
        one = pltpu.roll(joined, SPAN + 8 - 1, axis=0)
        further = weights[1:2] * joined + weights[0:1] * one
        summed = weights[3:4] * now + weights[2:3] * one[:SPAN]
        summed = summed + pltpu.roll(further, SPAN + 8 - 2, axis=0)[:SPAN]
        after[...] = now[0:8]
        made[rows, :] = summed
        out(span).start()

    each_span(spans, step, start, pieces, backwards=True, ahead=spans)
    first_ref[...] = after[...]
    drain(spans, [out])


def params(mib=54):
    return pltpu.CompilerParams(vmem_limit_bytes=mib << 20)


def cost(flops, nbytes):
    return pl.CostEstimate(flops=flops, bytes_accessed=nbytes, transcendentals=0)


def body(nseq, ny, nc, conv_input, grad_output, inject, readout, conv_weight, decay_codes):
    tokens, channels = conv_input.shape
    spans = decay_codes.shape[1]
    states = inject.shape[1]
    shape = jax.ShapeDtypeStruct
    height = 4 * states // nseq
    chunk = (nseq, height, 3 * LANES)
    smem = pl.BlockSpec(memory_space=pltpu.SMEM)
    wide, wide16 = shape((tokens, channels), f32), shape((tokens, channels), bf16)
    narrow, row = shape((tokens, states), f32), shape((spans, channels), f32)
    local = shape((spans, states, channels), f32)
    state = shape((states, channels), f32)

    up = [(i, i + 1) for i in range(nseq - 1)]
    down = [(i + 1, i) for i in range(nseq - 1)]
    halo = lax.ppermute(conv_input[tokens - PREV :], SEQ, up)

    anywhere = pl.BlockSpec(memory_space=pl.ANY)
    hbm = pl.BlockSpec(memory_space=pltpu.HBM)
    plain = pl.BlockSpec()
    wide_v, wide16_v = pltpu.VMEM(wide.shape, f32), pltpu.VMEM(wide.shape, bf16)
    narrow_v, narrow16_v = pltpu.VMEM(narrow.shape, f32), pltpu.VMEM(narrow.shape, bf16)
    row_v, state_v = pltpu.VMEM(row.shape, f32), pltpu.VMEM(state.shape, f32)
    local_v = pltpu.VMEM(local.shape, f32)
    halo_v, weight_v = pltpu.VMEM((PREV, channels), bf16), pltpu.VMEM(conv_weight.shape, bf16)
    dma = pltpu.SemaphoreType.DMA

    rates, prior, later, own_log, own_grad, after = pl.pallas_call(
        grads_kernel,
        in_specs=[hbm] * 3,
        out_specs=[plain] * 5 + [hbm],
        out_shape=[row, row, row, shape((1, channels), f32), state, local],
        scratch_shapes=[
            pltpu.VMEM(decay_codes.shape, jnp.int32), wide16_v, narrow16_v, local_v,
            dma, dma((spans,)), dma((spans,)), dma((spans,)),
        ],
        compiler_params=params(),
        cost_estimate=cost(4 * tokens * channels * states, 3 << 20),
        name="own_grads",
    )(decay_codes, grad_output, readout)

    payload, before = pl.pallas_call(
        states_kernel,
        in_specs=[hbm, anywhere, hbm, anywhere, hbm, anywhere, anywhere],
        out_specs=[plain, hbm],
        out_shape=[shape(chunk, jnp.int16), local],
        scratch_shapes=[
            wide16_v, halo_v, narrow16_v, row_v, weight_v, state_v, pltpu.VMEM((1, channels), f32),
            state_v, pltpu.VMEM((8, channels), f32), local_v,
            dma((spans,)), dma((spans,)), dma((5,)), dma((spans,)),
        ],
        compiler_params=params(),
        cost_estimate=cost(4 * tokens * channels * states, 4 << 20),
        name="own_states",
    )(conv_input, halo, inject, rates, conv_weight, own_grad, own_log)

    arrived = lax.all_to_all(payload, SEQ, 0, 0, tiled=True)

    act, pre, factor = pl.pallas_call(
        local_input_kernel,
        in_specs=[hbm] * 5 + [anywhere] * 3 + [hbm],
        out_specs=[hbm] * 3,
        out_shape=[wide16] * 3,
        scratch_shapes=[wide16_v, wide16_v, narrow16_v, narrow16_v, local_v, row_v, row_v]
        + [halo_v, weight_v] + [wide16_v] * 3 + [pltpu.VMEM((8, channels), f32)]
        + [dma((5, spans)), dma((4,)), dma((3, spans))],
        compiler_params=params(),
        cost_estimate=cost(8 * tokens * channels * SPAN, 13 << 20),
        name="local_input",
    )(conv_input, grad_output, inject, readout, after, rates, later, halo, conv_weight)
    arrived, act = lax.optimization_barrier((arrived, act))

    gi, gr = pl.pallas_call(
        local_shared_kernel,
        in_specs=[hbm] * 6 + [anywhere],
        out_specs=[hbm] * 2,
        out_shape=[narrow] * 2,
        scratch_shapes=[wide16_v] * 2 + [narrow16_v] * 2 + [local_v, local_v, row_v]
        + [narrow_v] * 2 + [dma((6, spans)), dma, dma((2, spans))],
        compiler_params=params(),
        cost_estimate=cost(12 * tokens * channels * SPAN, 9 << 20),
        name="local_shared",
    )(grad_output, act, inject, readout, after, before, rates)

    scanned = pl.pallas_call(
        scan_kernel,
        out_shape=shape(chunk, jnp.int16),
        scratch_shapes=[pltpu.VMEM((nseq, height, 2 * LANES), f32)],
        compiler_params=params(8),
        cost_estimate=cost(1 << 18, 1 << 20),
        name="carry",
    )(arrived)
    returned = lax.all_to_all(scanned, SEQ, 0, 0, tiled=True)

    core = lax.axis_index("c").astype(jnp.int32).reshape(1)
    stacked = pltpu.VMEM((2 * states, channels), bf16)

    def shared(turn):
        return pl.pallas_call(
            functools.partial(shared_kernel, turn),
            in_specs=[smem, plain] + [hbm] * 4 + [anywhere] * 3,
            out_specs=anywhere,
            out_shape=narrow,
            scratch_shapes=[wide16_v, narrow_v] + [row_v] * 3
            + [stacked, narrow_v, dma((2, spans)), dma((3,)), dma((spans,))],
            compiler_params=params(53),
            cost_estimate=cost(6 * tokens * channels * states, 4 << 20),
            name=f"shared_terms_{turn}",
        )(core, returned, grad_output, act, gr, gi, rates, prior, later)

    swap = [(i, i ^ 1) for i in range(nc)]
    swapped = lax.ppermute(shared(0), "c", swap)
    kept = shared(1)
    here = lax.axis_index("y")
    part = tokens // ny

    def turn(array, by):
        return lax.ppermute(array, "y", [(i, (i + by) % ny) for i in range(ny)])

    def cut(which):
        at = lax.rem(here + which, ny) * part
        return lax.dynamic_slice_in_dim(kept, at, part) + lax.dynamic_slice_in_dim(swapped, at, part)

    sent = [turn(cut(by).astype(bf16), by) for by in range(1, ny)]

    grad_input, first = pl.pallas_call(
        input_kernel,
        in_specs=[plain] + [hbm] * 3 + [plain],
        out_specs=[hbm, plain],
        out_shape=[wide, shape((8, channels), f32)],
        scratch_shapes=[
            wide16_v, wide16_v, narrow16_v, stacked, pltpu.VMEM((8, channels), f32), wide_v,
            dma((3, spans)), dma((spans,)),
        ],
        compiler_params=params(53),
        cost_estimate=cost(4 * tokens * channels * states, 13 << 20),
        name="input_grads",
    )(returned, pre, factor, inject, conv_weight)

    *sent, first = lax.optimization_barrier((*sent, first))
    quarter = cut(0)
    for piece in sent:
        quarter = quarter + piece.astype(f32)
    quarter = quarter.astype(bf16)
    turned = [turn(quarter, by) for by in range(1, ny)]
    next_rows = lax.ppermute(first, SEQ, down)
    *turned, next_rows = lax.optimization_barrier((*turned, next_rows))
    done = jnp.zeros((tokens, states), bf16)
    for by, piece in enumerate([quarter] + turned):
        done = lax.dynamic_update_slice_in_dim(
            done, piece, lax.rem(here - by + ny, ny) * part, 0
        )
    other = lax.ppermute(done, "c", swap)
    mine_is_first = lax.axis_index("c") == 0
    grad_inject = jnp.where(mine_is_first, done, other).astype(f32)
    grad_readout = jnp.where(mine_is_first, other, done).astype(f32)

    weights = conv_weight.astype(f32)
    tail_rows = []
    for row in range(3):
        tail_rows.append(sum(weights[k] * next_rows[row - k] for k in range(row + 1)))
    patch = jnp.concatenate([jnp.zeros((5, channels), f32), jnp.stack(tail_rows)], axis=0)
    last = lax.slice_in_dim(grad_input, tokens - 8, tokens) + patch
    grad_input = lax.dynamic_update_slice(grad_input, last, (tokens - 8, 0))
    return grad_input, grad_inject, grad_readout


def build(devices, sizes):
    fine = Mesh(devices.reshape(sizes), ("z", "x", "y", "c"))
    nz, nx, ny, nc = sizes
    return jax.shard_map(
        functools.partial(body, nz * nx, ny, nc),
        mesh=fine,
        in_specs=(P(SEQ, HG), P(SEQ, HG), P(SEQ, None), P(SEQ, None), P(None, HG), P(HG, SEQ)),
        out_specs=(P(SEQ, HG), P(SEQ, None), P(SEQ, None)),
        check_vma=False,
    )


def solution(mesh):
    return build(mesh.devices, (8, 4, 4, 2))
```

```python
import functools

import jax
import jax.numpy as jnp
from jax import lax
from jax.experimental import pallas as pl
from jax.experimental.pallas import tpu as pltpu
from jax.sharding import Mesh
from jax.sharding import PartitionSpec as P

f32, bf16 = jnp.float32, jnp.bfloat16
SPAN = 256
SEQ, HG = ("z", "x"), ("y", "c")
LANES = 128
PREV = 16

NN = (((1,), (0,)), ((), ()))
NT = (((1,), (1,)), ((), ()))
TN = (((0,), (0,)), ((), ()))


def dot(a, b, dims):
    return lax.dot_general(a, b, dims, preferred_element_type=f32)


def split(v):
    high = v.astype(bf16)
    return high, (v - high.astype(f32)).astype(bf16)


def dot2(exact, v, dims):
    high, low = split(v)
    return dot(exact, high, dims) + dot(exact, low, dims)


def dot3(ah, al, bh, bl, dims):
    return dot(ah, bh, dims) + (dot(ah, bl, dims) + dot(al, bh, dims))


def places():
    return lax.broadcasted_iota(jnp.int32, (SPAN, 1), 0).astype(f32)


def span_at(span):
    return pl.ds(pl.multiple_of(span * SPAN, SPAN), SPAN)


AHEAD = 3


def each_span(spans, step, start, pieces, backwards=False, ahead=AHEAD, unroll=1):
    def visit(i, _):
        span = spans - 1 - i if backwards else i
        for piece in pieces:
            piece(span).wait()

        @pl.when(i + ahead < spans)
        def _():
            start(span - ahead if backwards else span + ahead)

        step(span)
        return 0

    lax.fori_loop(0, spans, visit, 0, unroll=unroll)


def starting(pieces):
    def start(span):
        for piece in pieces:
            piece(span).start()

    return start


def by_span(source, target, sems):
    def piece(span):
        if len(source.shape) == 3:
            return pltpu.make_async_copy(source.at[span], target.at[span], sems.at[span])
        rows = span_at(span)
        return pltpu.make_async_copy(source.at[rows, :], target.at[rows, :], sems.at[span])

    return piece


def fetch(spans, whole, start, backwards=False, ahead=AHEAD):
    for copy in whole:
        copy.start()
    for i in range(min(ahead, spans)):
        start(spans - 1 - i if backwards else i)
    for copy in whole:
        copy.wait()


def drain(spans, pieces):
    for span in range(spans):
        for piece in pieces:
            piece(span).wait()


TOP = 32000.0
STEPS = 4096.0


def coded(v, axis):
    most = jnp.max(jnp.abs(v), axis=axis, keepdims=True)
    power = jnp.ceil(jnp.log2(jnp.maximum(most, 2.0**-120)))
    whole = jnp.round(v * jnp.exp2(-power) * TOP).astype(jnp.int32)
    return whole.astype(jnp.int16), power


def decoded(whole, power):
    return whole.astype(f32) * (jnp.exp2(power.astype(f32)) * (1.0 / TOP))


def log_codes(log):
    steps = log * -STEPS
    high = jnp.floor(steps)
    return high, jnp.round((steps - high) * TOP)


def log_of(high, low):
    return (high.astype(f32) + low.astype(f32) * (1.0 / TOP)) * (-1.0 / STEPS)


def side_tile(height, rows):
    blank = jnp.zeros((height - len(rows), rows[0].shape[1]), f32)
    return jnp.concatenate(rows + [blank], axis=0).astype(jnp.int32).astype(jnp.int16)


def grads_kernel(
    code_hbm, grad_hbm, read_hbm, rate_ref, prior_ref, later_ref, log_ref, carry, after_hbm,
    code_ref, grad_ref, read_ref, after_ref, csem, gsem, rsem, asem,
):
    heads, spans = code_ref.shape
    sending = by_span(after_ref, after_hbm, asem)
    channels = carry.shape[1]
    pieces = [by_span(grad_hbm, grad_ref, gsem), by_span(read_hbm, read_ref, rsem)]
    start = starting(pieces)
    fetch(spans, [pltpu.make_async_copy(code_hbm, code_ref, csem)], start, backwards=True)
    logs = jnp.log1p(-code_ref[...].astype(f32) * 1e-6)
    lane = lax.broadcasted_iota(jnp.int32, (heads, channels), 1)
    row = lax.broadcasted_iota(jnp.int32, (heads, channels), 0)
    width = channels // heads
    owns = jnp.where((lane >= row * width) & (lane < (row + 1) * width), 1.0, 0.0)
    rate_ref[...] = lax.dot_general(
        logs, owns, TN, precision=lax.Precision.HIGHEST, preferred_element_type=f32
    )
    total = jnp.zeros((1, channels), f32)
    for span in range(spans):
        prior_ref[span : span + 1, :] = total
        total = total + SPAN * rate_ref[span : span + 1, :]
    log_ref[...] = total
    total = jnp.zeros((1, channels), f32)
    for span in reversed(range(spans)):
        later_ref[span : span + 1, :] = total
        total = total + SPAN * rate_ref[span : span + 1, :]
    carry[...] = jnp.zeros_like(carry)

    def step(span):
        rate = rate_ref[pl.ds(span, 1), :]
        after = carry[...]
        after_ref[span] = after
        sending(span).start()
        up = grad_ref[span_at(span), :].astype(f32) * jnp.exp(places() * rate)
        fresh = dot2(read_ref[span_at(span), :], up, TN)
        carry[...] = jnp.exp(SPAN * rate) * after + jnp.exp(rate) * fresh

    each_span(spans, step, start, pieces, backwards=True)
    drain(spans, [sending])


def convolved(x, before, weights):
    rows = jnp.concatenate([before, x], axis=0)
    one = pltpu.roll(rows, 1, axis=0)
    older = weights[1:2] * rows + weights[0:1] * one
    return (weights[3:4] * x + weights[2:3] * one[8:]) + pltpu.roll(older, 2, axis=0)[8:]


def states_kernel(
    x_hbm, halo_hbm, inject_hbm, rate_hbm, weight_hbm, own_grad_hbm, log_hbm,
    pay_ref, before_hbm,
    x_ref, halo_ref, inject_ref, rate_ref, weight_ref, own_grad_ref, log_ref, carry, prev,
    before_ref, xsem, isem, sems, osem,
):
    spans = rate_ref.shape[0]
    pieces = [by_span(x_hbm, x_ref, xsem), by_span(inject_hbm, inject_ref, isem)]
    sending = by_span(before_ref, before_hbm, osem)
    start = starting(pieces)
    late = pltpu.make_async_copy(own_grad_hbm, own_grad_ref, sems.at[4])
    fetch(
        spans,
        [
            pltpu.make_async_copy(halo_hbm, halo_ref, sems.at[0]),
            pltpu.make_async_copy(rate_hbm, rate_ref, sems.at[1]),
            pltpu.make_async_copy(weight_hbm, weight_ref, sems.at[2]),
            pltpu.make_async_copy(log_hbm, log_ref, sems.at[3]),
        ],
        start,
    )
    late.start()
    carry[...] = jnp.zeros_like(carry)
    prev[...] = halo_ref[...].astype(f32)[PREV - 8 :]
    weights = weight_ref[...].astype(f32)

    def step(span):
        x = x_ref[span_at(span), :].astype(f32)
        preact = convolved(x, prev[...], weights)
        prev[...] = x[SPAN - 8 :]
        act = (preact * jax.nn.sigmoid(preact)).astype(bf16)
        rate = rate_ref[pl.ds(span, 1), :]
        tail = jnp.exp((SPAN - 1.0 - places()) * rate)
        before = carry[...]
        before_ref[span] = before
        sending(span).start()
        fresh = dot2(inject_ref[span_at(span), :], act.astype(f32) * tail, TN)
        carry[...] = jnp.exp(SPAN * rate) * before + fresh

    each_span(spans, step, start, pieces, unroll=True)
    late.wait()
    chunks, height, _ = pay_ref.shape
    state_codes, state_power = coded(carry[...], 0)
    grad_codes, grad_power = coded(own_grad_ref[...], 0)
    side = side_tile(height, [state_power, grad_power, *log_codes(log_ref[...])])
    for d in range(chunks):
        rows, lanes = chunk_place(d, height)
        pay_ref[d, :, 0:LANES] = state_codes[rows, lanes]
        pay_ref[d, :, LANES : 2 * LANES] = grad_codes[rows, lanes]
        pay_ref[d, :, 2 * LANES :] = side[:, lanes]
    drain(spans, [sending])


def chunk_place(d, height):
    r, l = height * (d // 4), LANES * (d % 4)
    return slice(r, r + height), slice(l, l + LANES)


def scan_kernel(own_ref, out_ref, made):
    chunks, height, _ = out_ref.shape
    gains, states, grads = [], [], []
    for e in range(chunks):
        side = own_ref[e, :, 2 * LANES :].astype(f32)
        gains.append(jnp.exp(log_of(side[2:3], side[3:4])))
        states.append(decoded(own_ref[e, :, 0:LANES], side[0:1]))
        grads.append(decoded(own_ref[e, :, LANES : 2 * LANES], side[1:2]))
    state = jnp.zeros((height, LANES), f32)
    grad = jnp.zeros((height, LANES), f32)
    for e in range(chunks):
        made[e, :, 0:LANES] = state
        state = gains[e] * state + states[e]
    for e in reversed(range(chunks)):
        made[e, :, LANES:] = grad
        grad = gains[e] * grad + grads[e]
    for e in range(chunks):
        codes, power = coded(made[e], 0)
        out_ref[e, :, 0 : 2 * LANES] = codes
        out_ref[e, :, 2 * LANES :] = side_tile(height, [power[:, :LANES], power[:, LANES:]])


def causal():
    row = lax.broadcasted_iota(jnp.int32, (SPAN, SPAN), 0)
    return row >= lax.broadcasted_iota(jnp.int32, (SPAN, SPAN), 1)


def local_input_kernel(
    x_hbm, grad_hbm, inject_hbm, read_hbm, after_hbm, rate_hbm, later_hbm, halo_hbm, weight_hbm,
    act_hbm, pre_hbm, factor_hbm,
    x_ref, grad_ref, inject_ref, read_ref, after_ref, rate_ref, later_ref, halo_ref, weight_ref,
    act_ref, pre_ref, factor_ref, prev, isems, sems, osems,
):
    spans = rate_ref.shape[0]
    sources = [x_hbm, grad_hbm, inject_hbm, read_hbm, after_hbm]
    targets = [x_ref, grad_ref, inject_ref, read_ref, after_ref]
    pieces = [by_span(a, b, isems.at[k]) for k, (a, b) in enumerate(zip(sources, targets))]
    start = starting(pieces)
    outs = [
        by_span(act_ref, act_hbm, osems.at[0]), by_span(pre_ref, pre_hbm, osems.at[1]),
        by_span(factor_ref, factor_hbm, osems.at[2]),
    ]
    fetch(
        spans,
        [
            pltpu.make_async_copy(rate_hbm, rate_ref, sems.at[0]),
            pltpu.make_async_copy(later_hbm, later_ref, sems.at[1]),
            pltpu.make_async_copy(halo_hbm, halo_ref, sems.at[2]),
            pltpu.make_async_copy(weight_hbm, weight_ref, sems.at[3]),
        ],
        start,
    )
    prev[...] = halo_ref[...].astype(f32)[PREV - 8 :]
    weights = weight_ref[...].astype(f32)

    def step(span):
        rows = span_at(span)
        rate = rate_ref[pl.ds(span, 1), :]
        later = jnp.exp(later_ref[pl.ds(span, 1), :])
        inject, read = inject_ref[rows, :], read_ref[rows, :]
        here = places()
        x = x_ref[rows, :].astype(f32)
        preact = convolved(x, prev[...], weights)
        prev[...] = x[SPAN - 8 :]
        squashed = jax.nn.sigmoid(preact)
        act_ref[rows, :] = (preact * squashed).astype(bf16)
        slope = squashed * (1.0 + preact * (1.0 - squashed))
        steep = slope * jnp.exp(-here * rate)
        end = jnp.exp((SPAN - 1.0) * rate)
        up = (grad_ref[rows, :].astype(f32) * jnp.exp(here * rate)).astype(bf16)
        mixing = jnp.where(causal(), dot(read, inject, NT), 0.0).astype(bf16)
        stacked = jnp.concatenate(split(after_ref[span] * end), axis=0)
        doubled = jnp.concatenate([inject, inject], axis=1)
        pre = steep * (dot(mixing, up, TN) + dot(doubled, stacked, NN))
        pre_ref[rows, :] = pre.astype(bf16)
        factor_ref[rows, :] = (steep * (end * later)).astype(bf16)
        for out in outs:
            out(span).start()

    each_span(spans, step, start, pieces)
    drain(spans, outs)


def wide_product(high, low, both, states):
    wide = dot(high, both, NT)
    return wide[:, :states] + (wide[:, states:] + dot(low, both[0:states, :], NT))


def local_shared_kernel(
    grad_hbm, act_hbm, inject_hbm, read_hbm, after_hbm, before_hbm, rate_hbm,
    gi_hbm, gr_hbm,
    grad_ref, act_ref, inject_ref, read_ref, after_ref, before_ref, rate_ref,
    gi_ref, gr_ref,
    isems, sem, osems,
):
    spans = rate_ref.shape[0]
    sources = [grad_hbm, act_hbm, inject_hbm, read_hbm, after_hbm, before_hbm]
    targets = [grad_ref, act_ref, inject_ref, read_ref, after_ref, before_ref]
    pieces = [by_span(a, b, isems.at[k]) for k, (a, b) in enumerate(zip(sources, targets))]
    start = starting(pieces)
    outs = [by_span(gi_ref, gi_hbm, osems.at[0]), by_span(gr_ref, gr_hbm, osems.at[1])]
    fetch(spans, [pltpu.make_async_copy(rate_hbm, rate_ref, sem)], start)

    def step(span):
        rows = span_at(span)
        rate = rate_ref[pl.ds(span, 1), :]
        inject, read = inject_ref[rows, :], read_ref[rows, :]
        states = inject.shape[1]
        here = places()
        up = grad_ref[rows, :].astype(f32) * jnp.exp(here * rate)
        down = act_ref[rows, :].astype(f32) * jnp.exp(-here * rate)
        uph, upl = split(up)
        downh, downl = split(down)
        pairs = jnp.where(causal(), dot(uph, downh, NT), 0.0).astype(bf16)
        end = jnp.exp((SPAN - 1.0) * rate)
        afters = jnp.concatenate(split(after_ref[span] * end), axis=0)
        befores = jnp.concatenate(split(before_ref[span] * jnp.exp(rate)), axis=0)
        gi_ref[rows, :] = dot(pairs, read, TN) + wide_product(downh, downl, afters, states)
        gr_ref[rows, :] = dot(pairs, inject, NN) + wide_product(uph, upl, befores, states)
        for out in outs:
            out(span).start()

    each_span(spans, step, start, pieces, unroll=True)
    drain(spans, outs)


def unpacked(back_ref, both, which):
    chunks, height, _ = back_ref.shape
    states = both.shape[0] // 2
    for d in range(chunks):
        rows, lanes = chunk_place(d, height)
        power = back_ref[d, :, 2 * LANES :].astype(f32)[which : which + 1]
        v = decoded(back_ref[d, :, LANES * which : LANES * which + LANES], power)
        high, low = split(v)
        both[rows, lanes] = high
        both[states + rows.start : states + rows.stop, lanes] = low


def shared_kernel(
    grads_turn, core_ref, back_ref, grad_hbm, act_hbm, gr_hbm, gi_hbm, rate_hbm, prior_hbm, later_hbm,
    out_hbm,
    in_ref, sum_ref, rate_ref, prior_ref, later_ref, both, out_ref, isems, sems, osems,
):
    tokens, states = sum_ref.shape
    spans = tokens // SPAN
    readouts = core_ref[0] == grads_turn
    small = [
        pltpu.make_async_copy(rate_hbm, rate_ref, sems.at[0]),
        pltpu.make_async_copy(prior_hbm, prior_ref, sems.at[1]),
        pltpu.make_async_copy(later_hbm, later_ref, sems.at[2]),
    ]
    for copy in small:
        copy.start()

    pieces = [by_span(grad_hbm, in_ref, isems.at[0]), by_span(gr_hbm, sum_ref, isems.at[1])]
    others = [by_span(act_hbm, in_ref, isems.at[0]), by_span(gi_hbm, sum_ref, isems.at[1])]

    def start(span):
        @pl.when(readouts)
        def _():
            starting(pieces)(span)

        @pl.when(jnp.logical_not(readouts))
        def _():
            starting(others)(span)

    fetch(spans, [], start, ahead=spans)

    @pl.when(readouts)
    def _():
        unpacked(back_ref, both, 0)

    @pl.when(jnp.logical_not(readouts))
    def _():
        unpacked(back_ref, both, 1)

    for copy in small:
        copy.wait()
    sending = by_span(out_ref, out_hbm, osems)

    def step(span):
        rows = span_at(span)
        rate = rate_ref[pl.ds(span, 1), :]
        ahead = rate + prior_ref[pl.ds(span, 1), :]
        behind = (SPAN - 1.0) * rate + later_ref[pl.ds(span, 1), :]
        slope = jnp.where(readouts, rate, -rate)
        offset = jnp.where(readouts, ahead, behind)
        high, low = split(in_ref[rows, :].astype(f32) * jnp.exp(places() * slope + offset))
        out_ref[rows, :] = sum_ref[rows, :] + wide_product(high, low, both[...], states)
        sending(span).start()

    each_span(spans, step, start, pieces, ahead=spans)
    drain(spans, [sending])


def input_kernel(
    back_ref, pre_hbm, factor_hbm, inject_hbm, weight_ref,
    out_hbm, first_ref,
    pre_ref, factor_ref, inject_ref, grads, after, made, isems, osems,
):
    spans = pre_ref.shape[0] // SPAN
    pieces = [
        by_span(pre_hbm, pre_ref, isems.at[0]), by_span(factor_hbm, factor_ref, isems.at[1]),
        by_span(inject_hbm, inject_ref, isems.at[2]),
    ]
    out = by_span(made, out_hbm, osems)
    start = starting(pieces)
    fetch(spans, [], start, backwards=True, ahead=spans)
    unpacked(back_ref, grads, 1)
    after[...] = jnp.zeros_like(after)
    weights = weight_ref[...].astype(f32)

    def step(span):
        rows = span_at(span)
        inject = inject_ref[rows, :]
        carried = dot(jnp.concatenate([inject, inject], axis=1), grads[...], NN)
        now = pre_ref[rows, :].astype(f32) + factor_ref[rows, :].astype(f32) * carried
        joined = jnp.concatenate([now, after[...]], axis=0)
        one = pltpu.roll(joined, SPAN + 8 - 1, axis=0)
        further = weights[1:2] * joined + weights[0:1] * one
        summed = weights[3:4] * now + weights[2:3] * one[:SPAN]
        summed = summed + pltpu.roll(further, SPAN + 8 - 2, axis=0)[:SPAN]
        after[...] = now[0:8]
        made[rows, :] = summed
        out(span).start()

    each_span(spans, step, start, pieces, backwards=True, ahead=spans)
    first_ref[...] = after[...]
    drain(spans, [out])


def params(mib=54):
    return pltpu.CompilerParams(vmem_limit_bytes=mib << 20)


def cost(flops, nbytes):
    return pl.CostEstimate(flops=flops, bytes_accessed=nbytes, transcendentals=0)


def body(nseq, ny, nc, conv_input, grad_output, inject, readout, conv_weight, decay_codes):
    tokens, channels = conv_input.shape
    spans = decay_codes.shape[1]
    states = inject.shape[1]
    shape = jax.ShapeDtypeStruct
    height = 4 * states // nseq
    chunk = (nseq, height, 3 * LANES)
    smem = pl.BlockSpec(memory_space=pltpu.SMEM)
    wide, wide16 = shape((tokens, channels), f32), shape((tokens, channels), bf16)
    narrow, row = shape((tokens, states), f32), shape((spans, channels), f32)
    local = shape((spans, states, channels), f32)
    state = shape((states, channels), f32)

    up = [(i, i + 1) for i in range(nseq - 1)]
    down = [(i + 1, i) for i in range(nseq - 1)]
    halo = lax.ppermute(conv_input[tokens - PREV :], SEQ, up)

    anywhere = pl.BlockSpec(memory_space=pl.ANY)
    hbm = pl.BlockSpec(memory_space=pltpu.HBM)
    plain = pl.BlockSpec()
    wide_v, wide16_v = pltpu.VMEM(wide.shape, f32), pltpu.VMEM(wide.shape, bf16)
    narrow_v, narrow16_v = pltpu.VMEM(narrow.shape, f32), pltpu.VMEM(narrow.shape, bf16)
    row_v, state_v = pltpu.VMEM(row.shape, f32), pltpu.VMEM(state.shape, f32)
    local_v = pltpu.VMEM(local.shape, f32)
    halo_v, weight_v = pltpu.VMEM((PREV, channels), bf16), pltpu.VMEM(conv_weight.shape, bf16)
    dma = pltpu.SemaphoreType.DMA

    rates, prior, later, own_log, own_grad, after = pl.pallas_call(
        grads_kernel,
        in_specs=[hbm] * 3,
        out_specs=[plain] * 5 + [hbm],
        out_shape=[row, row, row, shape((1, channels), f32), state, local],
        scratch_shapes=[
            pltpu.VMEM(decay_codes.shape, jnp.int32), wide16_v, narrow16_v, local_v,
            dma, dma((spans,)), dma((spans,)), dma((spans,)),
        ],
        compiler_params=params(),
        cost_estimate=cost(4 * tokens * channels * states, 3 << 20),
        name="own_grads",
    )(decay_codes, grad_output, readout)

    payload, before = pl.pallas_call(
        states_kernel,
        in_specs=[hbm, anywhere, hbm, anywhere, hbm, anywhere, anywhere],
        out_specs=[plain, hbm],
        out_shape=[shape(chunk, jnp.int16), local],
        scratch_shapes=[
            wide16_v, halo_v, narrow16_v, row_v, weight_v, state_v, pltpu.VMEM((1, channels), f32),
            state_v, pltpu.VMEM((8, channels), f32), local_v,
            dma((spans,)), dma((spans,)), dma((5,)), dma((spans,)),
        ],
        compiler_params=params(),
        cost_estimate=cost(4 * tokens * channels * states, 4 << 20),
        name="own_states",
    )(conv_input, halo, inject, rates, conv_weight, own_grad, own_log)

    arrived = lax.all_to_all(payload, SEQ, 0, 0, tiled=True)

    act, pre, factor = pl.pallas_call(
        local_input_kernel,
        in_specs=[hbm] * 5 + [anywhere] * 3 + [hbm],
        out_specs=[hbm] * 3,
        out_shape=[wide16] * 3,
        scratch_shapes=[wide16_v, wide16_v, narrow16_v, narrow16_v, local_v, row_v, row_v]
        + [halo_v, weight_v] + [wide16_v] * 3 + [pltpu.VMEM((8, channels), f32)]
        + [dma((5, spans)), dma((4,)), dma((3, spans))],
        compiler_params=params(),
        cost_estimate=cost(8 * tokens * channels * SPAN, 13 << 20),
        name="local_input",
    )(conv_input, grad_output, inject, readout, after, rates, later, halo, conv_weight)
    arrived, act = lax.optimization_barrier((arrived, act))

    gi, gr = pl.pallas_call(
        local_shared_kernel,
        in_specs=[hbm] * 6 + [anywhere],
        out_specs=[hbm] * 2,
        out_shape=[narrow] * 2,
        scratch_shapes=[wide16_v] * 2 + [narrow16_v] * 2 + [local_v, local_v, row_v]
        + [narrow_v] * 2 + [dma((6, spans)), dma, dma((2, spans))],
        compiler_params=params(),
        cost_estimate=cost(12 * tokens * channels * SPAN, 9 << 20),
        name="local_shared",
    )(grad_output, act, inject, readout, after, before, rates)

    scanned = pl.pallas_call(
        scan_kernel,
        out_shape=shape(chunk, jnp.int16),
        scratch_shapes=[pltpu.VMEM((nseq, height, 2 * LANES), f32)],
        compiler_params=params(8),
        cost_estimate=cost(1 << 18, 1 << 20),
        name="carry",
    )(arrived)
    returned = lax.all_to_all(scanned, SEQ, 0, 0, tiled=True)

    core = lax.axis_index("c").astype(jnp.int32).reshape(1)
    stacked = pltpu.VMEM((2 * states, channels), bf16)

    def shared(turn):
        return pl.pallas_call(
            functools.partial(shared_kernel, turn),
            in_specs=[smem, plain] + [hbm] * 4 + [anywhere] * 3,
            out_specs=anywhere,
            out_shape=narrow,
            scratch_shapes=[wide16_v, narrow_v] + [row_v] * 3
            + [stacked, narrow_v, dma((2, spans)), dma((3,)), dma((spans,))],
            compiler_params=params(53),
            cost_estimate=cost(6 * tokens * channels * states, 4 << 20),
            name=f"shared_terms_{turn}",
        )(core, returned, grad_output, act, gr, gi, rates, prior, later)

    swap = [(i, i ^ 1) for i in range(nc)]
    swapped = lax.ppermute(shared(0), "c", swap)
    kept = shared(1)
    here = lax.axis_index("y")
    part = tokens // ny

    def turn(array, by):
        return lax.ppermute(array, "y", [(i, (i + by) % ny) for i in range(ny)])

    def cut(which):
        at = lax.rem(here + which, ny) * part
        return lax.dynamic_slice_in_dim(kept, at, part) + lax.dynamic_slice_in_dim(swapped, at, part)

    sent = [turn(cut(by).astype(bf16), by) for by in range(1, ny)]

    grad_input, first = pl.pallas_call(
        input_kernel,
        in_specs=[plain] + [hbm] * 3 + [plain],
        out_specs=[hbm, plain],
        out_shape=[wide, shape((8, channels), f32)],
        scratch_shapes=[
            wide16_v, wide16_v, narrow16_v, stacked, pltpu.VMEM((8, channels), f32), wide_v,
            dma((3, spans)), dma((spans,)),
        ],
        compiler_params=params(53),
        cost_estimate=cost(4 * tokens * channels * states, 13 << 20),
        name="input_grads",
    )(returned, pre, factor, inject, conv_weight)

    *sent, first = lax.optimization_barrier((*sent, first))
    quarter = cut(0)
    for piece in sent:
        quarter = quarter + piece.astype(f32)
    quarter = quarter.astype(bf16)
    turned = [turn(quarter, by) for by in range(1, ny)]
    next_rows = lax.ppermute(first, SEQ, down)
    *turned, next_rows = lax.optimization_barrier((*turned, next_rows))
    done = jnp.zeros((tokens, states), bf16)
    for by, piece in enumerate([quarter] + turned):
        done = lax.dynamic_update_slice_in_dim(
            done, piece, lax.rem(here - by + ny, ny) * part, 0
        )
    other = lax.ppermute(done, "c", swap)
    mine_is_first = lax.axis_index("c") == 0
    grad_inject = jnp.where(mine_is_first, done, other).astype(f32)
    grad_readout = jnp.where(mine_is_first, other, done).astype(f32)

    weights = conv_weight.astype(f32)
    tail_rows = []
    for row in range(3):
        tail_rows.append(sum(weights[k] * next_rows[row - k] for k in range(row + 1)))
    patch = jnp.concatenate([jnp.zeros((5, channels), f32), jnp.stack(tail_rows)], axis=0)
    last = lax.slice_in_dim(grad_input, tokens - 8, tokens) + patch
    grad_input = lax.dynamic_update_slice(grad_input, last, (tokens - 8, 0))
    return grad_input, grad_inject, grad_readout


def build(devices, sizes):
    fine = Mesh(devices.reshape(sizes), ("z", "x", "y", "c"))
    nz, nx, ny, nc = sizes
    return jax.shard_map(
        functools.partial(body, nz * nx, ny, nc),
        mesh=fine,
        in_specs=(P(SEQ, HG), P(SEQ, HG), P(SEQ, None), P(SEQ, None), P(None, HG), P(HG, SEQ)),
        out_specs=(P(SEQ, HG), P(SEQ, None), P(SEQ, None)),
        check_vma=False,
    )


def solution(mesh):
    return build(mesh.devices, (8, 4, 4, 2))
```

```python
import functools

import jax
import jax.numpy as jnp
from jax import lax
from jax.experimental import pallas as pl
from jax.experimental.pallas import tpu as pltpu
from jax.sharding import Mesh
from jax.sharding import PartitionSpec as P

f32, bf16 = jnp.float32, jnp.bfloat16
SPAN = 256
SEQ, HG = ("z", "x"), ("y", "c")
LANES = 128
PREV = 16

NN = (((1,), (0,)), ((), ()))
NT = (((1,), (1,)), ((), ()))
TN = (((0,), (0,)), ((), ()))


def dot(a, b, dims):
    return lax.dot_general(a, b, dims, preferred_element_type=f32)


def split(v):
    high = v.astype(bf16)
    return high, (v - high.astype(f32)).astype(bf16)


def dot2(exact, v, dims):
    high, low = split(v)
    return dot(exact, high, dims) + dot(exact, low, dims)


def dot3(ah, al, bh, bl, dims):
    return dot(ah, bh, dims) + (dot(ah, bl, dims) + dot(al, bh, dims))


def places():
    return lax.broadcasted_iota(jnp.int32, (SPAN, 1), 0).astype(f32)


def span_at(span):
    return pl.ds(pl.multiple_of(span * SPAN, SPAN), SPAN)


AHEAD = 3


def each_span(spans, step, start, pieces, backwards=False, ahead=AHEAD, unroll=1):
    def visit(i, _):
        span = spans - 1 - i if backwards else i
        for piece in pieces:
            piece(span).wait()

        @pl.when(i + ahead < spans)
        def _():
            start(span - ahead if backwards else span + ahead)

        step(span)
        return 0

    lax.fori_loop(0, spans, visit, 0, unroll=unroll)


def starting(pieces):
    def start(span):
        for piece in pieces:
            piece(span).start()

    return start


def by_span(source, target, sems):
    def piece(span):
        if len(source.shape) == 3:
            return pltpu.make_async_copy(source.at[span], target.at[span], sems.at[span])
        rows = span_at(span)
        return pltpu.make_async_copy(source.at[rows, :], target.at[rows, :], sems.at[span])

    return piece


def fetch(spans, whole, start, backwards=False, ahead=AHEAD):
    for copy in whole:
        copy.start()
    for i in range(min(ahead, spans)):
        start(spans - 1 - i if backwards else i)
    for copy in whole:
        copy.wait()


def drain(spans, pieces):
    for span in range(spans):
        for piece in pieces:
            piece(span).wait()


TOP = 32000.0
STEPS = 4096.0


def coded(v, axis):
    most = jnp.max(jnp.abs(v), axis=axis, keepdims=True)
    power = jnp.ceil(jnp.log2(jnp.maximum(most, 2.0**-120)))
    whole = jnp.round(v * jnp.exp2(-power) * TOP).astype(jnp.int32)
    return whole.astype(jnp.int16), power


def decoded(whole, power):
    return whole.astype(f32) * (jnp.exp2(power.astype(f32)) * (1.0 / TOP))


def log_codes(log):
    steps = log * -STEPS
    high = jnp.floor(steps)
    return high, jnp.round((steps - high) * TOP)


def log_of(high, low):
    return (high.astype(f32) + low.astype(f32) * (1.0 / TOP)) * (-1.0 / STEPS)


def side_tile(height, rows):
    blank = jnp.zeros((height - len(rows), rows[0].shape[1]), f32)
    return jnp.concatenate(rows + [blank], axis=0).astype(jnp.int32).astype(jnp.int16)


def grads_kernel(
    code_hbm, grad_hbm, read_hbm, rate_ref, prior_ref, later_ref, log_ref, carry, after_hbm,
    code_ref, grad_ref, read_ref, after_ref, csem, gsem, rsem, asem,
):
    heads, spans = code_ref.shape
    sending = by_span(after_ref, after_hbm, asem)
    channels = carry.shape[1]
    pieces = [by_span(grad_hbm, grad_ref, gsem), by_span(read_hbm, read_ref, rsem)]
    start = starting(pieces)
    fetch(spans, [pltpu.make_async_copy(code_hbm, code_ref, csem)], start, backwards=True)
    logs = jnp.log1p(-code_ref[...].astype(f32) * 1e-6)
    lane = lax.broadcasted_iota(jnp.int32, (heads, channels), 1)
    row = lax.broadcasted_iota(jnp.int32, (heads, channels), 0)
    width = channels // heads
    owns = jnp.where((lane >= row * width) & (lane < (row + 1) * width), 1.0, 0.0)
    rate_ref[...] = lax.dot_general(
        logs, owns, TN, precision=lax.Precision.HIGHEST, preferred_element_type=f32
    )
    total = jnp.zeros((1, channels), f32)
    for span in range(spans):
        prior_ref[span : span + 1, :] = total
        total = total + SPAN * rate_ref[span : span + 1, :]
    log_ref[...] = total
    total = jnp.zeros((1, channels), f32)
    for span in reversed(range(spans)):
        later_ref[span : span + 1, :] = total
        total = total + SPAN * rate_ref[span : span + 1, :]
    carry[...] = jnp.zeros_like(carry)

    def step(span):
        rate = rate_ref[pl.ds(span, 1), :]
        after = carry[...]
        after_ref[span] = after
        sending(span).start()
        up = grad_ref[span_at(span), :].astype(f32) * jnp.exp(places() * rate)
        fresh = dot2(read_ref[span_at(span), :], up, TN)
        carry[...] = jnp.exp(SPAN * rate) * after + jnp.exp(rate) * fresh

    each_span(spans, step, start, pieces, backwards=True)
    drain(spans, [sending])


def convolved(x, before, weights):
    rows = jnp.concatenate([before, x], axis=0)
    one = pltpu.roll(rows, 1, axis=0)
    older = weights[1:2] * rows + weights[0:1] * one
    return (weights[3:4] * x + weights[2:3] * one[8:]) + pltpu.roll(older, 2, axis=0)[8:]


def states_kernel(
    x_hbm, halo_hbm, inject_hbm, rate_hbm, weight_hbm, own_grad_hbm, log_hbm,
    pay_ref, before_hbm,
    x_ref, halo_ref, inject_ref, rate_ref, weight_ref, own_grad_ref, log_ref, carry, prev,
    before_ref, xsem, isem, sems, osem,
):
    spans = rate_ref.shape[0]
    pieces = [by_span(x_hbm, x_ref, xsem), by_span(inject_hbm, inject_ref, isem)]
    sending = by_span(before_ref, before_hbm, osem)
    start = starting(pieces)
    late = pltpu.make_async_copy(own_grad_hbm, own_grad_ref, sems.at[4])
    fetch(
        spans,
        [
            pltpu.make_async_copy(halo_hbm, halo_ref, sems.at[0]),
            pltpu.make_async_copy(rate_hbm, rate_ref, sems.at[1]),
            pltpu.make_async_copy(weight_hbm, weight_ref, sems.at[2]),
            pltpu.make_async_copy(log_hbm, log_ref, sems.at[3]),
        ],
        start,
    )
    late.start()
    carry[...] = jnp.zeros_like(carry)
    prev[...] = halo_ref[...].astype(f32)[PREV - 8 :]
    weights = weight_ref[...].astype(f32)

    def step(span):
        x = x_ref[span_at(span), :].astype(f32)
        preact = convolved(x, prev[...], weights)
        prev[...] = x[SPAN - 8 :]
        act = (preact * jax.nn.sigmoid(preact)).astype(bf16)
        rate = rate_ref[pl.ds(span, 1), :]
        tail = jnp.exp((SPAN - 1.0 - places()) * rate)
        before = carry[...]
        before_ref[span] = before
        sending(span).start()
        fresh = dot2(inject_ref[span_at(span), :], act.astype(f32) * tail, TN)
        carry[...] = jnp.exp(SPAN * rate) * before + fresh

    each_span(spans, step, start, pieces, unroll=True)
    late.wait()
    chunks, height, _ = pay_ref.shape
    state_codes, state_power = coded(carry[...], 0)
    grad_codes, grad_power = coded(own_grad_ref[...], 0)
    side = side_tile(height, [state_power, grad_power, *log_codes(log_ref[...])])
    for d in range(chunks):
        rows, lanes = chunk_place(d, height)
        pay_ref[d, :, 0:LANES] = state_codes[rows, lanes]
        pay_ref[d, :, LANES : 2 * LANES] = grad_codes[rows, lanes]
        pay_ref[d, :, 2 * LANES :] = side[:, lanes]
    drain(spans, [sending])


def chunk_place(d, height):
    r, l = height * (d // 4), LANES * (d % 4)
    return slice(r, r + height), slice(l, l + LANES)


def scan_kernel(own_ref, out_ref, made):
    chunks, height, _ = out_ref.shape
    gains, states, grads = [], [], []
    for e in range(chunks):
        side = own_ref[e, :, 2 * LANES :].astype(f32)
        gains.append(jnp.exp(log_of(side[2:3], side[3:4])))
        states.append(decoded(own_ref[e, :, 0:LANES], side[0:1]))
        grads.append(decoded(own_ref[e, :, LANES : 2 * LANES], side[1:2]))
    state = jnp.zeros((height, LANES), f32)
    grad = jnp.zeros((height, LANES), f32)
    for e in range(chunks):
        made[e, :, 0:LANES] = state
        state = gains[e] * state + states[e]
    for e in reversed(range(chunks)):
        made[e, :, LANES:] = grad
        grad = gains[e] * grad + grads[e]
    for e in range(chunks):
        codes, power = coded(made[e], 0)
        out_ref[e, :, 0 : 2 * LANES] = codes
        out_ref[e, :, 2 * LANES :] = side_tile(height, [power[:, :LANES], power[:, LANES:]])


def causal():
    row = lax.broadcasted_iota(jnp.int32, (SPAN, SPAN), 0)
    return row >= lax.broadcasted_iota(jnp.int32, (SPAN, SPAN), 1)


def local_input_kernel(
    x_hbm, grad_hbm, inject_hbm, read_hbm, after_hbm, rate_hbm, later_hbm, halo_hbm, weight_hbm,
    act_hbm, pre_hbm, factor_hbm,
    x_ref, grad_ref, inject_ref, read_ref, after_ref, rate_ref, later_ref, halo_ref, weight_ref,
    act_ref, pre_ref, factor_ref, prev, isems, sems, osems,
):
    spans = rate_ref.shape[0]
    sources = [x_hbm, grad_hbm, inject_hbm, read_hbm, after_hbm]
    targets = [x_ref, grad_ref, inject_ref, read_ref, after_ref]
    pieces = [by_span(a, b, isems.at[k]) for k, (a, b) in enumerate(zip(sources, targets))]
    start = starting(pieces)
    outs = [
        by_span(act_ref, act_hbm, osems.at[0]), by_span(pre_ref, pre_hbm, osems.at[1]),
        by_span(factor_ref, factor_hbm, osems.at[2]),
    ]
    fetch(
        spans,
        [
            pltpu.make_async_copy(rate_hbm, rate_ref, sems.at[0]),
            pltpu.make_async_copy(later_hbm, later_ref, sems.at[1]),
            pltpu.make_async_copy(halo_hbm, halo_ref, sems.at[2]),
            pltpu.make_async_copy(weight_hbm, weight_ref, sems.at[3]),
        ],
        start,
    )
    prev[...] = halo_ref[...].astype(f32)[PREV - 8 :]
    weights = weight_ref[...].astype(f32)

    def step(span):
        rows = span_at(span)
        rate = rate_ref[pl.ds(span, 1), :]
        later = jnp.exp(later_ref[pl.ds(span, 1), :])
        inject, read = inject_ref[rows, :], read_ref[rows, :]
        here = places()
        x = x_ref[rows, :].astype(f32)
        preact = convolved(x, prev[...], weights)
        prev[...] = x[SPAN - 8 :]
        squashed = jax.nn.sigmoid(preact)
        act_ref[rows, :] = (preact * squashed).astype(bf16)
        slope = squashed * (1.0 + preact * (1.0 - squashed))
        steep = slope * jnp.exp(-here * rate)
        end = jnp.exp((SPAN - 1.0) * rate)
        up = (grad_ref[rows, :].astype(f32) * jnp.exp(here * rate)).astype(bf16)
        mixing = jnp.where(causal(), dot(read, inject, NT), 0.0).astype(bf16)
        stacked = jnp.concatenate(split(after_ref[span] * end), axis=0)
        doubled = jnp.concatenate([inject, inject], axis=1)
        pre = steep * (dot(mixing, up, TN) + dot(doubled, stacked, NN))
        pre_ref[rows, :] = pre.astype(bf16)
        factor_ref[rows, :] = (steep * (end * later)).astype(bf16)
        for out in outs:
            out(span).start()

    each_span(spans, step, start, pieces)
    drain(spans, outs)


def wide_product(high, low, both, states):
    wide = dot(high, both, NT)
    return wide[:, :states] + (wide[:, states:] + dot(low, both[0:states, :], NT))


def local_shared_kernel(
    grad_hbm, act_hbm, inject_hbm, read_hbm, after_hbm, before_hbm, rate_hbm,
    gi_hbm, gr_hbm,
    grad_ref, act_ref, inject_ref, read_ref, after_ref, before_ref, rate_ref,
    gi_ref, gr_ref,
    isems, sem, osems,
):
    spans = rate_ref.shape[0]
    sources = [grad_hbm, act_hbm, inject_hbm, read_hbm, after_hbm, before_hbm]
    targets = [grad_ref, act_ref, inject_ref, read_ref, after_ref, before_ref]
    pieces = [by_span(a, b, isems.at[k]) for k, (a, b) in enumerate(zip(sources, targets))]
    start = starting(pieces)
    outs = [by_span(gi_ref, gi_hbm, osems.at[0]), by_span(gr_ref, gr_hbm, osems.at[1])]
    fetch(spans, [pltpu.make_async_copy(rate_hbm, rate_ref, sem)], start)

    def step(span):
        rows = span_at(span)
        rate = rate_ref[pl.ds(span, 1), :]
        inject, read = inject_ref[rows, :], read_ref[rows, :]
        states = inject.shape[1]
        here = places()
        up = grad_ref[rows, :].astype(f32) * jnp.exp(here * rate)
        down = act_ref[rows, :].astype(f32) * jnp.exp(-here * rate)
        uph, upl = split(up)
        downh, downl = split(down)
        pairs = jnp.where(causal(), dot(uph, downh, NT), 0.0).astype(bf16)
        end = jnp.exp((SPAN - 1.0) * rate)
        afters = jnp.concatenate(split(after_ref[span] * end), axis=0)
        befores = jnp.concatenate(split(before_ref[span] * jnp.exp(rate)), axis=0)
        gi_ref[rows, :] = dot(pairs, read, TN) + wide_product(downh, downl, afters, states)
        gr_ref[rows, :] = dot(pairs, inject, NN) + wide_product(uph, upl, befores, states)
        for out in outs:
            out(span).start()

    each_span(spans, step, start, pieces, unroll=True)
    drain(spans, outs)


def unpacked(back_ref, both, which):
    chunks, height, _ = back_ref.shape
    states = both.shape[0] // 2
    for d in range(chunks):
        rows, lanes = chunk_place(d, height)
        power = back_ref[d, :, 2 * LANES :].astype(f32)[which : which + 1]
        v = decoded(back_ref[d, :, LANES * which : LANES * which + LANES], power)
        high, low = split(v)
        both[rows, lanes] = high
        both[states + rows.start : states + rows.stop, lanes] = low


def shared_kernel(
    grads_turn, core_ref, back_ref, grad_hbm, act_hbm, gr_hbm, gi_hbm, rate_hbm, prior_hbm, later_hbm,
    out_hbm,
    in_ref, sum_ref, rate_ref, prior_ref, later_ref, both, out_ref, isems, sems, osems,
):
    tokens, states = sum_ref.shape
    spans = tokens // SPAN
    readouts = core_ref[0] == grads_turn
    small = [
        pltpu.make_async_copy(rate_hbm, rate_ref, sems.at[0]),
        pltpu.make_async_copy(prior_hbm, prior_ref, sems.at[1]),
        pltpu.make_async_copy(later_hbm, later_ref, sems.at[2]),
    ]
    for copy in small:
        copy.start()

    pieces = [by_span(grad_hbm, in_ref, isems.at[0]), by_span(gr_hbm, sum_ref, isems.at[1])]
    others = [by_span(act_hbm, in_ref, isems.at[0]), by_span(gi_hbm, sum_ref, isems.at[1])]

    def start(span):
        @pl.when(readouts)
        def _():
            starting(pieces)(span)

        @pl.when(jnp.logical_not(readouts))
        def _():
            starting(others)(span)

    fetch(spans, [], start, ahead=spans)

    @pl.when(readouts)
    def _():
        unpacked(back_ref, both, 0)

    @pl.when(jnp.logical_not(readouts))
    def _():
        unpacked(back_ref, both, 1)

    for copy in small:
        copy.wait()
    sending = by_span(out_ref, out_hbm, osems)

    def step(span):
        rows = span_at(span)
        rate = rate_ref[pl.ds(span, 1), :]
        ahead = rate + prior_ref[pl.ds(span, 1), :]
        behind = (SPAN - 1.0) * rate + later_ref[pl.ds(span, 1), :]
        slope = jnp.where(readouts, rate, -rate)
        offset = jnp.where(readouts, ahead, behind)
        high, low = split(in_ref[rows, :].astype(f32) * jnp.exp(places() * slope + offset))
        out_ref[rows, :] = sum_ref[rows, :] + wide_product(high, low, both[...], states)
        sending(span).start()

    each_span(spans, step, start, pieces, ahead=spans)
    drain(spans, [sending])


def input_kernel(
    back_ref, pre_hbm, factor_hbm, inject_hbm, weight_ref,
    out_hbm, first_ref,
    pre_ref, factor_ref, inject_ref, grads, after, made, isems, osems,
):
    spans = pre_ref.shape[0] // SPAN
    pieces = [
        by_span(pre_hbm, pre_ref, isems.at[0]), by_span(factor_hbm, factor_ref, isems.at[1]),
        by_span(inject_hbm, inject_ref, isems.at[2]),
    ]
    out = by_span(made, out_hbm, osems)
    start = starting(pieces)
    fetch(spans, [], start, backwards=True, ahead=spans)
    unpacked(back_ref, grads, 1)
    after[...] = jnp.zeros_like(after)
    weights = weight_ref[...].astype(f32)

    def step(span):
        rows = span_at(span)
        inject = inject_ref[rows, :]
        carried = dot(jnp.concatenate([inject, inject], axis=1), grads[...], NN)
        now = pre_ref[rows, :].astype(f32) + factor_ref[rows, :].astype(f32) * carried
        joined = jnp.concatenate([now, after[...]], axis=0)
        one = pltpu.roll(joined, SPAN + 8 - 1, axis=0)
        further = weights[1:2] * joined + weights[0:1] * one
        summed = weights[3:4] * now + weights[2:3] * one[:SPAN]
        summed = summed + pltpu.roll(further, SPAN + 8 - 2, axis=0)[:SPAN]
        after[...] = now[0:8]
        made[rows, :] = summed
        out(span).start()

    each_span(spans, step, start, pieces, backwards=True, ahead=spans)
    first_ref[...] = after[...]
    drain(spans, [out])


def params(mib=54):
    return pltpu.CompilerParams(vmem_limit_bytes=mib << 20)


def cost(flops, nbytes):
    return pl.CostEstimate(flops=flops, bytes_accessed=nbytes, transcendentals=0)


def body(nseq, ny, nc, conv_input, grad_output, inject, readout, conv_weight, decay_codes):
    tokens, channels = conv_input.shape
    spans = decay_codes.shape[1]
    states = inject.shape[1]
    shape = jax.ShapeDtypeStruct
    height = 4 * states // nseq
    chunk = (nseq, height, 3 * LANES)
    smem = pl.BlockSpec(memory_space=pltpu.SMEM)
    wide, wide16 = shape((tokens, channels), f32), shape((tokens, channels), bf16)
    narrow, row = shape((tokens, states), f32), shape((spans, channels), f32)
    local = shape((spans, states, channels), f32)
    state = shape((states, channels), f32)

    up = [(i, i + 1) for i in range(nseq - 1)]
    down = [(i + 1, i) for i in range(nseq - 1)]
    halo = lax.ppermute(conv_input[tokens - PREV :], SEQ, up)

    anywhere = pl.BlockSpec(memory_space=pl.ANY)
    hbm = pl.BlockSpec(memory_space=pltpu.HBM)
    plain = pl.BlockSpec()
    wide_v, wide16_v = pltpu.VMEM(wide.shape, f32), pltpu.VMEM(wide.shape, bf16)
    narrow_v, narrow16_v = pltpu.VMEM(narrow.shape, f32), pltpu.VMEM(narrow.shape, bf16)
    row_v, state_v = pltpu.VMEM(row.shape, f32), pltpu.VMEM(state.shape, f32)
    local_v = pltpu.VMEM(local.shape, f32)
    halo_v, weight_v = pltpu.VMEM((PREV, channels), bf16), pltpu.VMEM(conv_weight.shape, bf16)
    dma = pltpu.SemaphoreType.DMA

    rates, prior, later, own_log, own_grad, after = pl.pallas_call(
        grads_kernel,
        in_specs=[hbm] * 3,
        out_specs=[plain] * 5 + [hbm],
        out_shape=[row, row, row, shape((1, channels), f32), state, local],
        scratch_shapes=[
            pltpu.VMEM(decay_codes.shape, jnp.int32), wide16_v, narrow16_v, local_v,
            dma, dma((spans,)), dma((spans,)), dma((spans,)),
        ],
        compiler_params=params(),
        cost_estimate=cost(4 * tokens * channels * states, 3 << 20),
        name="own_grads",
    )(decay_codes, grad_output, readout)

    payload, before = pl.pallas_call(
        states_kernel,
        in_specs=[hbm, anywhere, hbm, anywhere, hbm, anywhere, anywhere],
        out_specs=[plain, hbm],
        out_shape=[shape(chunk, jnp.int16), local],
        scratch_shapes=[
            wide16_v, halo_v, narrow16_v, row_v, weight_v, state_v, pltpu.VMEM((1, channels), f32),
            state_v, pltpu.VMEM((8, channels), f32), local_v,
            dma((spans,)), dma((spans,)), dma((5,)), dma((spans,)),
        ],
        compiler_params=params(),
        cost_estimate=cost(4 * tokens * channels * states, 4 << 20),
        name="own_states",
    )(conv_input, halo, inject, rates, conv_weight, own_grad, own_log)

    arrived = lax.all_to_all(payload, SEQ, 0, 0, tiled=True)

    act, pre, factor = pl.pallas_call(
        local_input_kernel,
        in_specs=[hbm] * 5 + [anywhere] * 3 + [hbm],
        out_specs=[hbm] * 3,
        out_shape=[wide16] * 3,
        scratch_shapes=[wide16_v, wide16_v, narrow16_v, narrow16_v, local_v, row_v, row_v]
        + [halo_v, weight_v] + [wide16_v] * 3 + [pltpu.VMEM((8, channels), f32)]
        + [dma((5, spans)), dma((4,)), dma((3, spans))],
        compiler_params=params(),
        cost_estimate=cost(8 * tokens * channels * SPAN, 13 << 20),
        name="local_input",
    )(conv_input, grad_output, inject, readout, after, rates, later, halo, conv_weight)
    arrived, act = lax.optimization_barrier((arrived, act))

    gi, gr = pl.pallas_call(
        local_shared_kernel,
        in_specs=[hbm] * 6 + [anywhere],
        out_specs=[hbm] * 2,
        out_shape=[narrow] * 2,
        scratch_shapes=[wide16_v] * 2 + [narrow16_v] * 2 + [local_v, local_v, row_v]
        + [narrow_v] * 2 + [dma((6, spans)), dma, dma((2, spans))],
        compiler_params=params(),
        cost_estimate=cost(12 * tokens * channels * SPAN, 9 << 20),
        name="local_shared",
    )(grad_output, act, inject, readout, after, before, rates)

    scanned = pl.pallas_call(
        scan_kernel,
        out_shape=shape(chunk, jnp.int16),
        scratch_shapes=[pltpu.VMEM((nseq, height, 2 * LANES), f32)],
        compiler_params=params(8),
        cost_estimate=cost(1 << 18, 1 << 20),
        name="carry",
    )(arrived)
    returned = lax.all_to_all(scanned, SEQ, 0, 0, tiled=True)

    core = lax.axis_index("c").astype(jnp.int32).reshape(1)
    stacked = pltpu.VMEM((2 * states, channels), bf16)

    def shared(turn):
        return pl.pallas_call(
            functools.partial(shared_kernel, turn),
            in_specs=[smem, plain] + [hbm] * 4 + [anywhere] * 3,
            out_specs=anywhere,
            out_shape=narrow,
            scratch_shapes=[wide16_v, narrow_v] + [row_v] * 3
            + [stacked, narrow_v, dma((2, spans)), dma((3,)), dma((spans,))],
            compiler_params=params(53),
            cost_estimate=cost(6 * tokens * channels * states, 4 << 20),
            name=f"shared_terms_{turn}",
        )(core, returned, grad_output, act, gr, gi, rates, prior, later)

    swap = [(i, i ^ 1) for i in range(nc)]
    swapped = lax.ppermute(shared(0), "c", swap)
    kept = shared(1)
    here = lax.axis_index("y")
    part = tokens // ny

    def turn(array, by):
        return lax.ppermute(array, "y", [(i, (i + by) % ny) for i in range(ny)])

    def cut(which):
        at = lax.rem(here + which, ny) * part
        return lax.dynamic_slice_in_dim(kept, at, part) + lax.dynamic_slice_in_dim(swapped, at, part)

    sent = [turn(cut(by).astype(bf16), by) for by in range(1, ny)]

    grad_input, first = pl.pallas_call(
        input_kernel,
        in_specs=[plain] + [hbm] * 3 + [plain],
        out_specs=[hbm, plain],
        out_shape=[wide, shape((8, channels), f32)],
        scratch_shapes=[
            wide16_v, wide16_v, narrow16_v, stacked, pltpu.VMEM((8, channels), f32), wide_v,
            dma((3, spans)), dma((spans,)),
        ],
        compiler_params=params(53),
        cost_estimate=cost(4 * tokens * channels * states, 13 << 20),
        name="input_grads",
    )(returned, pre, factor, inject, conv_weight)

    *sent, first = lax.optimization_barrier((*sent, first))
    quarter = cut(0)
    for piece in sent:
        quarter = quarter + piece.astype(f32)
    quarter = lax.optimization_barrier(quarter.astype(bf16))
    turned = [turn(quarter, by) for by in range(1, ny)]
    next_rows = lax.ppermute(first, SEQ, down)
    *turned, next_rows = lax.optimization_barrier((*turned, next_rows))
    done = jnp.zeros((tokens, states), bf16)
    for by, piece in enumerate([quarter] + turned):
        done = lax.dynamic_update_slice_in_dim(
            done, piece, lax.rem(here - by + ny, ny) * part, 0
        )
    other = lax.ppermute(done, "c", swap)
    mine_is_first = lax.axis_index("c") == 0
    grad_inject = jnp.where(mine_is_first, done, other).astype(f32)
    grad_readout = jnp.where(mine_is_first, other, done).astype(f32)

    weights = conv_weight.astype(f32)
    tail_rows = []
    for row in range(3):
        tail_rows.append(sum(weights[k] * next_rows[row - k] for k in range(row + 1)))
    patch = jnp.concatenate([jnp.zeros((5, channels), f32), jnp.stack(tail_rows)], axis=0)
    last = lax.slice_in_dim(grad_input, tokens - 8, tokens) + patch
    grad_input = lax.dynamic_update_slice(grad_input, last, (tokens - 8, 0))
    return grad_input, grad_inject, grad_readout


def build(devices, sizes):
    fine = Mesh(devices.reshape(sizes), ("z", "x", "y", "c"))
    nz, nx, ny, nc = sizes
    return jax.shard_map(
        functools.partial(body, nz * nx, ny, nc),
        mesh=fine,
        in_specs=(P(SEQ, HG), P(SEQ, HG), P(SEQ, None), P(SEQ, None), P(None, HG), P(HG, SEQ)),
        out_specs=(P(SEQ, HG), P(SEQ, None), P(SEQ, None)),
        check_vma=False,
    )


def solution(mesh):
    return build(mesh.devices, (8, 4, 4, 2))
```
